32 devices in a mesh: dp: 16 (over z, y, x), mp: 2 (over core).
Axes of the slice: x: 2, y: 2, z: 4, core: 2. Of those that a mesh axis runs over, the one named last changes fastest.
Arguments:
- latents: bfloat16 [131072, 1024], P(('dp', 'mp')), may hold values from -6 to 6
- first_scale: float32 [1024], replicated, may hold values from 0.25 to 1.75
- first_shift: float32 [1024], replicated, may hold values from -3 to 3
- input_weights: bfloat16 [3, 1024, 1024], P(None, None, 'mp'), may hold values from -0.1875 to 0.1875
- input_bias: bfloat16 [2, 1024], P(None, 'mp'), may hold values from -1.1953125 to 1.1953125
- output_weight: bfloat16 [1024, 1024], P('mp'), may hold values from -0.75 to 0.75
- output_bias: float32 [1024], replicated, may hold values from -3 to 3
- second_scale: float32 [1024], replicated, may hold values from 0.25 to 1.75
- second_shift: float32 [1024], replicated, may hold values from -3 to 3
- up_weight: bfloat16 [1024, 1024], P(None, 'mp'), may hold values from -0.1875 to 0.1875
- up_bias: bfloat16 [1024], P('mp'), may hold values from -3 to 3
- down_weight: bfloat16 [1024, 1024], P('mp'), may hold values from -0.1875 to 0.1875
- down_bias: float32 [1024], replicated, may hold values from -3 to 3
- output_grad: bfloat16 [131072, 1024], P(('dp', 'mp')), may hold values from -12 to 12
Outputs:
- block_output: float32 [131072, 1024], P(('dp', 'mp'))
- latents_grad: float32 [131072, 1024], P(('dp', 'mp'))
- first_scale_grad: float32 [1024], replicated
- first_shift_grad: float32 [1024], replicated
- input_weights_grad: float32 [3, 1024, 1024], P(None, None, 'mp')
- input_bias_grad: float32 [2, 1024], P(None, 'mp')
- output_weight_grad: float32 [1024, 1024], P('mp')
- output_bias_grad: float32 [1024], replicated
- second_scale_grad: float32 [1024], replicated
- second_shift_grad: float32 [1024], replicated
- up_weight_grad: float32 [1024, 1024], P(None, 'mp')
- up_bias_grad: float32 [1024], P('mp')
- down_weight_grad: float32 [1024, 1024], P('mp')
- down_bias_grad: float32 [1024], replicated
The draws below stay inside these ranges and needn't reach their ends.
All inputs are finite; a program needn't handle non-finite values.
Results may differ from the reference program's by a relative error of at most 0.02.
Values may be sent and summed in bfloat16 or wider, within the bound.
A program may use at most 384 MiB of HBM per device.

```python
import math
import jax
import jax.numpy as jnp
from jax import lax

D = 1024
HEADS = 8
HEAD = 128
FFN = 1024
LAT = 512
IMAGES = 256
TOKENS = 131072


def draw_output_grad(key, part):
    row_index = jnp.arange(TOKENS, dtype=jnp.float32)[:, None]
    rising = jnp.exp(jnp.log(3.0) * row_index / max(TOKENS - 1, 1))
    values = jnp.clip(jax.random.normal(key, (TOKENS, D), jnp.float32), -4.0, 4.0) * rising
    return values.astype(jnp.bfloat16)


def steps_of(key, extent, pieces, low, top_value):
    level, own = 1.0, jax.random.fold_in(key, 6)
    for position, blocks in pieces:
        draws = jnp.exp(jax.random.uniform(jax.random.fold_in(own, position), (blocks,), jnp.float32, low / len(pieces), top_value / len(pieces)))
        level = level * jnp.repeat(draws, extent[position] // blocks).reshape([-1 if axis == position else 1 for axis in range(len(extent))])
    return level


def bell_draw(own_key, shape, width, limit, cuts=(), kind=jnp.bfloat16):
    entries = jax.random.normal(own_key, shape, jnp.float32) * width
    if len(cuts) > 0:
        entries = steps_of(own_key, shape, cuts, -0.22, 0.18) * entries
    return jnp.clip(entries, min=-limit, max=limit).astype(kind)


def setup_inputs(seed: int = 0) -> dict:
    splits = jax.random.split(jax.random.key(seed), 15)
    latents = bell_draw(splits[0], (TOKENS, D), 1.0, 6.0, ((0, 32),))
    first_scale = jnp.clip(1.0 + 0.15 * jax.random.normal(splits[1], (D,), jnp.float32), 0.25, 1.75)
    first_shift = bell_draw(splits[2], (D,), 0.5, 3.0, (), jnp.float32)
    input_weights = bell_draw(splits[3], (3, D, D), D ** -0.5, 0.1875, ((2, 2),))
    input_bias = bell_draw(splits[4], (2, D), 0.2, 1.1953125, ((1, 2),))
    output_weight = bell_draw(splits[5], (D, D), (D // 16) ** -0.5, 0.75, ((0, 2),))
    output_bias = bell_draw(splits[6], (D,), 0.5, 3.0, (), jnp.float32)
    second_scale = jnp.clip(1.0 + 0.15 * jax.random.normal(splits[7], (D,), jnp.float32), 0.25, 1.75)
    second_shift = bell_draw(splits[8], (D,), 0.5, 3.0, (), jnp.float32)
    up_weight = bell_draw(splits[9], (D, FFN), D ** -0.5, 0.1875, ((1, 2),))
    up_bias = bell_draw(splits[10], (FFN,), 0.5, 3.0, ((0, 2),))
    down_weight = bell_draw(splits[11], (FFN, D), FFN ** -0.5, 0.1875, ((0, 2),))
    down_bias = bell_draw(splits[12], (D,), 0.5, 3.0, (), jnp.float32)
    output_grad = draw_output_grad(jax.random.fold_in(splits[14], 71), 0)
    return {"latents": latents, "first_scale": first_scale, "first_shift": first_shift, "input_weights": input_weights, "input_bias": input_bias, "output_weight": output_weight, "output_bias": output_bias, "second_scale": second_scale, "second_shift": second_shift, "up_weight": up_weight, "up_bias": up_bias, "down_weight": down_weight, "down_bias": down_bias, "output_grad": output_grad}


@jax.custom_vjp
def low(v):
    return lax.optimization_barrier(v.astype(jnp.bfloat16)).astype(jnp.float32)

@jax.custom_vjp
def low_back(v):
    return v

def low_keep(v):
    return (low(v), None)

def low_pass(kept, grad):
    return (grad,)

def back_keep(v):
    return (v, None)

def back_low(kept, grad):
    return (low(grad),)
low.defvjp(low_keep, low_pass)
low_back.defvjp(back_keep, back_low)
EPS = 1e-05
HIGH = lax.Precision.HIGHEST

def normalize(values, gain, offset):
    centre = lax.optimization_barrier(jnp.mean(values, axis=-1, keepdims=True))
    centred = values - centre
    spread = lax.optimization_barrier(jnp.mean(centred * centred, axis=-1, keepdims=True))
    return centred * lax.rsqrt(spread + EPS) * gain + offset

def project(inputs, weight):
    return jnp.einsum('nld,de->nle', inputs, weight, precision=HIGH)

def block_forward(image_rows, params):
    first_scale, first_shift, input_weights, input_bias, output_weight, output_bias, second_scale, second_shift, up_weight, up_bias, down_weight, down_bias = params
    image_count = image_rows.shape[0]
    normed_one = low(normalize(image_rows, first_scale, first_shift))
    query_rows = low(low_back(project(normed_one, input_weights[0]) + input_bias[0]))
    key_rows = low(low_back(project(normed_one, input_weights[1])))
    value_rows = low(low_back(project(normed_one, input_weights[2]) + input_bias[1]))
    split_shape = (image_count, LAT, HEADS, HEAD)
    scores = jnp.einsum('nqhe,nkhe->nhqk', query_rows.reshape(split_shape), key_rows.reshape(split_shape), precision=HIGH) * HEAD ** (-0.5)
    scores = low_back(scores)
    probs_low = low(jax.nn.softmax(scores, axis=-1))
    mixed_heads = jnp.einsum('nhqk,nkhe->nqhe', probs_low, value_rows.reshape(split_shape), precision=HIGH)
    mixed_heads = low(low_back(mixed_heads.reshape(image_count, LAT, D)))
    middle = image_rows + low_back(project(mixed_heads, output_weight)) + output_bias
    normed_two = low(normalize(middle, second_scale, second_shift))
    hidden = low_back(project(normed_two, up_weight) + up_bias)
    activated = low(jax.nn.gelu(hidden, approximate=True))
    return middle + low_back(project(activated, down_weight)) + down_bias

def reference(latents, first_scale, first_shift, input_weights, input_bias, output_weight, output_bias, second_scale, second_shift, up_weight, up_bias, down_weight, down_bias, output_grad):
    params = (first_scale.astype(jnp.float32), first_shift.astype(jnp.float32), input_weights.astype(jnp.float32), input_bias.astype(jnp.float32), output_weight.astype(jnp.float32), output_bias.astype(jnp.float32), second_scale.astype(jnp.float32), second_shift.astype(jnp.float32), up_weight.astype(jnp.float32), up_bias.astype(jnp.float32), down_weight.astype(jnp.float32), down_bias.astype(jnp.float32))
    inputs = latents.astype(jnp.float32)
    cotangent = output_grad.astype(jnp.float32)
    image_group = math.gcd(IMAGES, 8)

    def forward(rows_in, weights_in):

        def one_block(image_rows):
            return block_forward(image_rows, weights_in)
        blocks = rows_in.reshape(IMAGES // image_group, image_group, LAT, D)
        return lax.map(jax.checkpoint(one_block), blocks).reshape(TOKENS, D)
    output, pullback = jax.vjp(forward, inputs, params)
    latents_grad, param_grads = pullback(cotangent)
    g_first_scale, g_first_shift, g_input_weights, g_input_bias, g_output_weight, g_output_bias, g_second_scale, g_second_shift, g_up_weight, g_up_bias, g_down_weight, g_down_bias = param_grads
    factor = 1.0 / IMAGES
    return (output, latents_grad, g_first_scale * factor, g_first_shift * factor, g_input_weights * factor, g_input_bias * factor, g_output_weight * factor, g_output_bias * factor, g_second_scale * factor, g_second_shift * factor, g_up_weight * factor, g_up_bias * factor, g_down_weight * factor, g_down_bias * factor)
```

```python
import functools

import jax
import jax.numpy as jnp
from jax import lax
from jax.experimental import pallas as pl
from jax.experimental.pallas import tpu as pltpu
from jax.sharding import PartitionSpec as P

D = 1024
HEAD = 128
HEADS = 8
LAT = 512
HALF = 512
GROUPS = 2
EPS = 1e-05
SCALE = HEAD ** (-0.5)
LOG2E = 1.4426950408889634
GELU_A = 0.7978845608028654
GELU_B = 0.044715
MESH = pl.DeviceIdType.MESH
NN = (((1,), (0,)), ((), ()))
NT = (((1,), (1,)), ((), ()))
TN = (((0,), (0,)), ((), ()))
BF = jnp.bfloat16
F32 = jnp.float32
VMEM_LIMIT = 60 << 20


def mul(a, b, dims):
    return lax.dot_general(a, b, dims, preferred_element_type=F32)


def unit_of(rows):
    centred = rows - jnp.mean(rows, axis=-1, keepdims=True)
    inverse = lax.rsqrt(jnp.mean(centred * centred, axis=-1, keepdims=True) + EPS)
    return centred * inverse, inverse


def norm_back(upstream, unit, inverse, gain):
    scaled = upstream * gain
    inner = (
        scaled
        - jnp.mean(scaled, axis=-1, keepdims=True)
        - unit * jnp.mean(scaled * unit, axis=-1, keepdims=True)
    )
    return inverse * inner


def column_sum(values):
    return jnp.sum(values, axis=0, keepdims=True)


def row_spec(width):
    return pl.BlockSpec((LAT, width), lambda i: (i, 0))


def whole_spec(shape):
    return pl.BlockSpec(shape, lambda *_: (0,) * len(shape), pipeline_mode=pl.Buffered(1))


def kept_spec(shape):
    return pl.BlockSpec(shape, lambda *_: (0,) * len(shape))


ANY = pl.BlockSpec(memory_space=pl.ANY)


def shape_of(shape, dtype):
    return jax.ShapeDtypeStruct(shape, dtype)


def cost(flops, moved):
    return pl.CostEstimate(flops=int(flops), bytes_accessed=int(moved), transcendentals=0)


def dp_flip(bit):
    me = lax.axis_index("dp")
    step = 1 << bit
    on = lax.rem(me // step, 2)
    return (me + step - 2 * step * on, lax.axis_index("mp"))


def core_flip():
    return (lax.axis_index("dp"), 1 - lax.axis_index("mp"))


def greet(partners):
    barrier = pltpu.get_barrier_semaphore()
    for partner in partners:
        pl.semaphore_signal(barrier, inc=1, device_id=partner, device_id_type=MESH)
    pl.semaphore_wait(barrier, len(partners))


def remote(src, dst, send, recv, partner):
    return pltpu.make_async_remote_copy(
        src_ref=src,
        dst_ref=dst,
        send_sem=send,
        recv_sem=recv,
        device_id=partner,
        device_id_type=MESH,
    )


class Reduction:
    def __init__(self, rows, columns, parts, orders):
        self.rows, self.columns, self.parts, self.orders = rows, columns, parts, orders
        self.bits = len(orders[0])
        self.ticks = 2 * self.bits + 2

    def scratch(self):
        stages = 2 * self.bits
        return [
            pltpu.VMEM((self.rows, self.columns), BF),
            pltpu.VMEM((self.rows, self.columns), BF),
            pltpu.VMEM((self.rows, self.columns), BF),
            pltpu.SemaphoreType.DMA((2,)),
            pltpu.SemaphoreType.DMA((len(self.parts), stages)),
            pltpu.SemaphoreType.DMA((len(self.parts), stages)),
        ]

    def offset(self, part, level):
        me = lax.axis_index("dp")
        row = 0
        for stage in range(level):
            on = lax.rem(me // (1 << self.orders[part][stage]), 2)
            row = row + on * (self.rows >> (stage + 1))
        return row

    def aligned(self, row, size):
        return pl.ds(pl.multiple_of(row, size), size)

    def columns_of(self, part):
        first, last = self.parts[part]
        return pl.ds(first, last - first)

    def halving(self, refs, part, stage):
        cur, _, recv, _, send_sem, recv_sem = refs
        size = self.rows >> (stage + 1)
        bit = self.orders[part][stage]
        on = lax.rem(lax.axis_index("dp") // (1 << bit), 2)
        base = self.offset(part, stage)
        cols = self.columns_of(part)
        landing = self.rows - 2 * size
        copy = remote(
            cur.at[self.aligned(base + (1 - on) * size, size), cols],
            recv.at[pl.ds(landing, size), cols],
            send_sem.at[part, stage],
            recv_sem.at[part, stage],
            dp_flip(bit),
        )
        return copy, self.aligned(base + on * size, size), pl.ds(landing, size), cols

    def doubling(self, refs, part, step):
        _, full, _, _, send_sem, recv_sem = refs
        stage = self.bits - 1 - step
        size = self.rows >> (stage + 1)
        rows = self.aligned(self.offset(part, stage + 1), size)
        cols = self.columns_of(part)
        return remote(
            full.at[rows, cols],
            full.at[rows, cols],
            send_sem.at[part, self.bits + step],
            recv_sem.at[part, self.bits + step],
            dp_flip(self.orders[part][stage]),
        )

    def exchange(self, refs, other):
        return remote(other, refs[1], refs[3].at[0], refs[3].at[1], core_flip())

    def tick(self, refs, tick, other):
        cur, landed, recv = refs[:3]
        parts = range(len(self.parts))
        if tick == 0:
            self.exchange(refs, other).start()
            return
        if tick == 1:
            self.exchange(refs, other).wait()
            cur[...] = (cur[...].astype(F32) + landed[...].astype(F32)).astype(BF)
            for part in parts:
                self.halving(refs, part, 0)[0].start()
            return
        if tick <= self.bits + 1:
            for part in parts:
                copy, keep, landing, cols = self.halving(refs, part, tick - 2)
                copy.wait()
                total = (cur[keep, cols].astype(F32) + recv[landing, cols].astype(F32)).astype(BF)
                if tick <= self.bits:
                    cur[keep, cols] = total
                    self.halving(refs, part, tick - 1)[0].start()
                else:
                    landed[keep, cols] = total
                    self.doubling(refs, part, 0).start()
            return
        step = tick - self.bits - 2
        for part in parts:
            self.doubling(refs, part, step).wait()
            if step + 1 < self.bits:
                self.doubling(refs, part, step + 1).start()


ORDERS = ((0, 1, 2, 3), (1, 2, 3, 0), (2, 3, 0, 1))


def reduction_partners():
    return [core_flip()] + [dp_flip(bit) for bit in range(4)]


def first_kernel(
    spread, x_ref, gain_ref, shift_ref, bias_ref, w_in, *refs
):
    step = pl.program_id(0)
    if spread:
        sources = (w_in_any, w_out, w_up, w_down, bias_all) = refs[:5]
        normed_ref, heads_ref = refs[5:7]
        targets = refs[7:12]
        send_sem, recv_sem = refs[12:14]

        def copies():
            return [
                remote(src, dst, send_sem.at[n], recv_sem.at[n], core_flip())
                for n, (src, dst) in enumerate(zip(sources, targets))
            ]

        @pl.when(step == 0)
        def _():
            greet([core_flip()])
            for copy in copies():
                copy.start()
    else:
        normed_ref, heads_ref = refs

    unit, _ = unit_of(x_ref[...].astype(F32))
    normed_ref[...] = (unit * gain_ref[...] + shift_ref[...]).astype(BF)
    project(normed_ref, w_in, bias_ref, heads_ref)

    if spread:

        @pl.when(step == pl.num_programs(0) - 1)
        def _():
            for copy in copies():
                copy.wait()


def project(normed_ref, weights, bias_ref, heads_ref):
    for which in range(3):
        rows = mul(normed_ref[...], weights[which], NN)
        if which != 1:
            place = 0 if which == 0 else 1
            rows = rows + bias_ref[place : place + 1, :].astype(F32)
        heads_ref[which] = rows.astype(BF)


def forward_kernel(
    x_ref,
    normed_ref,
    own_ref,
    g_ref,
    w_in,
    in_bias,
    wo_own,
    wo_other,
    out_bias,
    gain_ref,
    shift_ref,
    wu_own,
    wu_other,
    ub_own,
    ub_other,
    wd_own,
    wd_other,
    down_bias,
    block_ref,
    other_ref,
    probs_ref,
    inv_ref,
    mixed_ref,
    middle_ref,
    slope_ref,
    gdown_ref,
    gsum_ref,
    acc,
    normed_two,
    act,
    wide,
):
    step = pl.program_id(0)

    @pl.when(step == 0)
    def _():
        acc[...] = jnp.zeros_like(acc)
        gsum_ref[...] = jnp.zeros_like(gsum_ref)

    project(normed_ref, w_in, in_bias, other_ref)
    lane = lax.broadcasted_iota(jnp.int32, (LAT, HEAD), 1)
    inverses = jnp.zeros((LAT, HEAD), F32)
    for half, heads_ref in enumerate((own_ref, other_ref)):
        for head in range(HALF // HEAD):
            cols = slice(head * HEAD, (head + 1) * HEAD)
            scores = mul(heads_ref[0, :, cols], heads_ref[1, :, cols], NT)
            highest = jnp.max(scores, axis=-1, keepdims=True)
            powers = jnp.exp2((scores - highest) * (SCALE * LOG2E))
            inverse = 1.0 / jnp.sum(powers, axis=-1, keepdims=True)
            low = powers.astype(BF)
            probs_ref[half, head] = low
            mixed = mul(low, heads_ref[2, :, cols], NN) * inverse
            mixed_ref[half, :, cols] = mixed.astype(BF)
            inverses = jnp.where(lane == half * 4 + head, inverse, inverses)
    inv_ref[...] = inverses
    for chunk in range(4):
        cols = slice(chunk * 256, (chunk + 1) * 256)
        wide[:, cols] = (
            x_ref[:, cols].astype(F32)
            + mul(mixed_ref[0], wo_own[:, cols], NN)
            + mul(mixed_ref[1], wo_other[:, cols], NN)
            + out_bias[:, cols]
        )
    middle = wide[...]
    middle_ref[...] = middle.astype(BF)
    unit, _ = unit_of(middle)
    normed_two[...] = (unit * gain_ref[...] + shift_ref[...]).astype(BF)
    for half, (weight, bias) in enumerate(((wu_own, ub_own), (wu_other, ub_other))):
        for chunk in range(2):
            cols = slice(chunk * 256, (chunk + 1) * 256)
            hidden = mul(normed_two[...], weight[:, cols], NN) + bias[:, cols].astype(F32)
            square = hidden * hidden
            gate = jnp.tanh(GELU_A * (hidden + GELU_B * (square * hidden)))
            lift = 0.5 * (1.0 + gate)
            act[half, :, cols] = (hidden * lift).astype(BF)
            slope = lift + (0.5 * GELU_A) * hidden * (1.0 - gate * gate) * (
                1.0 + (3.0 * GELU_B) * square
            )
            slope_ref[half, :, cols] = slope.astype(BF)
    for chunk in range(4):
        cols = slice(chunk * 256, (chunk + 1) * 256)
        block_ref[:, cols] = (
            wide[:, cols]
            + mul(act[0], wd_own[:, cols], NN)
            + mul(act[1], wd_other[:, cols], NN)
            + down_bias[:, cols]
        )
    for half in range(2):
        acc[half] += mul(act[half], g_ref[...], TN)
    gsum_ref[0:1, :] += column_sum(g_ref[...].astype(F32))

    @pl.when(step == pl.num_programs(0) - 1)
    def _():
        gdown_ref[...] = acc[...].astype(BF)


def feed_back_kernel(
    g_ref,
    slope_ref,
    middle_ref,
    mixed_ref,
    inv_ref,
    wd_own,
    wd_other,
    wu_own,
    wu_other,
    wo_own,
    wo_other,
    gain_ref,
    shift_ref,
    dmid_ref,
    dmix_ref,
    dot_ref,
    gup_ref,
    gout_ref,
    vec_ref,
    ubias_ref,
    acc_up,
    acc_out,
    normed_two,
    unit_ref,
    dhid,
    wide,
):
    step = pl.program_id(0)

    @pl.when(step == 0)
    def _():
        acc_up[...] = jnp.zeros_like(acc_up)
        acc_out[...] = jnp.zeros_like(acc_out)
        vec_ref[...] = jnp.zeros_like(vec_ref)
        ubias_ref[...] = jnp.zeros_like(ubias_ref)

    for half, weight in enumerate((wd_own, wd_other)):
        for chunk in range(2):
            cols = slice(chunk * 256, (chunk + 1) * 256)
            down = mul(g_ref[...], weight[cols, :], NT)
            dhid[half, :, cols] = (down * slope_ref[half, :, cols].astype(F32)).astype(BF)
        ubias_ref[half : half + 1, :] += column_sum(dhid[half].astype(F32))
    unit, inverse = unit_of(middle_ref[...].astype(F32))
    unit_ref[...] = unit
    normed_two[...] = (unit * gain_ref[...] + shift_ref[...]).astype(BF)
    for half in range(2):
        acc_up[half] += mul(dhid[half], normed_two[...], TN)
    for chunk in range(4):
        rows = slice(chunk * 256, (chunk + 1) * 256)
        wide[:, rows] = mul(dhid[0], wu_own[rows, :], NT) + mul(dhid[1], wu_other[rows, :], NT)
    upstream = wide[...]
    unit = unit_ref[...]
    vec_ref[0:1, :] += column_sum(upstream * unit)
    vec_ref[1:2, :] += column_sum(upstream)
    dmid = g_ref[...].astype(F32) + norm_back(upstream, unit, inverse, gain_ref[...])
    vec_ref[2:3, :] += column_sum(dmid)
    dmid_ref[...] = dmid.astype(BF)
    lane = lax.broadcasted_iota(jnp.int32, (LAT, HEAD), 1)
    dots = jnp.zeros((LAT, HEAD), F32)
    for half, weight in enumerate((wo_own, wo_other)):
        acc_out[half] += mul(mixed_ref[half], dmid_ref[...], TN)
        for pair in range(2):
            both = mul(dmid_ref[...], weight[pair * 256 : (pair + 1) * 256, :], NT)
            for one in range(2):
                head = pair * 2 + one
                cols = slice(head * HEAD, (head + 1) * HEAD)
                place = half * 4 + head
                scaled = both[:, one * HEAD : (one + 1) * HEAD] * inv_ref[:, place : place + 1]
                dmix_ref[half, :, cols] = scaled.astype(BF)
                total = jnp.sum(
                    scaled * mixed_ref[half, :, cols].astype(F32), axis=-1, keepdims=True
                )
                dots = jnp.where(lane == place, total, dots)
    dot_ref[...] = dots

    @pl.when(step == pl.num_programs(0) - 1)
    def _():
        gup_ref[...] = acc_up[...].astype(BF)
        gout_ref[...] = acc_out[...].astype(BF)


def attend_back_kernel(
    normed_ref,
    own_ref,
    other_ref,
    probs_ref,
    dmix_ref,
    dot_ref,
    dheads_ref,
    gin_ref,
    vec_ref,
    acc,
    joined,
    dots_now,
):
    group, step = pl.program_id(0), pl.program_id(1)
    per_group = HALF // HEAD // GROUPS
    width = per_group * HEAD

    @pl.when(step == 0)
    def _():
        acc[...] = jnp.zeros_like(acc)
        vec_ref[...] = jnp.zeros_like(vec_ref)

    @pl.when(group == 0)
    def _():
        for place in range(4):
            lane = (place // 2) * 4 + place % 2
            dots_now[:, place : place + 1] = dot_ref[:, lane : lane + 1]

    @pl.when(group == 1)
    def _():
        for place in range(4):
            lane = (place // 2) * 4 + 2 + place % 2
            dots_now[:, place : place + 1] = dot_ref[:, lane : lane + 1]

    for half, heads_ref in enumerate((own_ref, other_ref)):
        for head in range(per_group):
            cols = slice(head * HEAD, (head + 1) * HEAD)
            place = half * per_group + head
            probs = probs_ref[half, head]
            upstream = dmix_ref[half, :, cols]
            d_probs = mul(upstream, heads_ref[2, :, cols], NT) - dots_now[:, place : place + 1]
            d_scores = (probs.astype(F32) * d_probs).astype(BF)
            d_query = (mul(d_scores, heads_ref[1, :, cols], NN) * SCALE).astype(BF)
            d_keys = (mul(heads_ref[0, :, cols], d_scores, TN) * SCALE).T.astype(BF)
            d_values = mul(probs, upstream, TN).astype(BF)
            for which, value in enumerate((d_query, d_keys, d_values)):
                dheads_ref[half, which, :, cols] = value
                first = half * 3 * width + which * width + head * HEAD
                joined[:, first : first + HEAD] = value
    vec_ref[0:1, :] += column_sum(joined[...].astype(F32))
    for chunk in range(4):
        rows = slice(chunk * 256, (chunk + 1) * 256)
        acc[rows, :] += mul(normed_ref[:, rows], joined[...], TN)

    @pl.when(step == pl.num_programs(1) - 1)
    def _():
        for half in range(2):
            cols = slice(half * 3 * width, (half + 1) * 3 * width)
            gin_ref[half] = acc[:, cols].astype(BF)


def last_kernel(
    x_ref,
    dheads_ref,
    dmid_ref,
    w_own,
    w_other,
    gain_ref,
    grad_ref,
    vec_ref,
    wide,
):
    step = pl.program_id(0)

    @pl.when(step == 0)
    def _():
        vec_ref[...] = jnp.zeros_like(vec_ref)

    for chunk in range(4):
        rows = slice(chunk * 256, (chunk + 1) * 256)
        total = None
        for half, weight in enumerate((w_own, w_other)):
            for which in range(3):
                term = mul(dheads_ref[half, which], weight[which, rows, :], NT)
                total = term if total is None else total + term
        wide[:, rows] = total
    unit, inverse = unit_of(x_ref[...].astype(F32))
    upstream = wide[...]
    vec_ref[0:1, :] += column_sum(upstream * unit)
    vec_ref[1:2, :] += column_sum(upstream)
    grad_ref[...] = dmid_ref[...].astype(F32) + norm_back(upstream, unit, inverse, gain_ref[...])


def reduce_kernel(jobs, *refs):
    count = len(jobs)
    sources, results = refs[:count], refs[count : 2 * count]
    scratch = refs[2 * count : -1]
    own_sem = refs[-1]
    greet(reduction_partners())
    for n, job in enumerate(jobs):
        mine = scratch[6 * n : 6 * n + 6]
        copy = pltpu.make_async_copy(sources[n].at[0], mine[0], own_sem.at[n])
        copy.start()
        copy.wait()
        for tick in range(job.ticks):
            job.tick(mine, tick, sources[n].at[1])
        out = pltpu.make_async_copy(mine[1], results[n], own_sem.at[n])
        out.start()
        out.wait()


def params(**more):
    return pltpu.CompilerParams(vmem_limit_bytes=VMEM_LIMIT, **more)


def per_device(
    latents,
    first_scale,
    first_shift,
    input_weights,
    input_bias,
    output_weight,
    output_bias,
    second_scale,
    second_shift,
    up_weight,
    up_bias,
    down_weight,
    down_bias,
    output_grad,
):
    rows = latents.shape[0]
    images = rows // LAT
    dp, mp = lax.axis_size("dp"), lax.axis_size("mp")
    direct = dp == 16 and mp == 2
    factor = LAT / (rows * dp * mp)
    row = lambda v: v[None, :]
    first_scale, first_shift = row(first_scale), row(first_shift)
    second_scale, second_shift = row(second_scale), row(second_shift)
    output_bias, down_bias = row(output_bias), row(down_bias)

    if direct:
        own = (input_weights, output_weight, up_weight, down_weight)
        small = jnp.concatenate(
            [input_bias, up_bias[None], jnp.zeros((13, HALF), BF)], axis=0
        )
    else:
        gather = lambda v, axis: lax.all_gather(v, "mp", axis=axis, tiled=True)
        w_in, w_out = gather(input_weights, 2), gather(output_weight, 0)
        w_up, w_down = gather(up_weight, 1), gather(down_weight, 0)
        small = jnp.concatenate([gather(input_bias, 1), gather(up_bias, 0)[None]], axis=0)
        own = (w_in[..., :HALF], w_out[:HALF], w_up[:, :HALF], w_down[:HALF])
        others = (w_in[..., HALF:], w_out[HALF:], w_up[:, HALF:], w_down[HALF:], small[:, HALF:])
        small = small[:, :HALF]

    w_shapes = [(3, D, HALF), (HALF, D), (D, HALF), (HALF, D), (16, HALF)]
    normed_shape = shape_of((rows, D), BF)
    heads_shape = shape_of((3, rows, HALF), BF)
    heads_spec = pl.BlockSpec((3, LAT, HALF), lambda i: (0, i, 0))
    vector = kept_spec((1, D))
    bias_spec = whole_spec(small.shape)
    outs = pl.pallas_call(
        functools.partial(first_kernel, direct),
        grid=(images,),
        name="project_own",
        in_specs=[row_spec(D), vector, vector, bias_spec, whole_spec((3, D, HALF))]
        + ([ANY] * 5 if direct else []),
        out_specs=[row_spec(D), heads_spec] + ([ANY] * 5 if direct else []),
        out_shape=[normed_shape, heads_shape]
        + ([shape_of(s, BF) for s in w_shapes] if direct else []),
        scratch_shapes=[pltpu.SemaphoreType.DMA((5,))] * 2 if direct else [],
        compiler_params=params(collective_id=0, has_side_effects=True) if direct else params(),
        cost_estimate=cost(6 * rows * D * HALF, 12 * rows * D),
    )(
        latents,
        first_scale,
        first_shift,
        small,
        own[0],
        *((own + (small,)) if direct else ()),
    )
    normed_one, heads_own = outs[:2]
    if direct:
        others = outs[2:]
    w_in_other, w_out_other, w_up_other, w_down_other, small_other = others
    w_in_own, w_out_own, w_up_own, w_down_own = own

    half_spec = pl.BlockSpec((2, LAT, HALF), lambda i: (0, i, 0))
    half_shape = shape_of((2, rows, HALF), BF)
    head_count = HALF // HEAD
    probs_shape = shape_of((2, head_count, rows, LAT), BF)
    probs_spec = pl.BlockSpec((2, head_count, LAT, LAT), lambda i: (0, 0, i, 0))
    square = (HALF, D)
    tall = (D, HALF)
    (
        block_output,
        heads_other,
        probs,
        inverses,
        mixed,
        middle,
        slope,
        g_down,
        g_sum,
    ) = pl.pallas_call(
        forward_kernel,
        grid=(images,),
        name="forward",
        in_specs=[
            row_spec(D),
            row_spec(D),
            heads_spec,
            row_spec(D),
            whole_spec((3, D, HALF)),
            whole_spec(small_other.shape),
            whole_spec(square),
            whole_spec(square),
            vector,
            vector,
            vector,
            whole_spec(tall),
            whole_spec(tall),
            kept_spec((1, HALF)),
            kept_spec((1, HALF)),
            whole_spec(square),
            whole_spec(square),
            vector,
        ],
        out_specs=[
            row_spec(D),
            heads_spec,
            probs_spec,
            row_spec(HEAD),
            half_spec,
            row_spec(D),
            half_spec,
            kept_spec((2, HALF, D)),
            kept_spec((8, D)),
        ],
        out_shape=[
            shape_of((rows, D), F32),
            heads_shape,
            probs_shape,
            shape_of((rows, HEAD), F32),
            half_shape,
            shape_of((rows, D), BF),
            half_shape,
            shape_of((2, HALF, D), BF),
            shape_of((8, D), F32),
        ],
        scratch_shapes=[
            pltpu.VMEM((2, HALF, D), F32),
            pltpu.VMEM((LAT, D), BF),
            pltpu.VMEM((2, LAT, HALF), BF),
            pltpu.VMEM((LAT, D), F32),
        ],
        compiler_params=params(),
        cost_estimate=cost(16 * rows * D * D, 24 * rows * D),
    )(
        latents,
        normed_one,
        heads_own,
        output_grad,
        w_in_other,
        small_other,
        w_out_own,
        w_out_other,
        output_bias,
        second_scale,
        second_shift,
        w_up_own,
        w_up_other,
        small[2:3],
        small_other[2:3],
        w_down_own,
        w_down_other,
        down_bias,
    )

    d_middle, d_mixed, d_dots, g_up, g_out, vec_two, vec_up = pl.pallas_call(
        feed_back_kernel,
        grid=(images,),
        name="feed_back",
        in_specs=[
            row_spec(D),
            half_spec,
            row_spec(D),
            half_spec,
            row_spec(HEAD),
            whole_spec(square),
            whole_spec(square),
            whole_spec(tall),
            whole_spec(tall),
            whole_spec(square),
            whole_spec(square),
            vector,
            vector,
        ],
        out_specs=[
            row_spec(D),
            half_spec,
            row_spec(HEAD),
            kept_spec((2, HALF, D)),
            kept_spec((2, HALF, D)),
            kept_spec((8, D)),
            kept_spec((8, HALF)),
        ],
        out_shape=[
            shape_of((rows, D), BF),
            half_shape,
            shape_of((rows, HEAD), F32),
            shape_of((2, HALF, D), BF),
            shape_of((2, HALF, D), BF),
            shape_of((8, D), F32),
            shape_of((8, HALF), F32),
        ],
        scratch_shapes=[
            pltpu.VMEM((2, HALF, D), F32),
            pltpu.VMEM((2, HALF, D), F32),
            pltpu.VMEM((LAT, D), BF),
            pltpu.VMEM((LAT, D), F32),
            pltpu.VMEM((2, LAT, HALF), BF),
            pltpu.VMEM((LAT, D), F32),
        ],
        compiler_params=params(),
        cost_estimate=cost(10 * rows * D * D, 14 * rows * D),
    )(
        output_grad,
        slope,
        middle,
        mixed,
        inverses,
        w_down_own,
        w_down_other,
        w_up_own,
        w_up_other,
        w_out_own,
        w_out_other,
        second_scale,
        second_shift,
    )

    per_group = head_count // GROUPS
    width = per_group * HEAD
    group_heads = pl.BlockSpec((3, LAT, width), lambda g, i: (0, i, g))
    d_heads, g_in, vec_in = pl.pallas_call(
        attend_back_kernel,
        grid=(GROUPS, images),
        name="attend_back",
        in_specs=[
            pl.BlockSpec((LAT, D), lambda g, i: (i, 0)),
            group_heads,
            group_heads,
            pl.BlockSpec((2, per_group, LAT, LAT), lambda g, i: (0, g, i, 0)),
            pl.BlockSpec((2, LAT, width), lambda g, i: (0, i, g)),
            pl.BlockSpec((LAT, HEAD), lambda g, i: (i, 0)),
        ],
        out_specs=[
            pl.BlockSpec((2, 3, LAT, width), lambda g, i: (0, 0, i, g)),
            pl.BlockSpec((None, 2, D, 3 * width), lambda g, i: (g, 0, 0, 0)),
            pl.BlockSpec((None, 8, 6 * width), lambda g, i: (g, 0, 0)),
        ],
        out_shape=[
            shape_of((2, 3, rows, HALF), BF),
            shape_of((GROUPS, 2, D, 3 * width), BF),
            shape_of((GROUPS, 8, 6 * width), F32),
        ],
        scratch_shapes=[
            pltpu.VMEM((D, 6 * width), F32),
            pltpu.VMEM((LAT, 6 * width), BF),
            pltpu.VMEM((LAT, HEAD), F32),
        ],
        compiler_params=params(),
        cost_estimate=cost(8 * rows * D * D, 20 * rows * D),
    )(normed_one, heads_own, heads_other, probs, d_mixed, d_dots)

    latents_grad, vec_one = pl.pallas_call(
        last_kernel,
        grid=(images,),
        name="input_back",
        in_specs=[
            row_spec(D),
            pl.BlockSpec((2, 3, LAT, HALF), lambda i: (0, 0, i, 0)),
            row_spec(D),
            whole_spec((3, D, HALF)),
            whole_spec((3, D, HALF)),
            vector,
        ],
        out_specs=[row_spec(D), kept_spec((8, D))],
        out_shape=[shape_of((rows, D), F32), shape_of((8, D), F32)],
        scratch_shapes=[pltpu.VMEM((LAT, D), F32)],
        compiler_params=params(),
        cost_estimate=cost(6 * rows * D * D, 14 * rows * D),
    )(latents, d_heads, d_middle, w_in_own, w_in_other, first_scale)

    g_first_scale, g_first_shift = vec_one[0], vec_one[1]
    g_second_scale, g_second_shift, g_output_bias = vec_two[0], vec_two[1], vec_two[2]
    g_down_bias = g_sum[0]
    by_group = vec_in[:, 0].reshape(GROUPS, 2, 3, width)
    in_bias = jnp.transpose(by_group, (1, 2, 0, 3)).reshape(2, 3, HALF)
    sharded = jnp.stack([in_bias[:, 0], in_bias[:, 2], vec_up[:2]], axis=1)

    if direct:
        me = lax.axis_index("mp")
        sharded = jnp.where(me == 0, sharded, sharded[::-1])
        sharded = jnp.transpose(sharded, (1, 0, 2)).reshape(3, D)
    else:
        sharded = jnp.transpose(sharded, (1, 0, 2)).reshape(3, D)
    vectors = lax.psum(
        jnp.concatenate(
            [
                jnp.stack(
                    [
                        g_first_scale,
                        g_first_shift,
                        g_output_bias,
                        g_second_scale,
                        g_second_shift,
                        g_down_bias,
                    ]
                ),
                sharded,
            ]
        ),
        ("dp", "mp"),
    )
    vectors = vectors * factor
    own_width = D // mp
    mine = lax.dynamic_slice_in_dim(vectors[6:], lax.axis_index("mp") * own_width, own_width, 1)

    if direct:
        parts = ((0, 384), (384, 768), (768, 1024))
        jobs = [
            Reduction(HALF, D, parts, ORDERS),
            Reduction(HALF, D, parts, ORDERS),
            Reduction(HALF, D, parts, ORDERS),
        ] + [
            Reduction(D, 3 * width, ((0, width), (width, 2 * width), (2 * width, 3 * width)), ORDERS)
        ] * GROUPS
        sources = [g_down, g_up, g_out] + [g_in[g] for g in range(GROUPS)]
        g_down, g_up, g_out, *g_in = pl.pallas_call(
            functools.partial(reduce_kernel, jobs),
            name="reduce",
            in_specs=[ANY] * len(jobs),
            out_specs=[ANY] * len(jobs),
            out_shape=[shape_of((job.rows, job.columns), BF) for job in jobs],
            scratch_shapes=sum([job.scratch() for job in jobs], [])
            + [pltpu.SemaphoreType.DMA((len(jobs),))],
            compiler_params=params(collective_id=1, has_side_effects=True),
        )(*sources)
        g_up = g_up.T
        g_in = jnp.stack([part.reshape(D, 3, width) for part in g_in], axis=2)
        g_in = jnp.transpose(g_in, (1, 0, 2, 3)).reshape(3, D, HALF)
    else:
        g_down, g_up, g_out = (v.reshape(D, D) for v in (g_down, g_up, g_out))
        g_in = jnp.transpose(g_in.reshape(GROUPS, 2, D, 3, width), (3, 2, 1, 0, 4))
        g_in = g_in.reshape(3, D, D)
        scatter = lambda v, axis: lax.psum(
            lax.psum_scatter(v, "mp", scatter_dimension=axis, tiled=True), "dp"
        )
        g_down, g_up, g_out = scatter(g_down, 0), scatter(g_up.T, 1), scatter(g_out, 0)
        g_in = scatter(g_in, 2)

    final = lambda v: v.astype(F32) * factor
    return (
        block_output,
        latents_grad,
        vectors[0],
        vectors[1],
        final(g_in),
        mine[:2],
        final(g_out),
        vectors[2],
        vectors[3],
        vectors[4],
        final(g_up),
        mine[2],
        final(g_down),
        vectors[5],
    )


def solution(mesh):
    return jax.shard_map(
        per_device,
        mesh=mesh,
        in_specs=(
            P(("dp", "mp"), None),
            P(),
            P(),
            P(None, None, "mp"),
            P(None, "mp"),
            P("mp", None),
            P(),
            P(),
            P(),
            P(None, "mp"),
            P("mp"),
            P("mp", None),
            P(),
            P(("dp", "mp"), None),
        ),
        out_specs=(
            P(("dp", "mp"), None),
            P(("dp", "mp"), None),
            P(),
            P(),
            P(None, None, "mp"),
            P(None, "mp"),
            P("mp", None),
            P(),
            P(),
            P(),
            P(None, "mp"),
            P("mp"),
            P("mp", None),
            P(),
        ),
        check_vma=False,
    )
```

```python
import functools

import jax
import jax.numpy as jnp
from jax import lax
from jax.experimental import pallas as pl
from jax.experimental.pallas import tpu as pltpu
from jax.sharding import PartitionSpec as P

D = 1024
HEAD = 128
HEADS = 8
LAT = 512
HALF = 512
GROUPS = 2
EPS = 1e-05
SCALE = HEAD ** (-0.5)
LOG2E = 1.4426950408889634
GELU_A = 0.7978845608028654
GELU_B = 0.044715
MESH = pl.DeviceIdType.MESH
NN = (((1,), (0,)), ((), ()))
NT = (((1,), (1,)), ((), ()))
TN = (((0,), (0,)), ((), ()))
BF = jnp.bfloat16
F32 = jnp.float32
VMEM_LIMIT = 60 << 20


def mul(a, b, dims):
    return lax.dot_general(a, b, dims, preferred_element_type=F32)


def unit_of(rows):
    centred = rows - jnp.mean(rows, axis=-1, keepdims=True)
    inverse = lax.rsqrt(jnp.mean(centred * centred, axis=-1, keepdims=True) + EPS)
    return centred * inverse, inverse


def norm_back(upstream, unit, inverse, gain):
    scaled = upstream * gain
    inner = (
        scaled
        - jnp.mean(scaled, axis=-1, keepdims=True)
        - unit * jnp.mean(scaled * unit, axis=-1, keepdims=True)
    )
    return inverse * inner


def column_sum(values):
    return jnp.sum(values.reshape(values.shape[0] // 8, 8, values.shape[1]), axis=0)


def row_spec(width):
    return pl.BlockSpec((LAT, width), lambda i: (i, 0))


def whole_spec(shape):
    return pl.BlockSpec(shape, lambda *_: (0,) * len(shape), pipeline_mode=pl.Buffered(1))


def kept_spec(shape):
    return pl.BlockSpec(shape, lambda *_: (0,) * len(shape))


ANY = pl.BlockSpec(memory_space=pl.ANY)


def shape_of(shape, dtype):
    return jax.ShapeDtypeStruct(shape, dtype)


def cost(flops, moved):
    return pl.CostEstimate(flops=int(flops), bytes_accessed=int(moved), transcendentals=0)


def dp_flip(bit):
    me = lax.axis_index("dp")
    step = 1 << bit
    on = lax.rem(me // step, 2)
    return (me + step - 2 * step * on, lax.axis_index("mp"))


def core_flip():
    return (lax.axis_index("dp"), 1 - lax.axis_index("mp"))


def greet(partners):
    barrier = pltpu.get_barrier_semaphore()
    for partner in partners:
        pl.semaphore_signal(barrier, inc=1, device_id=partner, device_id_type=MESH)
    pl.semaphore_wait(barrier, len(partners))


def remote(src, dst, send, recv, partner):
    return pltpu.make_async_remote_copy(
        src_ref=src,
        dst_ref=dst,
        send_sem=send,
        recv_sem=recv,
        device_id=partner,
        device_id_type=MESH,
    )


class Reduction:
    def __init__(self, rows, columns, parts, orders):
        self.rows, self.columns, self.parts, self.orders = rows, columns, parts, orders
        self.bits = len(orders[0])
        self.ticks = 2 * self.bits + 2

    def scratch(self):
        stages = 2 * self.bits
        return [
            pltpu.VMEM((self.rows, self.columns), BF),
            pltpu.VMEM((self.rows, self.columns), BF),
            pltpu.VMEM((self.rows, self.columns), BF),
            pltpu.SemaphoreType.DMA((2,)),
            pltpu.SemaphoreType.DMA((len(self.parts), stages)),
            pltpu.SemaphoreType.DMA((len(self.parts), stages)),
            pltpu.SemaphoreType.DMA((2,)),
        ]

    def offset(self, part, level):
        me = lax.axis_index("dp")
        row = 0
        for stage in range(level):
            on = lax.rem(me // (1 << self.orders[part][stage]), 2)
            row = row + on * (self.rows >> (stage + 1))
        return row

    def aligned(self, row, size):
        return pl.ds(pl.multiple_of(row, size), size)

    def columns_of(self, part):
        first, last = self.parts[part]
        return pl.ds(first, last - first)

    def halving(self, refs, part, stage):
        cur, _, recv, _, send_sem, recv_sem = refs[:6]
        size = self.rows >> (stage + 1)
        bit = self.orders[part][stage]
        on = lax.rem(lax.axis_index("dp") // (1 << bit), 2)
        base = self.offset(part, stage)
        cols = self.columns_of(part)
        landing = self.rows - 2 * size
        copy = remote(
            cur.at[self.aligned(base + (1 - on) * size, size), cols],
            recv.at[pl.ds(landing, size), cols],
            send_sem.at[part, stage],
            recv_sem.at[part, stage],
            dp_flip(bit),
        )
        return copy, self.aligned(base + on * size, size), pl.ds(landing, size), cols

    def doubling(self, refs, part, step):
        _, full, _, _, send_sem, recv_sem = refs[:6]
        stage = self.bits - 1 - step
        size = self.rows >> (stage + 1)
        rows = self.aligned(self.offset(part, stage + 1), size)
        cols = self.columns_of(part)
        return remote(
            full.at[rows, cols],
            full.at[rows, cols],
            send_sem.at[part, self.bits + step],
            recv_sem.at[part, self.bits + step],
            dp_flip(self.orders[part][stage]),
        )

    def exchange(self, refs, other):
        return remote(other, refs[1], refs[3].at[0], refs[3].at[1], core_flip())

    def tick(self, refs, tick, other):
        cur, landed, recv = refs[:3]
        parts = range(len(self.parts))
        if tick == 0:
            self.exchange(refs, other).start()
            return
        if tick == 1:
            self.exchange(refs, other).wait()
            cur[...] = (cur[...].astype(F32) + landed[...].astype(F32)).astype(BF)
            for part in parts:
                self.halving(refs, part, 0)[0].start()
            return
        if tick <= self.bits + 1:
            for part in parts:
                copy, keep, landing, cols = self.halving(refs, part, tick - 2)
                copy.wait()
                total = (cur[keep, cols].astype(F32) + recv[landing, cols].astype(F32)).astype(BF)
                if tick <= self.bits:
                    cur[keep, cols] = total
                    self.halving(refs, part, tick - 1)[0].start()
                else:
                    landed[keep, cols] = total
                    self.doubling(refs, part, 0).start()
            return
        step = tick - self.bits - 2
        for part in parts:
            self.doubling(refs, part, step).wait()
            if step + 1 < self.bits:
                self.doubling(refs, part, step + 1).start()


class Task:
    def __init__(self, job, refs, source, result, places, staged=False):
        self.job, self.refs, self.source, self.result = job, refs, source, result
        self.places, self.staged = places, staged

    def load(self):
        return pltpu.make_async_copy(self.source.at[0], self.refs[0], self.refs[6].at[0])

    def store(self):
        return pltpu.make_async_copy(self.refs[1], self.result, self.refs[6].at[1])

    def run(self, tick):
        if tick == 0 and not self.staged:
            self.load().start()
        if tick == 1 and not self.staged:
            self.load().wait()
        self.job.tick(self.refs, tick, self.source if self.staged else self.source.at[1])
        if tick == self.job.ticks - 1:
            self.store().start()

    def finish(self):
        self.store().wait()


def run_tasks(step, place, tasks):
    for now in sorted({at[0] for task in tasks for at in task.places if at[1] == place}):

        @pl.when(step == now)
        def _():
            for task in tasks:
                for tick, at in enumerate(task.places):
                    if at == (now, place):
                        task.run(tick)


ORDERS = ((0, 1, 2, 3), (1, 2, 3, 0), (2, 3, 0, 1))


def halves(*numbers):
    return tuple((n // 2, n % 2) for n in numbers)


FEED_PLACES = halves(0, 1, 2, 3, 4, 5, 6, 7, 8, 10)
ATTEND_PLACES = (
    halves(0, 1, 3, 5, 6, 7, 8, 9, 11, 13),
    halves(2, 3, 6, 8, 9, 10, 11, 12, 14, 16),
    ((7, 2),) + halves(17, 20, 22, 24, 25, 26, 28, 30) + ((15, 2),),
)
LAST_PLACES = halves(0, 1, 4, 6, 8, 9, 10, 12, 14) + ((7, 2),)


def reduction_partners():
    return [core_flip()] + [dp_flip(bit) for bit in range(4)]


def first_kernel(
    spread, x_ref, gain_ref, shift_ref, bias_ref, w_in, *refs
):
    step = pl.program_id(0)
    if spread:
        sources = (w_in_any, w_out, w_up, w_down, bias_all) = refs[:5]
        normed_ref, heads_ref = refs[5:7]
        targets = refs[7:12]
        send_sem, recv_sem = refs[12:14]

        def copies():
            return [
                remote(src, dst, send_sem.at[n], recv_sem.at[n], core_flip())
                for n, (src, dst) in enumerate(zip(sources, targets))
            ]

        @pl.when(step == 0)
        def _():
            greet([core_flip()])
            for copy in copies():
                copy.start()
    else:
        normed_ref, heads_ref = refs

    unit, _ = unit_of(x_ref[...].astype(F32))
    normed_ref[...] = (unit * gain_ref[...] + shift_ref[...]).astype(BF)
    project(normed_ref, w_in, bias_ref, heads_ref)

    if spread:

        @pl.when(step == pl.num_programs(0) - 1)
        def _():
            for copy in copies():
                copy.wait()


def project(normed_ref, weights, bias_ref, heads_ref):
    for which in range(3):
        rows = mul(normed_ref[...], weights[which], NN)
        if which != 1:
            place = 0 if which == 0 else 1
            rows = rows + bias_ref[place : place + 1, :].astype(F32)
        heads_ref[which] = rows.astype(BF)


def forward_kernel(
    x_ref,
    normed_ref,
    own_ref,
    g_ref,
    w_in,
    in_bias,
    wo_own,
    wo_other,
    out_bias,
    gain_ref,
    shift_ref,
    wu_own,
    wu_other,
    ub_own,
    ub_other,
    wd_own,
    wd_other,
    down_bias,
    block_ref,
    other_ref,
    probs_ref,
    inv_ref,
    mixed_ref,
    middle_ref,
    slope_ref,
    gdown_ref,
    gsum_ref,
    acc,
    normed_two,
    act,
    wide,
):
    step = pl.program_id(0)

    @pl.when(step == 0)
    def _():
        acc[...] = jnp.zeros_like(acc)
        gsum_ref[...] = jnp.zeros_like(gsum_ref)

    project(normed_ref, w_in, in_bias, other_ref)
    lane = lax.broadcasted_iota(jnp.int32, (LAT, HEAD), 1)
    inverses = jnp.zeros((LAT, HEAD), F32)
    for half, heads_ref in enumerate((own_ref, other_ref)):
        for head in range(HALF // HEAD):
            cols = slice(head * HEAD, (head + 1) * HEAD)
            scores = mul(heads_ref[0, :, cols], heads_ref[1, :, cols], NT)
            highest = jnp.max(scores, axis=-1, keepdims=True)
            powers = jnp.exp2((scores - highest) * (SCALE * LOG2E))
            inverse = 1.0 / jnp.sum(powers, axis=-1, keepdims=True)
            low = powers.astype(BF)
            probs_ref[half, head] = low
            mixed = mul(low, heads_ref[2, :, cols], NN) * inverse
            mixed_ref[half, :, cols] = mixed.astype(BF)
            inverses = jnp.where(lane == half * 4 + head, inverse, inverses)
    inv_ref[...] = inverses
    for chunk in range(4):
        cols = slice(chunk * 256, (chunk + 1) * 256)
        wide[:, cols] = (
            x_ref[:, cols].astype(F32)
            + mul(mixed_ref[0], wo_own[:, cols], NN)
            + mul(mixed_ref[1], wo_other[:, cols], NN)
            + out_bias[:, cols]
        )
    middle = wide[...]
    middle_ref[...] = middle.astype(BF)
    unit, _ = unit_of(middle)
    normed_two[...] = (unit * gain_ref[...] + shift_ref[...]).astype(BF)
    for half, (weight, bias) in enumerate(((wu_own, ub_own), (wu_other, ub_other))):
        for chunk in range(2):
            cols = slice(chunk * 256, (chunk + 1) * 256)
            hidden = mul(normed_two[...], weight[:, cols], NN) + bias[:, cols].astype(F32)
            square = hidden * hidden
            gate = jnp.tanh(GELU_A * (hidden + GELU_B * (square * hidden)))
            lift = 0.5 * (1.0 + gate)
            act[half, :, cols] = (hidden * lift).astype(BF)
            slope = lift + (0.5 * GELU_A) * hidden * (1.0 - gate * gate) * (
                1.0 + (3.0 * GELU_B) * square
            )
            slope_ref[half, :, cols] = slope.astype(BF)
    for chunk in range(4):
        cols = slice(chunk * 256, (chunk + 1) * 256)
        block_ref[:, cols] = (
            wide[:, cols]
            + mul(act[0], wd_own[:, cols], NN)
            + mul(act[1], wd_other[:, cols], NN)
            + down_bias[:, cols]
        )
    for half in range(2):
        acc[half] += mul(act[half], g_ref[...], TN)
    gsum_ref[...] += column_sum(g_ref[...].astype(F32))

    @pl.when(step == pl.num_programs(0) - 1)
    def _():
        gdown_ref[...] = acc[...].astype(BF)


def feed_back_kernel(
    job,
    places,
    g_ref,
    slope_ref,
    middle_ref,
    mixed_ref,
    inv_ref,
    wd_own,
    wd_other,
    wu_own,
    wu_other,
    wo_own,
    wo_other,
    gain_ref,
    shift_ref,
    *refs,
):
    tasks = []
    if job is not None:
        source, refs = refs[0], refs[1:]
    outs, refs = refs[:7], refs[7:]
    if job is not None:
        result, refs = refs[0], refs[1:]
    dmid_ref, dmix_ref, dot_ref, gup_ref, gout_ref, vec_ref, ubias_ref = outs
    acc_up, acc_out, normed_two, unit_ref, dhid, wide = refs[:6]
    if job is not None:
        tasks.append(Task(job, refs[6:], source, result, places))
    step = pl.program_id(0)

    @pl.when(step == 0)
    def _():
        if tasks:
            greet(reduction_partners())
        acc_up[...] = jnp.zeros_like(acc_up)
        acc_out[...] = jnp.zeros_like(acc_out)
        vec_ref[...] = jnp.zeros_like(vec_ref)
        ubias_ref[...] = jnp.zeros_like(ubias_ref)

    run_tasks(step, 0, tasks)
    for half, weight in enumerate((wd_own, wd_other)):
        for chunk in range(2):
            cols = slice(chunk * 256, (chunk + 1) * 256)
            down = mul(g_ref[...], weight[cols, :], NT)
            dhid[half, :, cols] = (down * slope_ref[half, :, cols].astype(F32)).astype(BF)
        ubias_ref[half] += column_sum(dhid[half].astype(F32))
    unit, inverse = unit_of(middle_ref[...].astype(F32))
    unit_ref[...] = unit
    normed_two[...] = (unit * gain_ref[...] + shift_ref[...]).astype(BF)
    for half in range(2):
        acc_up[half] += mul(dhid[half], normed_two[...], TN)
    for chunk in range(4):
        rows = slice(chunk * 256, (chunk + 1) * 256)
        wide[:, rows] = mul(dhid[0], wu_own[rows, :], NT) + mul(dhid[1], wu_other[rows, :], NT)
    run_tasks(step, 1, tasks)
    upstream = wide[...]
    unit = unit_ref[...]
    vec_ref[0] += column_sum(upstream * unit)
    vec_ref[1] += column_sum(upstream)
    dmid = g_ref[...].astype(F32) + norm_back(upstream, unit, inverse, gain_ref[...])
    vec_ref[2] += column_sum(dmid)
    dmid_ref[...] = dmid.astype(BF)
    lane = lax.broadcasted_iota(jnp.int32, (LAT, HEAD), 1)
    dots = jnp.zeros((LAT, HEAD), F32)
    for half, weight in enumerate((wo_own, wo_other)):
        acc_out[half] += mul(mixed_ref[half], dmid_ref[...], TN)
        for pair in range(2):
            both = mul(dmid_ref[...], weight[pair * 256 : (pair + 1) * 256, :], NT)
            for one in range(2):
                head = pair * 2 + one
                cols = slice(head * HEAD, (head + 1) * HEAD)
                place = half * 4 + head
                scaled = both[:, one * HEAD : (one + 1) * HEAD] * inv_ref[:, place : place + 1]
                dmix_ref[half, :, cols] = scaled.astype(BF)
                total = jnp.sum(
                    scaled * mixed_ref[half, :, cols].astype(F32), axis=-1, keepdims=True
                )
                dots = jnp.where(lane == place, total, dots)
    dot_ref[...] = dots

    @pl.when(step == pl.num_programs(0) - 1)
    def _():
        gup_ref[...] = acc_up[...].astype(BF)
        gout_ref[...] = acc_out[...].astype(BF)
        for task in tasks:
            task.finish()


def attend_back_kernel(
    jobs,
    places,
    normed_ref,
    own_ref,
    other_ref,
    probs_ref,
    dmix_ref,
    dot_ref,
    *refs,
):
    tasks, count = [], len(jobs)
    if jobs:
        sources, refs = refs[: count - 1], refs[count - 1 :]
    dheads_ref, gin_ref, vec_ref = refs[:3]
    refs = refs[3:]
    if jobs:
        results, refs = refs[:count], refs[count:]
    acc, joined, dots_now = refs[:3]
    if jobs:
        staged, refs = refs[3], refs[4:]
        for n, job in enumerate(jobs):
            mine = refs[7 * n : 7 * n + 7]
            last = n == count - 1
            tasks.append(Task(job, mine, staged if last else sources[n], results[n], places[n], last))
    group, step = pl.program_id(0), pl.program_id(1)
    now = group * pl.num_programs(1) + step
    per_group = HALF // HEAD // GROUPS
    width = per_group * HEAD

    if tasks:

        @pl.when(now == 0)
        def _():
            greet(reduction_partners())

    @pl.when(step == 0)
    def _():
        acc[...] = jnp.zeros_like(acc)
        vec_ref[...] = jnp.zeros_like(vec_ref)

    @pl.when(group == 0)
    def _():
        for place in range(4):
            lane = (place // 2) * 4 + place % 2
            dots_now[:, place : place + 1] = dot_ref[:, lane : lane + 1]

    @pl.when(group == 1)
    def _():
        for place in range(4):
            lane = (place // 2) * 4 + 2 + place % 2
            dots_now[:, place : place + 1] = dot_ref[:, lane : lane + 1]

    run_tasks(now, 0, tasks)
    for half, heads_ref in enumerate((own_ref, other_ref)):
        for head in range(per_group):
            cols = slice(head * HEAD, (head + 1) * HEAD)
            place = half * per_group + head
            probs = probs_ref[half, head]
            upstream = dmix_ref[half, :, cols]
            d_probs = mul(upstream, heads_ref[2, :, cols], NT) - dots_now[:, place : place + 1]
            d_scores = (probs.astype(F32) * d_probs).astype(BF)
            d_query = (mul(d_scores, heads_ref[1, :, cols], NN) * SCALE).astype(BF)
            d_keys = (mul(heads_ref[0, :, cols], d_scores, TN) * SCALE).T.astype(BF)
            d_values = mul(probs, upstream, TN).astype(BF)
            for which, value in enumerate((d_query, d_keys, d_values)):
                dheads_ref[half, which, :, cols] = value
                first = half * 3 * width + which * width + head * HEAD
                joined[:, first : first + HEAD] = value
            if half == 1 and head == per_group - 1:
                run_tasks(now, 1, tasks)
    vec_ref[...] += column_sum(joined[...].astype(F32))
    for chunk in range(4):
        rows = slice(chunk * 256, (chunk + 1) * 256)
        acc[rows, :] += mul(normed_ref[:, rows], joined[...], TN)

    @pl.when((now if tasks else step) == pl.num_programs(1) * (GROUPS if tasks else 1) - 1)
    def _():
        for half in range(2):
            cols = slice(half * 3 * width, (half + 1) * 3 * width)
            gin_ref[half] = acc[:, cols].astype(BF)

    if tasks:

        @pl.when(now == pl.num_programs(1) - 1)
        def _():
            tasks[-1].refs[0][...] = acc[:, : 3 * width].astype(BF)
            staged[...] = acc[:, 3 * width :].astype(BF)

    run_tasks(now, 2, tasks)

    if tasks:

        @pl.when(now == pl.num_programs(0) * pl.num_programs(1) - 1)
        def _():
            for task in tasks:
                task.finish()


def pack_vectors(vec_ref, two_ref, sum_ref, up_ref, in_ref, out_ref):
    total = lambda v: jnp.sum(v, axis=0, keepdims=True)
    width = HALF // GROUPS
    out_ref[...] = jnp.zeros_like(out_ref)
    out_ref[0:1, :] = total(vec_ref[0])
    out_ref[1:2, :] = total(vec_ref[1])
    out_ref[2:3, :] = total(two_ref[2])
    out_ref[3:4, :] = total(two_ref[0])
    out_ref[4:5, :] = total(two_ref[1])
    out_ref[5:6, :] = total(sum_ref[...])
    for half in range(2):
        for group in range(GROUPS):
            cols = slice(half * HALF + group * width, half * HALF + (group + 1) * width)
            for row, which in ((6, 0), (7, 2)):
                first = (half * 3 + which) * width
                out_ref[row : row + 1, cols] = total(in_ref[group, :, first : first + width])
        out_ref[8:9, half * HALF : (half + 1) * HALF] = total(up_ref[half])


def sum_vectors(held, landed, send_sem, recv_sem):
    partners = reduction_partners()
    for stage, partner in enumerate(partners):
        copy = remote(
            held.at[stage], landed.at[stage], send_sem.at[stage], recv_sem.at[stage], partner
        )
        copy.start()
        copy.wait()
        got = landed[stage]
        if stage == 0:
            crossed = jnp.concatenate([got[:, HALF:], got[:, :HALF]], axis=1)
            row = lax.broadcasted_iota(jnp.int32, got.shape, 0)
            got = jnp.where(row < 6, got, crossed)
        held[stage + 1] = held[stage] + got


def last_kernel(
    job,
    places,
    factor,
    x_ref,
    dheads_ref,
    dmid_ref,
    w_own,
    w_other,
    gain_ref,
    two_ref,
    sum_ref,
    up_ref,
    in_ref,
    *refs,
):
    tasks = []
    if job is not None:
        source, refs = refs[0], refs[1:]
    (grad_ref, total_ref), refs = refs[:2], refs[2:]
    if job is not None:
        result, refs = refs[0], refs[1:]
    (wide, vec_ref), refs = refs[:2], refs[2:]
    if job is not None:
        vectors, refs = refs[:4], refs[4:]
        tasks.append(Task(job, refs, source, result, places))
    step = pl.program_id(0)
    last = pl.num_programs(0) - 1

    @pl.when(step == 0)
    def _():
        if tasks:
            greet(reduction_partners())
        vec_ref[...] = jnp.zeros_like(vec_ref)

    run_tasks(step, 0, tasks)
    for chunk in range(4):
        rows = slice(chunk * 256, (chunk + 1) * 256)
        total = None
        for half, weight in enumerate((w_own, w_other)):
            for which in range(3):
                term = mul(dheads_ref[half, which], weight[which, rows, :], NT)
                total = term if total is None else total + term
        wide[:, rows] = total
    run_tasks(step, 1, tasks)
    unit, inverse = unit_of(x_ref[...].astype(F32))
    upstream = wide[...]
    vec_ref[0] += column_sum(upstream * unit)
    vec_ref[1] += column_sum(upstream)
    grad = dmid_ref[...].astype(F32) + norm_back(upstream, unit, inverse, gain_ref[...])
    grad_ref[...] = grad.astype(BF)
    run_tasks(step, 2, tasks)

    @pl.when(step == last)
    def _():
        if tasks:
            pack_vectors(vec_ref, two_ref, sum_ref, up_ref, in_ref, vectors[0].at[0])
            sum_vectors(*vectors)
            total_ref[...] = vectors[0][len(reduction_partners())] * factor
        else:
            pack_vectors(vec_ref, two_ref, sum_ref, up_ref, in_ref, total_ref)
        for task in tasks:
            task.finish()


def finish_kernel(factor, lat_ref, *refs):
    if len(refs) > 1:
        down_in, up_in, out_in, in_a, in_b, lat_out, down_out, up_out, out_out, in_out = refs
        width = HALF // GROUPS
        down_out[...] = down_in[...].astype(F32) * factor
        out_out[...] = out_in[...].astype(F32) * factor
        up_out[...] = up_in[...].astype(F32).T * factor
        for which in range(3):
            for group, part in enumerate((in_a, in_b)):
                in_out[which, :, group * width : (group + 1) * width] = (
                    part[:, which * width : (which + 1) * width].astype(F32) * factor
                )
    else:
        (lat_out,) = refs
    lat_out[...] = lat_ref[...].astype(F32)


def params(**more):
    return pltpu.CompilerParams(vmem_limit_bytes=VMEM_LIMIT, **more)


def per_device(
    latents,
    first_scale,
    first_shift,
    input_weights,
    input_bias,
    output_weight,
    output_bias,
    second_scale,
    second_shift,
    up_weight,
    up_bias,
    down_weight,
    down_bias,
    output_grad,
):
    rows = latents.shape[0]
    images = rows // LAT
    dp, mp = lax.axis_size("dp"), lax.axis_size("mp")
    direct = dp == 16 and mp == 2
    factor = LAT / (rows * dp * mp)
    row = lambda v: v[None, :]
    first_scale, first_shift = row(first_scale), row(first_shift)
    second_scale, second_shift = row(second_scale), row(second_shift)
    output_bias, down_bias = row(output_bias), row(down_bias)

    if direct:
        own = (input_weights, output_weight, up_weight, down_weight)
        small = jnp.concatenate(
            [input_bias, up_bias[None], jnp.zeros((13, HALF), BF)], axis=0
        )
    else:
        gather = lambda v, axis: lax.all_gather(v, "mp", axis=axis, tiled=True)
        w_in, w_out = gather(input_weights, 2), gather(output_weight, 0)
        w_up, w_down = gather(up_weight, 1), gather(down_weight, 0)
        small = jnp.concatenate([gather(input_bias, 1), gather(up_bias, 0)[None]], axis=0)
        own = (w_in[..., :HALF], w_out[:HALF], w_up[:, :HALF], w_down[:HALF])
        others = (w_in[..., HALF:], w_out[HALF:], w_up[:, HALF:], w_down[HALF:], small[:, HALF:])
        small = small[:, :HALF]

    w_shapes = [(3, D, HALF), (HALF, D), (D, HALF), (HALF, D), (16, HALF)]
    normed_shape = shape_of((rows, D), BF)
    heads_shape = shape_of((3, rows, HALF), BF)
    heads_spec = pl.BlockSpec((3, LAT, HALF), lambda i: (0, i, 0))
    vector = kept_spec((1, D))
    bias_spec = whole_spec(small.shape)
    outs = pl.pallas_call(
        functools.partial(first_kernel, direct),
        grid=(images,),
        name="project_own",
        in_specs=[row_spec(D), vector, vector, bias_spec, whole_spec((3, D, HALF))]
        + ([ANY] * 5 if direct else []),
        out_specs=[row_spec(D), heads_spec] + ([ANY] * 5 if direct else []),
        out_shape=[normed_shape, heads_shape]
        + ([shape_of(s, BF) for s in w_shapes] if direct else []),
        scratch_shapes=[pltpu.SemaphoreType.DMA((5,))] * 2 if direct else [],
        compiler_params=params(collective_id=0, has_side_effects=True) if direct else params(),
        cost_estimate=cost(6 * rows * D * HALF, 12 * rows * D),
    )(
        latents,
        first_scale,
        first_shift,
        small,
        own[0],
        *((own + (small,)) if direct else ()),
    )
    normed_one, heads_own = outs[:2]
    if direct:
        others = outs[2:]
    w_in_other, w_out_other, w_up_other, w_down_other, small_other = others
    w_in_own, w_out_own, w_up_own, w_down_own = own

    half_spec = pl.BlockSpec((2, LAT, HALF), lambda i: (0, i, 0))
    half_shape = shape_of((2, rows, HALF), BF)
    head_count = HALF // HEAD
    probs_shape = shape_of((2, head_count, rows, LAT), BF)
    probs_spec = pl.BlockSpec((2, head_count, LAT, LAT), lambda i: (0, 0, i, 0))
    square = (HALF, D)
    tall = (D, HALF)
    parts = ((0, 384), (384, 768), (768, 1024))
    job = Reduction(HALF, D, parts, ORDERS) if direct else None
    result = shape_of(square, BF)
    (
        block_output,
        heads_other,
        probs,
        inverses,
        mixed,
        middle,
        slope,
        g_down,
        g_sum,
    ) = pl.pallas_call(
        forward_kernel,
        grid=(images,),
        name="forward",
        in_specs=[
            row_spec(D),
            row_spec(D),
            heads_spec,
            row_spec(D),
            whole_spec((3, D, HALF)),
            whole_spec(small_other.shape),
            whole_spec(square),
            whole_spec(square),
            vector,
            vector,
            vector,
            whole_spec(tall),
            whole_spec(tall),
            kept_spec((1, HALF)),
            kept_spec((1, HALF)),
            whole_spec(square),
            whole_spec(square),
            vector,
        ],
        out_specs=[
            row_spec(D),
            heads_spec,
            probs_spec,
            row_spec(HEAD),
            half_spec,
            row_spec(D),
            half_spec,
            kept_spec((2, HALF, D)),
            kept_spec((8, D)),
        ],
        out_shape=[
            shape_of((rows, D), F32),
            heads_shape,
            probs_shape,
            shape_of((rows, HEAD), F32),
            half_shape,
            shape_of((rows, D), BF),
            half_shape,
            shape_of((2, HALF, D), BF),
            shape_of((8, D), F32),
        ],
        scratch_shapes=[
            pltpu.VMEM((2, HALF, D), F32),
            pltpu.VMEM((LAT, D), BF),
            pltpu.VMEM((2, LAT, HALF), BF),
            pltpu.VMEM((LAT, D), F32),
        ],
        compiler_params=params(),
        cost_estimate=cost(16 * rows * D * D, 24 * rows * D),
    )(
        latents,
        normed_one,
        heads_own,
        output_grad,
        w_in_other,
        small_other,
        w_out_own,
        w_out_other,
        output_bias,
        second_scale,
        second_shift,
        w_up_own,
        w_up_other,
        small[2:3],
        small_other[2:3],
        w_down_own,
        w_down_other,
        down_bias,
    )

    d_middle, d_mixed, d_dots, g_up, g_out, vec_two, vec_up, *sums = pl.pallas_call(
        functools.partial(feed_back_kernel, job, FEED_PLACES),
        grid=(images,),
        name="feed_back",
        in_specs=[
            row_spec(D),
            half_spec,
            row_spec(D),
            half_spec,
            row_spec(HEAD),
            whole_spec(square),
            whole_spec(square),
            whole_spec(tall),
            whole_spec(tall),
            whole_spec(square),
            whole_spec(square),
            vector,
            vector,
        ]
        + ([ANY] if direct else []),
        out_specs=[
            row_spec(D),
            half_spec,
            row_spec(HEAD),
            kept_spec((2, HALF, D)),
            kept_spec((2, HALF, D)),
            kept_spec((3, 8, D)),
            kept_spec((2, 8, HALF)),
        ]
        + ([ANY] if direct else []),
        out_shape=[
            shape_of((rows, D), BF),
            half_shape,
            shape_of((rows, HEAD), F32),
            shape_of((2, HALF, D), BF),
            shape_of((2, HALF, D), BF),
            shape_of((3, 8, D), F32),
            shape_of((2, 8, HALF), F32),
        ]
        + ([result] if direct else []),
        scratch_shapes=[
            pltpu.VMEM((2, HALF, D), F32),
            pltpu.VMEM((2, HALF, D), F32),
            pltpu.VMEM((LAT, D), BF),
            pltpu.VMEM((LAT, D), F32),
            pltpu.VMEM((2, LAT, HALF), BF),
            pltpu.VMEM((LAT, D), F32),
        ]
        + (job.scratch() if direct else []),
        compiler_params=params(collective_id=1, has_side_effects=True) if direct else params(),
        cost_estimate=cost(10 * rows * D * D, 14 * rows * D),
    )(
        output_grad,
        slope,
        middle,
        mixed,
        inverses,
        w_down_own,
        w_down_other,
        w_up_own,
        w_up_other,
        w_out_own,
        w_out_other,
        second_scale,
        second_shift,
        *((g_down,) if direct else ()),
    )

    per_group = head_count // GROUPS
    width = per_group * HEAD
    group_heads = pl.BlockSpec((3, LAT, width), lambda g, i: (0, i, g))
    group_job = Reduction(
        D, 3 * width, tuple((n * width, (n + 1) * width) for n in range(3)), ORDERS
    )
    group_result = shape_of((D, 3 * width), BF)
    jobs = [job, job, group_job] if direct else []
    d_heads, g_in, vec_in, *more = pl.pallas_call(
        functools.partial(attend_back_kernel, jobs, ATTEND_PLACES),
        grid=(GROUPS, images),
        name="attend_back",
        in_specs=[
            pl.BlockSpec((LAT, D), lambda g, i: (i, 0)),
            group_heads,
            group_heads,
            pl.BlockSpec((2, per_group, LAT, LAT), lambda g, i: (0, g, i, 0)),
            pl.BlockSpec((2, LAT, width), lambda g, i: (0, i, g)),
            pl.BlockSpec((LAT, HEAD), lambda g, i: (i, 0)),
        ]
        + ([ANY] * 2 if direct else []),
        out_specs=[
            pl.BlockSpec((2, 3, LAT, width), lambda g, i: (0, 0, i, g)),
            pl.BlockSpec(
                (None, 2, D, 3 * width), lambda g, i: (0 if direct else g, 0, 0, 0)
            ),
            pl.BlockSpec((None, 8, 6 * width), lambda g, i: (g, 0, 0)),
        ]
        + [ANY] * len(jobs),
        out_shape=[
            shape_of((2, 3, rows, HALF), BF),
            shape_of((1 if direct else GROUPS, 2, D, 3 * width), BF),
            shape_of((GROUPS, 8, 6 * width), F32),
        ]
        + ([result, result, group_result] if direct else []),
        scratch_shapes=[
            pltpu.VMEM((D, 6 * width), F32),
            pltpu.VMEM((LAT, 6 * width), BF),
            pltpu.VMEM((LAT, HEAD), F32),
        ]
        + ([pltpu.VMEM((D, 3 * width), BF)] if direct else [])
        + sum([one.scratch() for one in jobs], []),
        compiler_params=params(collective_id=2, has_side_effects=True) if direct else params(),
        cost_estimate=cost(8 * rows * D * D, 20 * rows * D),
    )(
        normed_one,
        heads_own,
        heads_other,
        probs,
        d_mixed,
        d_dots,
        *((g_up, g_out) if direct else ()),
    )

    stages = 1 + len(ORDERS[0])
    grad_low, vectors, *last = pl.pallas_call(
        functools.partial(
            last_kernel, group_job if direct else None, LAST_PLACES, factor
        ),
        grid=(images,),
        name="input_back",
        in_specs=[
            row_spec(D),
            pl.BlockSpec((2, 3, LAT, HALF), lambda i: (0, 0, i, 0)),
            row_spec(D),
            whole_spec((3, D, HALF)),
            whole_spec((3, D, HALF)),
            vector,
            kept_spec((3, 8, D)),
            kept_spec((8, D)),
            kept_spec((2, 8, HALF)),
            kept_spec((GROUPS, 8, 6 * width)),
        ]
        + ([ANY] if direct else []),
        out_specs=[row_spec(D), kept_spec((16, D))] + ([ANY] if direct else []),
        out_shape=[shape_of((rows, D), BF), shape_of((16, D), F32)]
        + ([group_result] if direct else []),
        scratch_shapes=[pltpu.VMEM((LAT, D), F32), pltpu.VMEM((2, 8, D), F32)]
        + (
            [
                pltpu.VMEM((stages + 1, 16, D), F32),
                pltpu.VMEM((stages, 16, D), F32),
                pltpu.SemaphoreType.DMA((stages,)),
                pltpu.SemaphoreType.DMA((stages,)),
            ]
            + group_job.scratch()
            if direct
            else []
        ),
        compiler_params=params(collective_id=3, has_side_effects=True) if direct else params(),
        cost_estimate=cost(6 * rows * D * D, 14 * rows * D),
    )(
        latents,
        d_heads,
        d_middle,
        w_in_own,
        w_in_other,
        first_scale,
        vec_two,
        g_sum,
        vec_up,
        vec_in,
        *((g_in.reshape(2, D, 3 * width),) if direct else ()),
    )

    pieces = 8
    cut = rows // pieces
    if direct:
        latents_grad, g_down, g_up, g_out, g_in = pl.pallas_call(
            functools.partial(finish_kernel, factor),
            grid=(pieces,),
            name="finish",
            in_specs=[
                pl.BlockSpec((cut, D), lambda i: (i, 0)),
                pl.BlockSpec((HALF // pieces, D), lambda i: (i, 0)),
                pl.BlockSpec((HALF, D // pieces), lambda i: (0, i)),
                pl.BlockSpec((HALF // pieces, D), lambda i: (i, 0)),
                pl.BlockSpec((D // pieces, 3 * width), lambda i: (i, 0)),
                pl.BlockSpec((D // pieces, 3 * width), lambda i: (i, 0)),
            ],
            out_specs=[
                pl.BlockSpec((cut, D), lambda i: (i, 0)),
                pl.BlockSpec((HALF // pieces, D), lambda i: (i, 0)),
                pl.BlockSpec((D // pieces, HALF), lambda i: (i, 0)),
                pl.BlockSpec((HALF // pieces, D), lambda i: (i, 0)),
                pl.BlockSpec((3, D // pieces, HALF), lambda i: (0, i, 0)),
            ],
            out_shape=[
                shape_of((rows, D), F32),
                shape_of((HALF, D), F32),
                shape_of((D, HALF), F32),
                shape_of((HALF, D), F32),
                shape_of((3, D, HALF), F32),
            ],
            compiler_params=params(),
        )(grad_low, sums[0], more[0], more[1], more[2], last[0])
        mine = vectors[6:9, :HALF]
    else:
        latents_grad = pl.pallas_call(
            functools.partial(finish_kernel, factor),
            grid=(pieces,),
            name="finish",
            in_specs=[pl.BlockSpec((cut, D), lambda i: (i, 0))],
            out_specs=pl.BlockSpec((cut, D), lambda i: (i, 0)),
            out_shape=shape_of((rows, D), F32),
            compiler_params=params(),
        )(grad_low)
        vectors = lax.psum(vectors, ("dp", "mp")) * factor
        own_width = D // mp
        mine = lax.dynamic_slice_in_dim(
            vectors[6:9], lax.axis_index("mp") * own_width, own_width, 1
        )
        g_down, g_up, g_out = (v.reshape(D, D) for v in (g_down, g_up, g_out))
        g_in = jnp.transpose(g_in.reshape(GROUPS, 2, D, 3, width), (3, 2, 1, 0, 4))
        g_in = g_in.reshape(3, D, D)

        def scatter(v, axis):
            v = lax.psum_scatter(v, "mp", scatter_dimension=axis, tiled=True)
            return lax.psum(v, "dp").astype(F32) * factor

        g_down, g_up, g_out = scatter(g_down, 0), scatter(g_up.T, 1), scatter(g_out, 0)
        g_in = scatter(g_in, 2)

    return (
        block_output,
        latents_grad,
        vectors[0],
        vectors[1],
        g_in,
        mine[:2],
        g_out,
        vectors[2],
        vectors[3],
        vectors[4],
        g_up,
        mine[2],
        g_down,
        vectors[5],
    )


def solution(mesh):
    return jax.shard_map(
        per_device,
        mesh=mesh,
        in_specs=(
            P(("dp", "mp"), None),
            P(),
            P(),
            P(None, None, "mp"),
            P(None, "mp"),
            P("mp", None),
            P(),
            P(),
            P(),
            P(None, "mp"),
            P("mp"),
            P("mp", None),
            P(),
            P(("dp", "mp"), None),
        ),
        out_specs=(
            P(("dp", "mp"), None),
            P(("dp", "mp"), None),
            P(),
            P(),
            P(None, None, "mp"),
            P(None, "mp"),
            P("mp", None),
            P(),
            P(),
            P(),
            P(None, "mp"),
            P("mp"),
            P("mp", None),
            P(),
        ),
        check_vma=False,
    )
```

```python
import functools

import jax
import jax.numpy as jnp
from jax import lax
from jax.experimental import pallas as pl
from jax.experimental.pallas import tpu as pltpu
from jax.sharding import PartitionSpec as P

D = 1024
HEAD = 128
HEADS = 8
LAT = 512
HALF = 512
GROUPS = 2
EPS = 1e-05
SCALE = HEAD ** (-0.5)
LOG2E = 1.4426950408889634
GELU_A = 0.7978845608028654
GELU_B = 0.044715
MESH = pl.DeviceIdType.MESH
NN = (((1,), (0,)), ((), ()))
NT = (((1,), (1,)), ((), ()))
TN = (((0,), (0,)), ((), ()))
BF = jnp.bfloat16
F32 = jnp.float32
VMEM_LIMIT = 60 << 20


def mul(a, b, dims):
    return lax.dot_general(a, b, dims, preferred_element_type=F32)


def unit_of(rows):
    centred = rows - jnp.mean(rows, axis=-1, keepdims=True)
    inverse = lax.rsqrt(jnp.mean(centred * centred, axis=-1, keepdims=True) + EPS)
    return centred * inverse, inverse


def norm_back(upstream, unit, inverse, gain):
    scaled = upstream * gain
    inner = (
        scaled
        - jnp.mean(scaled, axis=-1, keepdims=True)
        - unit * jnp.mean(scaled * unit, axis=-1, keepdims=True)
    )
    return inverse * inner


def column_sum(values):
    return jnp.sum(values.reshape(values.shape[0] // 8, 8, values.shape[1]), axis=0)


def row_spec(width):
    return pl.BlockSpec((LAT, width), lambda i: (i, 0))


def whole_spec(shape):
    return pl.BlockSpec(shape, lambda *_: (0,) * len(shape), pipeline_mode=pl.Buffered(1))


def kept_spec(shape):
    return pl.BlockSpec(shape, lambda *_: (0,) * len(shape))


ANY = pl.BlockSpec(memory_space=pl.ANY)


def shape_of(shape, dtype):
    return jax.ShapeDtypeStruct(shape, dtype)


def cost(flops, moved):
    return pl.CostEstimate(flops=int(flops), bytes_accessed=int(moved), transcendentals=0)


def flipped(place, other):
    for bit in (1, 2):
        if other & bit:
            place = place + bit - 2 * bit * lax.rem(place // bit, 2)
    return place


def dp_flip(shift, other):
    me = lax.axis_index("dp")
    place = lax.rem(me // (1 << shift), 4)
    return (me + (flipped(place, other) - place) * (1 << shift), lax.axis_index("mp"))


def start(copies):
    for copy in copies:
        copy.start()


def wait(copies):
    for copy in copies:
        copy.wait()


def core_flip():
    return (lax.axis_index("dp"), 1 - lax.axis_index("mp"))


def greet(partners):
    barrier = pltpu.get_barrier_semaphore()
    for partner in partners:
        pl.semaphore_signal(barrier, inc=1, device_id=partner, device_id_type=MESH)
    pl.semaphore_wait(barrier, len(partners))


def remote(src, dst, send, recv, partner):
    return pltpu.make_async_remote_copy(
        src_ref=src,
        dst_ref=dst,
        send_sem=send,
        recv_sem=recv,
        device_id=partner,
        device_id_type=MESH,
    )


class Reduction:
    def __init__(self, rows, columns, parts, orders):
        self.rows, self.columns, self.parts, self.orders = rows, columns, parts, orders
        self.stages = len(orders[0])
        self.ticks = 2 * self.stages + 2

    def scratch(self):
        copies = (len(self.parts), 2 * self.stages, 3)
        return [
            pltpu.VMEM((self.rows, self.columns), BF),
            pltpu.VMEM((self.rows, self.columns), BF),
            pltpu.VMEM((self.rows, self.columns), BF),
            pltpu.SemaphoreType.DMA((2,)),
            pltpu.SemaphoreType.DMA(copies),
            pltpu.SemaphoreType.DMA(copies),
            pltpu.SemaphoreType.DMA((2,)),
        ]

    def place(self, part, stage):
        shift, members = self.orders[part][stage]
        return lax.rem(lax.axis_index("dp") // (1 << shift), members)

    def size(self, stage):
        rows = self.rows
        for _, members in self.orders[0][: stage + 1]:
            rows //= members
        return rows

    def others(self, stage):
        return (1,) if self.orders[0][stage][1] == 2 else (3, 1, 2)

    def offset(self, part, level):
        row = 0
        for stage in range(level):
            row = row + self.place(part, stage) * self.size(stage)
        return row

    def aligned(self, row, size):
        return pl.ds(pl.multiple_of(row, size), size)

    def columns_of(self, part):
        first, last = self.parts[part]
        return pl.ds(first, last - first)

    def partner(self, part, stage, other):
        return dp_flip(self.orders[part][stage][0], other)

    def landing(self, stage, other):
        size = self.size(stage)
        first = self.rows - self.orders[0][stage][1] * size
        return pl.ds(first + (other - 1) * size, size)

    def adding(self, refs, part, stage):
        cur, _, recv, _, send_sem, recv_sem = refs[:6]
        size = self.size(stage)
        base, cols = self.offset(part, stage), self.columns_of(part)
        copies = []
        for other in self.others(stage):
            theirs = flipped(self.place(part, stage), other)
            copies.append(
                remote(
                    cur.at[self.aligned(base + theirs * size, size), cols],
                    recv.at[self.landing(stage, other), cols],
                    send_sem.at[part, stage, other - 1],
                    recv_sem.at[part, stage, other - 1],
                    self.partner(part, stage, other),
                )
            )
        return copies

    def handing(self, refs, part, step):
        _, full, _, _, send_sem, recv_sem = refs[:6]
        stage = self.stages - 1 - step
        size = self.size(stage)
        rows, cols = self.aligned(self.offset(part, stage + 1), size), self.columns_of(part)
        return [
            remote(
                full.at[rows, cols],
                full.at[rows, cols],
                send_sem.at[part, self.stages + step, other - 1],
                recv_sem.at[part, self.stages + step, other - 1],
                self.partner(part, stage, other),
            )
            for other in self.others(stage)
        ]

    def exchange(self, refs, other):
        return remote(other, refs[1], refs[3].at[0], refs[3].at[1], core_flip())

    def tick(self, refs, tick, other):
        cur, landed, recv = refs[:3]
        parts = range(len(self.parts))
        if tick == 0:
            self.exchange(refs, other).start()
            return
        if tick == 1:
            self.exchange(refs, other).wait()
            cur[...] = (cur[...].astype(F32) + landed[...].astype(F32)).astype(BF)
            for part in parts:
                start(self.adding(refs, part, 0))
            return
        if tick <= self.stages + 1:
            stage = tick - 2
            for part in parts:
                wait(self.adding(refs, part, stage))
                size = self.size(stage)
                keep, cols = self.aligned(self.offset(part, stage + 1), size), self.columns_of(part)
                total = cur[keep, cols].astype(F32)
                for other in sorted(self.others(stage)):
                    total = total + recv[self.landing(stage, other), cols].astype(F32)
                if stage + 1 < self.stages:
                    cur[keep, cols] = total.astype(BF)
                    start(self.adding(refs, part, stage + 1))
                else:
                    landed[keep, cols] = total.astype(BF)
                    start(self.handing(refs, part, 0))
            return
        step = tick - self.stages - 2
        for part in parts:
            wait(self.handing(refs, part, step))
            if step + 1 < self.stages:
                start(self.handing(refs, part, step + 1))


class Task:
    def __init__(self, job, refs, source, result, places, staged=False, piece=0):
        self.job, self.refs, self.places, self.staged = job, refs, places, staged
        window = pl.ds(piece * job.rows, job.rows)
        self.own = None if staged else source.at[0, window]
        self.other = source.at[window] if staged else source.at[1, window]
        self.result = result.at[window]

    def load(self):
        return pltpu.make_async_copy(self.own, self.refs[0], self.refs[6].at[0])

    def store(self):
        return pltpu.make_async_copy(self.refs[1], self.result, self.refs[6].at[1])

    def run(self, tick):
        if tick == 0 and not self.staged:
            self.load().start()
        if tick == 1 and not self.staged:
            self.load().wait()
        self.job.tick(self.refs, tick, self.other)
        if tick == self.job.ticks - 1:
            self.store().start()

    def finish(self):
        self.store().wait()


def run_tasks(step, place, tasks):
    for now in sorted({at[0] for task in tasks for at in task.places if at[1] == place}):

        @pl.when(step == now)
        def _():
            for task in tasks:
                for tick, at in enumerate(task.places):
                    if at == (now, place):
                        task.run(tick)


ORDERS = (((0, 2), (1, 2), (2, 4)), ((1, 2), (0, 2), (2, 4)), ((2, 2), (3, 2), (0, 4)))
SHIFTS = (0, 2)


def halves(steps, *numbers):
    return tuple((n // 2, n % 2) if n < 2 * steps else (steps - 1, 2) for n in numbers)


FEED_PLACES = halves(8, 0, 2, 4, 7, 9, 11, 12, 14)
ATTEND_PLACES = (
    halves(16, 0, 1, 5, 7, 10, 13, 16, 27),
    halves(16, 1, 3, 6, 9, 12, 15, 22, 29),
    ((7, 2),) + halves(16, 17, 20, 22, 25, 27, 29, 32),
    halves(16, 17, 19, 21, 24, 26, 28, 30, 32),
)
LAST_PLACES = (
    halves(8, 0, 1, 3, 5, 7, 10, 12, 16),
    halves(8, 0, 2, 4, 6, 8, 11, 14, 16),
)


def reduction_partners():
    return [core_flip()] + [dp_flip(shift, other) for shift in SHIFTS for other in (1, 2, 3)]


def first_kernel(
    spread, x_ref, gain_ref, shift_ref, bias_ref, w_in, *refs
):
    step = pl.program_id(0)
    if spread:
        sources = (w_in_any, w_out, w_up, w_down, bias_all) = refs[:5]
        normed_ref, heads_ref = refs[5:7]
        targets = refs[7:12]
        send_sem, recv_sem = refs[12:14]

        def copies():
            return [
                remote(src, dst, send_sem.at[n], recv_sem.at[n], core_flip())
                for n, (src, dst) in enumerate(zip(sources, targets))
            ]

        @pl.when(step == 0)
        def _():
            greet([core_flip()])
            for copy in copies():
                copy.start()
    else:
        normed_ref, heads_ref = refs

    unit, _ = unit_of(x_ref[...].astype(F32))
    normed_ref[...] = (unit * gain_ref[...] + shift_ref[...]).astype(BF)
    project(normed_ref, w_in, bias_ref, heads_ref)

    if spread:

        @pl.when(step == pl.num_programs(0) - 1)
        def _():
            for copy in copies():
                copy.wait()


def project(normed_ref, weights, bias_ref, heads_ref):
    for which in range(3):
        rows = mul(normed_ref[...], weights[which], NN)
        if which != 1:
            place = 0 if which == 0 else 1
            rows = rows + bias_ref[place : place + 1, :].astype(F32)
        heads_ref[which] = rows.astype(BF)


def forward_kernel(
    x_ref,
    normed_ref,
    own_ref,
    g_ref,
    w_in,
    in_bias,
    wo_own,
    wo_other,
    out_bias,
    gain_ref,
    shift_ref,
    wu_own,
    wu_other,
    ub_own,
    ub_other,
    wd_own,
    wd_other,
    down_bias,
    block_ref,
    other_ref,
    probs_ref,
    inv_ref,
    mixed_ref,
    middle_ref,
    slope_ref,
    gdown_ref,
    gsum_ref,
    acc,
    normed_two,
    act,
    wide,
):
    step = pl.program_id(0)

    @pl.when(step == 0)
    def _():
        acc[...] = jnp.zeros_like(acc)
        gsum_ref[...] = jnp.zeros_like(gsum_ref)

    project(normed_ref, w_in, in_bias, other_ref)
    lane = lax.broadcasted_iota(jnp.int32, (LAT, HEAD), 1)
    inverses = jnp.zeros((LAT, HEAD), F32)
    for half, heads_ref in enumerate((own_ref, other_ref)):
        for head in range(HALF // HEAD):
            cols = slice(head * HEAD, (head + 1) * HEAD)
            scores = mul(heads_ref[0, :, cols], heads_ref[1, :, cols], NT)
            highest = jnp.max(scores, axis=-1, keepdims=True)
            powers = jnp.exp2((scores - highest) * (SCALE * LOG2E))
            inverse = 1.0 / jnp.sum(powers, axis=-1, keepdims=True)
            low = powers.astype(BF)
            probs_ref[half, head] = low
            mixed = mul(low, heads_ref[2, :, cols], NN) * inverse
            mixed_ref[half, :, cols] = mixed.astype(BF)
            inverses = jnp.where(lane == half * 4 + head, inverse, inverses)
    inv_ref[...] = inverses
    for chunk in range(4):
        cols = slice(chunk * 256, (chunk + 1) * 256)
        wide[:, cols] = (
            x_ref[:, cols].astype(F32)
            + mul(mixed_ref[0], wo_own[:, cols], NN)
            + mul(mixed_ref[1], wo_other[:, cols], NN)
            + out_bias[:, cols]
        )
    middle = wide[...]
    middle_ref[...] = middle.astype(BF)
    unit, _ = unit_of(middle)
    normed_two[...] = (unit * gain_ref[...] + shift_ref[...]).astype(BF)
    for half, (weight, bias) in enumerate(((wu_own, ub_own), (wu_other, ub_other))):
        for chunk in range(2):
            cols = slice(chunk * 256, (chunk + 1) * 256)
            hidden = mul(normed_two[...], weight[:, cols], NN) + bias[:, cols].astype(F32)
            square = hidden * hidden
            gate = jnp.tanh(GELU_A * (hidden + GELU_B * (square * hidden)))
            lift = 0.5 * (1.0 + gate)
            act[half, :, cols] = (hidden * lift).astype(BF)
            slope = lift + (0.5 * GELU_A) * hidden * (1.0 - gate * gate) * (
                1.0 + (3.0 * GELU_B) * square
            )
            slope_ref[half, :, cols] = slope.astype(BF)
    for chunk in range(4):
        cols = slice(chunk * 256, (chunk + 1) * 256)
        block_ref[:, cols] = (
            wide[:, cols]
            + mul(act[0], wd_own[:, cols], NN)
            + mul(act[1], wd_other[:, cols], NN)
            + down_bias[:, cols]
        )
    for half in range(2):
        acc[half] += mul(act[half], g_ref[...], TN)
    gsum_ref[...] += column_sum(g_ref[...].astype(F32))

    @pl.when(step == pl.num_programs(0) - 1)
    def _():
        gdown_ref[...] = acc[...].astype(BF)


def feed_back_kernel(
    job,
    places,
    g_ref,
    slope_ref,
    middle_ref,
    mixed_ref,
    inv_ref,
    wd_own,
    wd_other,
    wu_own,
    wu_other,
    wo_own,
    wo_other,
    gain_ref,
    shift_ref,
    *refs,
):
    tasks = []
    if job is not None:
        source, refs = refs[0], refs[1:]
    outs, refs = refs[:7], refs[7:]
    if job is not None:
        result, refs = refs[0], refs[1:]
    dmid_ref, dmix_ref, dot_ref, gup_ref, gout_ref, vec_ref, ubias_ref = outs
    acc_up, acc_out, normed_two, unit_ref, dhid, wide = refs[:6]
    if job is not None:
        tasks.append(Task(job, refs[6:], source, result, places))
    step = pl.program_id(0)

    @pl.when(step == 0)
    def _():
        if tasks:
            greet(reduction_partners())
        acc_up[...] = jnp.zeros_like(acc_up)
        acc_out[...] = jnp.zeros_like(acc_out)
        vec_ref[...] = jnp.zeros_like(vec_ref)
        ubias_ref[...] = jnp.zeros_like(ubias_ref)

    run_tasks(step, 0, tasks)
    for half, weight in enumerate((wd_own, wd_other)):
        for chunk in range(2):
            cols = slice(chunk * 256, (chunk + 1) * 256)
            down = mul(g_ref[...], weight[cols, :], NT)
            dhid[half, :, cols] = (down * slope_ref[half, :, cols].astype(F32)).astype(BF)
        ubias_ref[half] += column_sum(dhid[half].astype(F32))
    unit, inverse = unit_of(middle_ref[...].astype(F32))
    unit_ref[...] = unit
    normed_two[...] = (unit * gain_ref[...] + shift_ref[...]).astype(BF)
    for half in range(2):
        acc_up[half] += mul(dhid[half], normed_two[...], TN)
    for chunk in range(4):
        rows = slice(chunk * 256, (chunk + 1) * 256)
        wide[:, rows] = mul(dhid[0], wu_own[rows, :], NT) + mul(dhid[1], wu_other[rows, :], NT)
    run_tasks(step, 1, tasks)
    upstream = wide[...]
    unit = unit_ref[...]
    vec_ref[0] += column_sum(upstream * unit)
    vec_ref[1] += column_sum(upstream)
    dmid = g_ref[...].astype(F32) + norm_back(upstream, unit, inverse, gain_ref[...])
    vec_ref[2] += column_sum(dmid)
    dmid_ref[...] = dmid.astype(BF)
    lane = lax.broadcasted_iota(jnp.int32, (LAT, HEAD), 1)
    dots = jnp.zeros((LAT, HEAD), F32)
    for half, weight in enumerate((wo_own, wo_other)):
        acc_out[half] += mul(mixed_ref[half], dmid_ref[...], TN)
        for pair in range(2):
            both = mul(dmid_ref[...], weight[pair * 256 : (pair + 1) * 256, :], NT)
            for one in range(2):
                head = pair * 2 + one
                cols = slice(head * HEAD, (head + 1) * HEAD)
                place = half * 4 + head
                scaled = both[:, one * HEAD : (one + 1) * HEAD] * inv_ref[:, place : place + 1]
                dmix_ref[half, :, cols] = scaled.astype(BF)
                total = jnp.sum(
                    scaled * mixed_ref[half, :, cols].astype(F32), axis=-1, keepdims=True
                )
                dots = jnp.where(lane == place, total, dots)
    dot_ref[...] = dots

    @pl.when(step == pl.num_programs(0) - 1)
    def _():
        gup_ref[...] = acc_up[...].astype(BF)
        gout_ref[...] = acc_out[...].astype(BF)
        for task in tasks:
            task.finish()


def attend_back_kernel(
    jobs,
    places,
    normed_ref,
    own_ref,
    other_ref,
    probs_ref,
    dmix_ref,
    dot_ref,
    *refs,
):
    tasks, count = [], len(jobs)
    if jobs:
        sources, refs = refs[: count - 2], refs[count - 2 :]
    dheads_ref, gin_ref, vec_ref = refs[:3]
    refs = refs[3:]
    if jobs:
        results, refs = refs[: count - 1], refs[count - 1 :]
    acc, joined, dots_now = refs[:3]
    if jobs:
        staged, refs = refs[3], refs[4:]
        for n, job in enumerate(jobs):
            mine = refs[7 * n : 7 * n + 7]
            if n < count - 2:
                tasks.append(Task(job, mine, sources[n], results[n], places[n]))
            else:
                piece = n - (count - 2)
                tasks.append(Task(job, mine, staged, results[-1], places[n], True, piece))
    group, step = pl.program_id(0), pl.program_id(1)
    now = group * pl.num_programs(1) + step
    per_group = HALF // HEAD // GROUPS
    width = per_group * HEAD

    if tasks:

        @pl.when(now == 0)
        def _():
            greet(reduction_partners())

    @pl.when(step == 0)
    def _():
        acc[...] = jnp.zeros_like(acc)
        vec_ref[...] = jnp.zeros_like(vec_ref)

    @pl.when(group == 0)
    def _():
        for place in range(4):
            lane = (place // 2) * 4 + place % 2
            dots_now[:, place : place + 1] = dot_ref[:, lane : lane + 1]

    @pl.when(group == 1)
    def _():
        for place in range(4):
            lane = (place // 2) * 4 + 2 + place % 2
            dots_now[:, place : place + 1] = dot_ref[:, lane : lane + 1]

    run_tasks(now, 0, tasks)
    for half, heads_ref in enumerate((own_ref, other_ref)):
        for head in range(per_group):
            cols = slice(head * HEAD, (head + 1) * HEAD)
            place = half * per_group + head
            probs = probs_ref[half, head]
            upstream = dmix_ref[half, :, cols]
            d_probs = mul(upstream, heads_ref[2, :, cols], NT) - dots_now[:, place : place + 1]
            d_scores = (probs.astype(F32) * d_probs).astype(BF)
            d_query = (mul(d_scores, heads_ref[1, :, cols], NN) * SCALE).astype(BF)
            d_keys = (mul(heads_ref[0, :, cols], d_scores, TN) * SCALE).T.astype(BF)
            d_values = mul(probs, upstream, TN).astype(BF)
            for which, value in enumerate((d_query, d_keys, d_values)):
                dheads_ref[half, which, :, cols] = value
                first = half * 3 * width + which * width + head * HEAD
                joined[:, first : first + HEAD] = value
            if half == 1 and head == per_group - 1:
                run_tasks(now, 1, tasks)
    vec_ref[...] += column_sum(joined[...].astype(F32))
    for chunk in range(4):
        rows = slice(chunk * 256, (chunk + 1) * 256)
        acc[rows, :] += mul(normed_ref[:, rows], joined[...], TN)

    @pl.when((now if tasks else step) == pl.num_programs(1) * (GROUPS if tasks else 1) - 1)
    def _():
        for half in range(2):
            cols = slice(half * 3 * width, (half + 1) * 3 * width)
            gin_ref[half] = acc[:, cols].astype(BF)

    if tasks:

        @pl.when(now == pl.num_programs(1) - 1)
        def _():
            for piece in range(2):
                rows = slice(piece * D // 2, (piece + 1) * D // 2)
                tasks[piece - 2].refs[0][...] = acc[rows, : 3 * width].astype(BF)
            staged[...] = acc[:, 3 * width :].astype(BF)

    run_tasks(now, 2, tasks)

    if tasks:

        @pl.when(now == pl.num_programs(0) * pl.num_programs(1) - 1)
        def _():
            for task in tasks:
                task.finish()


def pack_vectors(vec_ref, two_ref, sum_ref, up_ref, in_ref, out_ref):
    total = lambda v: jnp.sum(v, axis=0, keepdims=True)
    width = HALF // GROUPS
    out_ref[...] = jnp.zeros_like(out_ref)
    out_ref[0:1, :] = total(vec_ref[0])
    out_ref[1:2, :] = total(vec_ref[1])
    out_ref[2:3, :] = total(two_ref[2])
    out_ref[3:4, :] = total(two_ref[0])
    out_ref[4:5, :] = total(two_ref[1])
    out_ref[5:6, :] = total(sum_ref[...])
    for half in range(2):
        for group in range(GROUPS):
            cols = slice(half * HALF + group * width, half * HALF + (group + 1) * width)
            for row, which in ((6, 0), (7, 2)):
                first = (half * 3 + which) * width
                out_ref[row : row + 1, cols] = total(in_ref[group, :, first : first + width])
        out_ref[8:9, half * HALF : (half + 1) * HALF] = total(up_ref[half])


def sum_vectors(held, landed, send_sem, recv_sem):
    groups = [[core_flip()]] + [[dp_flip(shift, n) for n in (1, 2, 3)] for shift in SHIFTS]
    for stage, partners in enumerate(groups):
        copies = [
            remote(
                held.at[stage],
                landed.at[stage, n],
                send_sem.at[stage, n],
                recv_sem.at[stage, n],
                partner,
            )
            for n, partner in enumerate(partners)
        ]
        start(copies)
        wait(copies)
        if stage == 0:
            got = landed[0, 0]
            crossed = jnp.concatenate([got[:, HALF:], got[:, :HALF]], axis=1)
            row = lax.broadcasted_iota(jnp.int32, got.shape, 0)
            held[1] = held[0] + jnp.where(row < 6, got, crossed)
        else:
            held[stage + 1] = (held[stage] + landed[stage, 0]) + (
                landed[stage, 1] + landed[stage, 2]
            )


def last_kernel(
    job,
    places,
    factor,
    x_ref,
    dheads_ref,
    dmid_ref,
    w_own,
    w_other,
    gain_ref,
    two_ref,
    sum_ref,
    up_ref,
    in_ref,
    *refs,
):
    tasks = []
    if job is not None:
        source, refs = refs[0], refs[1:]
    (grad_ref, total_ref), refs = refs[:2], refs[2:]
    if job is not None:
        result, refs = refs[0], refs[1:]
    (wide, vec_ref), refs = refs[:2], refs[2:]
    if job is not None:
        vectors, refs = refs[:4], refs[4:]
        for piece in range(2):
            mine = refs[7 * piece : 7 * piece + 7]
            tasks.append(Task(job, mine, source, result, places[piece], piece=piece))
    step = pl.program_id(0)
    last = pl.num_programs(0) - 1

    @pl.when(step == 0)
    def _():
        if tasks:
            greet(reduction_partners())
        vec_ref[...] = jnp.zeros_like(vec_ref)

    run_tasks(step, 0, tasks)
    for chunk in range(4):
        rows = slice(chunk * 256, (chunk + 1) * 256)
        total = None
        for half, weight in enumerate((w_own, w_other)):
            for which in range(3):
                term = mul(dheads_ref[half, which], weight[which, rows, :], NT)
                total = term if total is None else total + term
        wide[:, rows] = total
    run_tasks(step, 1, tasks)
    unit, inverse = unit_of(x_ref[...].astype(F32))
    upstream = wide[...]
    vec_ref[0] += column_sum(upstream * unit)
    vec_ref[1] += column_sum(upstream)
    grad = dmid_ref[...].astype(F32) + norm_back(upstream, unit, inverse, gain_ref[...])
    grad_ref[...] = grad.astype(BF)
    run_tasks(step, 2, tasks)

    @pl.when(step == last)
    def _():
        if tasks:
            pack_vectors(vec_ref, two_ref, sum_ref, up_ref, in_ref, vectors[0].at[0])
            sum_vectors(*vectors)
            total_ref[...] = vectors[0][1 + len(SHIFTS)] * factor
        else:
            pack_vectors(vec_ref, two_ref, sum_ref, up_ref, in_ref, total_ref)
        for task in tasks:
            task.finish()


def finish_kernel(factor, lat_ref, *refs):
    if len(refs) > 1:
        down_in, up_in, out_in, in_a, in_b, lat_out, down_out, up_out, out_out, in_out = refs
        width = HALF // GROUPS
        down_out[...] = down_in[...].astype(F32) * factor
        out_out[...] = out_in[...].astype(F32) * factor
        up_out[...] = up_in[...].astype(F32).T * factor
        for which in range(3):
            for group, part in enumerate((in_a, in_b)):
                in_out[which, :, group * width : (group + 1) * width] = (
                    part[:, which * width : (which + 1) * width].astype(F32) * factor
                )
    else:
        (lat_out,) = refs
    lat_out[...] = lat_ref[...].astype(F32)


def params(**more):
    return pltpu.CompilerParams(vmem_limit_bytes=VMEM_LIMIT, **more)


def per_device(
    latents,
    first_scale,
    first_shift,
    input_weights,
    input_bias,
    output_weight,
    output_bias,
    second_scale,
    second_shift,
    up_weight,
    up_bias,
    down_weight,
    down_bias,
    output_grad,
):
    rows = latents.shape[0]
    images = rows // LAT
    dp, mp = lax.axis_size("dp"), lax.axis_size("mp")
    direct = dp == 16 and mp == 2
    factor = LAT / (rows * dp * mp)
    row = lambda v: v[None, :]
    first_scale, first_shift = row(first_scale), row(first_shift)
    second_scale, second_shift = row(second_scale), row(second_shift)
    output_bias, down_bias = row(output_bias), row(down_bias)

    if direct:
        own = (input_weights, output_weight, up_weight, down_weight)
        small = jnp.concatenate(
            [input_bias, up_bias[None], jnp.zeros((13, HALF), BF)], axis=0
        )
    else:
        gather = lambda v, axis: lax.all_gather(v, "mp", axis=axis, tiled=True)
        w_in, w_out = gather(input_weights, 2), gather(output_weight, 0)
        w_up, w_down = gather(up_weight, 1), gather(down_weight, 0)
        small = jnp.concatenate([gather(input_bias, 1), gather(up_bias, 0)[None]], axis=0)
        own = (w_in[..., :HALF], w_out[:HALF], w_up[:, :HALF], w_down[:HALF])
        others = (w_in[..., HALF:], w_out[HALF:], w_up[:, HALF:], w_down[HALF:], small[:, HALF:])
        small = small[:, :HALF]

    w_shapes = [(3, D, HALF), (HALF, D), (D, HALF), (HALF, D), (16, HALF)]
    normed_shape = shape_of((rows, D), BF)
    heads_shape = shape_of((3, rows, HALF), BF)
    heads_spec = pl.BlockSpec((3, LAT, HALF), lambda i: (0, i, 0))
    vector = kept_spec((1, D))
    bias_spec = whole_spec(small.shape)
    outs = pl.pallas_call(
        functools.partial(first_kernel, direct),
        grid=(images,),
        name="project_own",
        in_specs=[row_spec(D), vector, vector, bias_spec, whole_spec((3, D, HALF))]
        + ([ANY] * 5 if direct else []),
        out_specs=[row_spec(D), heads_spec] + ([ANY] * 5 if direct else []),
        out_shape=[normed_shape, heads_shape]
        + ([shape_of(s, BF) for s in w_shapes] if direct else []),
        scratch_shapes=[pltpu.SemaphoreType.DMA((5,))] * 2 if direct else [],
        compiler_params=params(collective_id=0, has_side_effects=True) if direct else params(),
        cost_estimate=cost(6 * rows * D * HALF, 12 * rows * D),
    )(
        latents,
        first_scale,
        first_shift,
        small,
        own[0],
        *((own + (small,)) if direct else ()),
    )
    normed_one, heads_own = outs[:2]
    if direct:
        others = outs[2:]
    w_in_other, w_out_other, w_up_other, w_down_other, small_other = others
    w_in_own, w_out_own, w_up_own, w_down_own = own

    half_spec = pl.BlockSpec((2, LAT, HALF), lambda i: (0, i, 0))
    half_shape = shape_of((2, rows, HALF), BF)
    head_count = HALF // HEAD
    probs_shape = shape_of((2, head_count, rows, LAT), BF)
    probs_spec = pl.BlockSpec((2, head_count, LAT, LAT), lambda i: (0, 0, i, 0))
    square = (HALF, D)
    tall = (D, HALF)
    parts = ((0, 384), (384, 768), (768, 1024))
    job = Reduction(HALF, D, parts, ORDERS) if direct else None
    result = shape_of(square, BF)
    (
        block_output,
        heads_other,
        probs,
        inverses,
        mixed,
        middle,
        slope,
        g_down,
        g_sum,
    ) = pl.pallas_call(
        forward_kernel,
        grid=(images,),
        name="forward",
        in_specs=[
            row_spec(D),
            row_spec(D),
            heads_spec,
            row_spec(D),
            whole_spec((3, D, HALF)),
            whole_spec(small_other.shape),
            whole_spec(square),
            whole_spec(square),
            vector,
            vector,
            vector,
            whole_spec(tall),
            whole_spec(tall),
            kept_spec((1, HALF)),
            kept_spec((1, HALF)),
            whole_spec(square),
            whole_spec(square),
            vector,
        ],
        out_specs=[
            row_spec(D),
            heads_spec,
            probs_spec,
            row_spec(HEAD),
            half_spec,
            row_spec(D),
            half_spec,
            kept_spec((2, HALF, D)),
            kept_spec((8, D)),
        ],
        out_shape=[
            shape_of((rows, D), F32),
            heads_shape,
            probs_shape,
            shape_of((rows, HEAD), F32),
            half_shape,
            shape_of((rows, D), BF),
            half_shape,
            shape_of((2, HALF, D), BF),
            shape_of((8, D), F32),
        ],
        scratch_shapes=[
            pltpu.VMEM((2, HALF, D), F32),
            pltpu.VMEM((LAT, D), BF),
            pltpu.VMEM((2, LAT, HALF), BF),
            pltpu.VMEM((LAT, D), F32),
        ],
        compiler_params=params(),
        cost_estimate=cost(16 * rows * D * D, 24 * rows * D),
    )(
        latents,
        normed_one,
        heads_own,
        output_grad,
        w_in_other,
        small_other,
        w_out_own,
        w_out_other,
        output_bias,
        second_scale,
        second_shift,
        w_up_own,
        w_up_other,
        small[2:3],
        small_other[2:3],
        w_down_own,
        w_down_other,
        down_bias,
    )

    d_middle, d_mixed, d_dots, g_up, g_out, vec_two, vec_up, *sums = pl.pallas_call(
        functools.partial(feed_back_kernel, job, FEED_PLACES),
        grid=(images,),
        name="feed_back",
        in_specs=[
            row_spec(D),
            half_spec,
            row_spec(D),
            half_spec,
            row_spec(HEAD),
            whole_spec(square),
            whole_spec(square),
            whole_spec(tall),
            whole_spec(tall),
            whole_spec(square),
            whole_spec(square),
            vector,
            vector,
        ]
        + ([ANY] if direct else []),
        out_specs=[
            row_spec(D),
            half_spec,
            row_spec(HEAD),
            kept_spec((2, HALF, D)),
            kept_spec((2, HALF, D)),
            kept_spec((3, 8, D)),
            kept_spec((2, 8, HALF)),
        ]
        + ([ANY] if direct else []),
        out_shape=[
            shape_of((rows, D), BF),
            half_shape,
            shape_of((rows, HEAD), F32),
            shape_of((2, HALF, D), BF),
            shape_of((2, HALF, D), BF),
            shape_of((3, 8, D), F32),
            shape_of((2, 8, HALF), F32),
        ]
        + ([result] if direct else []),
        scratch_shapes=[
            pltpu.VMEM((2, HALF, D), F32),
            pltpu.VMEM((2, HALF, D), F32),
            pltpu.VMEM((LAT, D), BF),
            pltpu.VMEM((LAT, D), F32),
            pltpu.VMEM((2, LAT, HALF), BF),
            pltpu.VMEM((LAT, D), F32),
        ]
        + (job.scratch() if direct else []),
        compiler_params=params(collective_id=1, has_side_effects=True) if direct else params(),
        cost_estimate=cost(10 * rows * D * D, 14 * rows * D),
    )(
        output_grad,
        slope,
        middle,
        mixed,
        inverses,
        w_down_own,
        w_down_other,
        w_up_own,
        w_up_other,
        w_out_own,
        w_out_other,
        second_scale,
        second_shift,
        *((g_down,) if direct else ()),
    )

    per_group = head_count // GROUPS
    width = per_group * HEAD
    group_heads = pl.BlockSpec((3, LAT, width), lambda g, i: (0, i, g))
    group_job = Reduction(
        D // 2, 3 * width, tuple((n * width, (n + 1) * width) for n in range(3)), ORDERS
    )
    group_result = shape_of((D, 3 * width), BF)
    jobs = [job, job, group_job, group_job] if direct else []
    d_heads, g_in, vec_in, *more = pl.pallas_call(
        functools.partial(attend_back_kernel, jobs, ATTEND_PLACES),
        grid=(GROUPS, images),
        name="attend_back",
        in_specs=[
            pl.BlockSpec((LAT, D), lambda g, i: (i, 0)),
            group_heads,
            group_heads,
            pl.BlockSpec((2, per_group, LAT, LAT), lambda g, i: (0, g, i, 0)),
            pl.BlockSpec((2, LAT, width), lambda g, i: (0, i, g)),
            pl.BlockSpec((LAT, HEAD), lambda g, i: (i, 0)),
        ]
        + ([ANY] * 2 if direct else []),
        out_specs=[
            pl.BlockSpec((2, 3, LAT, width), lambda g, i: (0, 0, i, g)),
            pl.BlockSpec(
                (None, 2, D, 3 * width), lambda g, i: (0 if direct else g, 0, 0, 0)
            ),
            pl.BlockSpec((None, 8, 6 * width), lambda g, i: (g, 0, 0)),
        ]
        + [ANY] * (3 if direct else 0),
        out_shape=[
            shape_of((2, 3, rows, HALF), BF),
            shape_of((1 if direct else GROUPS, 2, D, 3 * width), BF),
            shape_of((GROUPS, 8, 6 * width), F32),
        ]
        + ([result, result, group_result] if direct else []),
        scratch_shapes=[
            pltpu.VMEM((D, 6 * width), F32),
            pltpu.VMEM((LAT, 6 * width), BF),
            pltpu.VMEM((LAT, HEAD), F32),
        ]
        + ([pltpu.VMEM((D, 3 * width), BF)] if direct else [])
        + sum([one.scratch() for one in jobs], []),
        compiler_params=params(collective_id=2, has_side_effects=True) if direct else params(),
        cost_estimate=cost(8 * rows * D * D, 20 * rows * D),
    )(
        normed_one,
        heads_own,
        heads_other,
        probs,
        d_mixed,
        d_dots,
        *((g_up, g_out) if direct else ()),
    )

    stages = 1 + len(SHIFTS)
    grad_low, vectors, *last = pl.pallas_call(
        functools.partial(
            last_kernel, group_job if direct else None, LAST_PLACES, factor
        ),
        grid=(images,),
        name="input_back",
        in_specs=[
            row_spec(D),
            pl.BlockSpec((2, 3, LAT, HALF), lambda i: (0, 0, i, 0)),
            row_spec(D),
            whole_spec((3, D, HALF)),
            whole_spec((3, D, HALF)),
            vector,
            kept_spec((3, 8, D)),
            kept_spec((8, D)),
            kept_spec((2, 8, HALF)),
            kept_spec((GROUPS, 8, 6 * width)),
        ]
        + ([ANY] if direct else []),
        out_specs=[row_spec(D), kept_spec((16, D))] + ([ANY] if direct else []),
        out_shape=[shape_of((rows, D), BF), shape_of((16, D), F32)]
        + ([group_result] if direct else []),
        scratch_shapes=[pltpu.VMEM((LAT, D), F32), pltpu.VMEM((2, 8, D), F32)]
        + (
            [
                pltpu.VMEM((stages + 1, 16, D), F32),
                pltpu.VMEM((stages, 3, 16, D), F32),
                pltpu.SemaphoreType.DMA((stages, 3)),
                pltpu.SemaphoreType.DMA((stages, 3)),
            ]
            + group_job.scratch() * 2
            if direct
            else []
        ),
        compiler_params=params(collective_id=3, has_side_effects=True) if direct else params(),
        cost_estimate=cost(6 * rows * D * D, 14 * rows * D),
    )(
        latents,
        d_heads,
        d_middle,
        w_in_own,
        w_in_other,
        first_scale,
        vec_two,
        g_sum,
        vec_up,
        vec_in,
        *((g_in.reshape(2, D, 3 * width),) if direct else ()),
    )

    pieces = 8
    cut = rows // pieces
    if direct:
        latents_grad, g_down, g_up, g_out, g_in = pl.pallas_call(
            functools.partial(finish_kernel, factor),
            grid=(pieces,),
            name="finish",
            in_specs=[
                pl.BlockSpec((cut, D), lambda i: (i, 0)),
                pl.BlockSpec((HALF // pieces, D), lambda i: (i, 0)),
                pl.BlockSpec((HALF, D // pieces), lambda i: (0, i)),
                pl.BlockSpec((HALF // pieces, D), lambda i: (i, 0)),
                pl.BlockSpec((D // pieces, 3 * width), lambda i: (i, 0)),
                pl.BlockSpec((D // pieces, 3 * width), lambda i: (i, 0)),
            ],
            out_specs=[
                pl.BlockSpec((cut, D), lambda i: (i, 0)),
                pl.BlockSpec((HALF // pieces, D), lambda i: (i, 0)),
                pl.BlockSpec((D // pieces, HALF), lambda i: (i, 0)),
                pl.BlockSpec((HALF // pieces, D), lambda i: (i, 0)),
                pl.BlockSpec((3, D // pieces, HALF), lambda i: (0, i, 0)),
            ],
            out_shape=[
                shape_of((rows, D), F32),
                shape_of((HALF, D), F32),
                shape_of((D, HALF), F32),
                shape_of((HALF, D), F32),
                shape_of((3, D, HALF), F32),
            ],
            compiler_params=params(),
        )(grad_low, sums[0], more[0], more[1], more[2], last[0])
        mine = vectors[6:9, :HALF]
    else:
        latents_grad = pl.pallas_call(
            functools.partial(finish_kernel, factor),
            grid=(pieces,),
            name="finish",
            in_specs=[pl.BlockSpec((cut, D), lambda i: (i, 0))],
            out_specs=pl.BlockSpec((cut, D), lambda i: (i, 0)),
            out_shape=shape_of((rows, D), F32),
            compiler_params=params(),
        )(grad_low)
        vectors = lax.psum(vectors, ("dp", "mp")) * factor
        own_width = D // mp
        mine = lax.dynamic_slice_in_dim(
            vectors[6:9], lax.axis_index("mp") * own_width, own_width, 1
        )
        g_down, g_up, g_out = (v.reshape(D, D) for v in (g_down, g_up, g_out))
        g_in = jnp.transpose(g_in.reshape(GROUPS, 2, D, 3, width), (3, 2, 1, 0, 4))
        g_in = g_in.reshape(3, D, D)

        def scatter(v, axis):
            v = lax.psum_scatter(v, "mp", scatter_dimension=axis, tiled=True)
            return lax.psum(v, "dp").astype(F32) * factor

        g_down, g_up, g_out = scatter(g_down, 0), scatter(g_up.T, 1), scatter(g_out, 0)
        g_in = scatter(g_in, 2)

    return (
        block_output,
        latents_grad,
        vectors[0],
        vectors[1],
        g_in,
        mine[:2],
        g_out,
        vectors[2],
        vectors[3],
        vectors[4],
        g_up,
        mine[2],
        g_down,
        vectors[5],
    )


def solution(mesh):
    return jax.shard_map(
        per_device,
        mesh=mesh,
        in_specs=(
            P(("dp", "mp"), None),
            P(),
            P(),
            P(None, None, "mp"),
            P(None, "mp"),
            P("mp", None),
            P(),
            P(),
            P(),
            P(None, "mp"),
            P("mp"),
            P("mp", None),
            P(),
            P(("dp", "mp"), None),
        ),
        out_specs=(
            P(("dp", "mp"), None),
            P(("dp", "mp"), None),
            P(),
            P(),
            P(None, None, "mp"),
            P(None, "mp"),
            P("mp", None),
            P(),
            P(),
            P(),
            P(None, "mp"),
            P("mp"),
            P("mp", None),
            P(),
        ),
        check_vma=False,
    )
```

```python
import functools

import jax
import jax.numpy as jnp
from jax import lax
from jax.experimental import pallas as pl
from jax.experimental.pallas import tpu as pltpu
from jax.sharding import PartitionSpec as P

D = 1024
HEAD = 128
HEADS = 8
LAT = 512
HALF = 512
GROUPS = 2
EPS = 1e-05
SCALE = HEAD ** (-0.5)
LOG2E = 1.4426950408889634
GELU_A = 0.7978845608028654
GELU_B = 0.044715
MESH = pl.DeviceIdType.MESH
NN = (((1,), (0,)), ((), ()))
NT = (((1,), (1,)), ((), ()))
TN = (((0,), (0,)), ((), ()))
BF = jnp.bfloat16
F32 = jnp.float32
VMEM_LIMIT = 60 << 20


def mul(a, b, dims):
    return lax.dot_general(a, b, dims, preferred_element_type=F32)


def unit_of(rows):
    centred = rows - jnp.mean(rows, axis=-1, keepdims=True)
    inverse = lax.rsqrt(jnp.mean(centred * centred, axis=-1, keepdims=True) + EPS)
    return centred * inverse, inverse


def norm_back(upstream, unit, inverse, gain):
    scaled = upstream * gain
    inner = (
        scaled
        - jnp.mean(scaled, axis=-1, keepdims=True)
        - unit * jnp.mean(scaled * unit, axis=-1, keepdims=True)
    )
    return inverse * inner


def column_sum(values):
    return jnp.sum(values.reshape(values.shape[0] // 8, 8, values.shape[1]), axis=0)


def row_spec(width):
    return pl.BlockSpec((LAT, width), lambda i: (i, 0))


def whole_spec(shape):
    return pl.BlockSpec(shape, lambda *_: (0,) * len(shape), pipeline_mode=pl.Buffered(1))


def kept_spec(shape):
    return pl.BlockSpec(shape, lambda *_: (0,) * len(shape))


ANY = pl.BlockSpec(memory_space=pl.ANY)


def shape_of(shape, dtype):
    return jax.ShapeDtypeStruct(shape, dtype)


def cost(flops, moved):
    return pl.CostEstimate(flops=int(flops), bytes_accessed=int(moved), transcendentals=0)


def flipped(place, other):
    for bit in (1, 2):
        if other & bit:
            place = place + bit - 2 * bit * lax.rem(place // bit, 2)
    return place


def dp_flip(shift, other):
    me = lax.axis_index("dp")
    place = lax.rem(me // (1 << shift), 4)
    return (me + (flipped(place, other) - place) * (1 << shift), lax.axis_index("mp"))


def start(copies):
    for copy in copies:
        copy.start()


def wait(copies):
    for copy in copies:
        copy.wait()


def core_flip():
    return (lax.axis_index("dp"), 1 - lax.axis_index("mp"))


def greet(partners):
    barrier = pltpu.get_barrier_semaphore()
    for partner in partners:
        pl.semaphore_signal(barrier, inc=1, device_id=partner, device_id_type=MESH)
    pl.semaphore_wait(barrier, len(partners))


def remote(src, dst, send, recv, partner):
    return pltpu.make_async_remote_copy(
        src_ref=src,
        dst_ref=dst,
        send_sem=send,
        recv_sem=recv,
        device_id=partner,
        device_id_type=MESH,
    )


class Reduction:
    def __init__(self, rows, columns, parts, orders):
        self.rows, self.columns, self.parts, self.orders = rows, columns, parts, orders
        self.stages = len(orders[0])
        self.ticks = 2 * self.stages + 2

    def scratch(self):
        copies = (len(self.parts), 2 * self.stages, 3)
        return [
            pltpu.VMEM((self.rows, self.columns), BF),
            pltpu.VMEM((self.rows, self.columns), BF),
            pltpu.VMEM((self.rows, self.columns), BF),
            pltpu.SemaphoreType.DMA((2,)),
            pltpu.SemaphoreType.DMA(copies),
            pltpu.SemaphoreType.DMA(copies),
            pltpu.SemaphoreType.DMA((2,)),
        ]

    def place(self, part, stage):
        shift, members = self.orders[part][stage]
        return lax.rem(lax.axis_index("dp") // (1 << shift), members)

    def size(self, stage):
        rows = self.rows
        for _, members in self.orders[0][: stage + 1]:
            rows //= members
        return rows

    def others(self, stage):
        return (1,) if self.orders[0][stage][1] == 2 else (3, 1, 2)

    def offset(self, part, level):
        row = 0
        for stage in range(level):
            row = row + self.place(part, stage) * self.size(stage)
        return row

    def aligned(self, row, size):
        return pl.ds(pl.multiple_of(row, size), size)

    def columns_of(self, part):
        first, last = self.parts[part]
        return pl.ds(first, last - first)

    def partner(self, part, stage, other):
        return dp_flip(self.orders[part][stage][0], other)

    def landing(self, stage, other):
        size = self.size(stage)
        first = self.rows - self.orders[0][stage][1] * size
        return pl.ds(first + (other - 1) * size, size)

    def adding(self, refs, part, stage):
        cur, _, recv, _, send_sem, recv_sem = refs[:6]
        size = self.size(stage)
        base, cols = self.offset(part, stage), self.columns_of(part)
        copies = []
        for other in self.others(stage):
            theirs = flipped(self.place(part, stage), other)
            copies.append(
                remote(
                    cur.at[self.aligned(base + theirs * size, size), cols],
                    recv.at[self.landing(stage, other), cols],
                    send_sem.at[part, stage, other - 1],
                    recv_sem.at[part, stage, other - 1],
                    self.partner(part, stage, other),
                )
            )
        return copies

    def handing(self, refs, part, step):
        _, full, _, _, send_sem, recv_sem = refs[:6]
        stage = self.stages - 1 - step
        size = self.size(stage)
        rows, cols = self.aligned(self.offset(part, stage + 1), size), self.columns_of(part)
        return [
            remote(
                full.at[rows, cols],
                full.at[rows, cols],
                send_sem.at[part, self.stages + step, other - 1],
                recv_sem.at[part, self.stages + step, other - 1],
                self.partner(part, stage, other),
            )
            for other in self.others(stage)
        ]

    def exchange(self, refs, other):
        return remote(other, refs[1], refs[3].at[0], refs[3].at[1], core_flip())

    def tick(self, refs, tick, other):
        cur, landed, recv = refs[:3]
        parts = range(len(self.parts))
        if tick == 0:
            self.exchange(refs, other).start()
            return
        if tick == 1:
            self.exchange(refs, other).wait()
            cur[...] = (cur[...].astype(F32) + landed[...].astype(F32)).astype(BF)
            for part in parts:
                start(self.adding(refs, part, 0))
            return
        if tick <= self.stages + 1:
            stage = tick - 2
            for part in parts:
                wait(self.adding(refs, part, stage))
                size = self.size(stage)
                keep, cols = self.aligned(self.offset(part, stage + 1), size), self.columns_of(part)
                total = cur[keep, cols].astype(F32)
                for other in sorted(self.others(stage)):
                    total = total + recv[self.landing(stage, other), cols].astype(F32)
                if stage + 1 < self.stages:
                    cur[keep, cols] = total.astype(BF)
                    start(self.adding(refs, part, stage + 1))
                else:
                    landed[keep, cols] = total.astype(BF)
                    start(self.handing(refs, part, 0))
            return
        step = tick - self.stages - 2
        for part in parts:
            wait(self.handing(refs, part, step))
            if step + 1 < self.stages:
                start(self.handing(refs, part, step + 1))


class Task:
    def __init__(self, job, refs, source, result, places, staged=False, piece=0):
        self.job, self.refs, self.places, self.staged = job, refs, places, staged
        window = pl.ds(piece * job.rows, job.rows)
        self.own = None if staged else source.at[0, window]
        self.other = source.at[window] if staged else source.at[1, window]
        self.result = result.at[window]

    def load(self):
        return pltpu.make_async_copy(self.own, self.refs[0], self.refs[6].at[0])

    def store(self):
        return pltpu.make_async_copy(self.refs[1], self.result, self.refs[6].at[1])

    def run(self, tick):
        if tick == 0 and not self.staged:
            self.load().start()
        if tick == 1 and not self.staged:
            self.load().wait()
        self.job.tick(self.refs, tick, self.other)
        if tick == self.job.ticks - 1:
            self.store().start()

    def finish(self):
        self.store().wait()


def run_tasks(step, place, tasks):
    for now in sorted({at[0] for task in tasks for at in task.places if at[1] == place}):

        @pl.when(step == now)
        def _():
            for task in tasks:
                for tick, at in enumerate(task.places):
                    if at == (now, place):
                        task.run(tick)


ORDERS = (((0, 2), (1, 2), (2, 4)), ((1, 2), (0, 2), (2, 4)), ((2, 2), (3, 2), (0, 4)))
SHIFTS = (0, 2)


def starts(steps, *numbers):
    return tuple((n, 0) if n < steps else (steps - 1, 1) for n in numbers)


FEED_PLACES = starts(8, 0, 1, 2, 3, 4, 5, 6, 7)
ATTEND_PLACES = (
    starts(16, 0, 1, 2, 3, 5, 7, 8, 12),
    starts(16, 1, 2, 4, 6, 8, 10, 12, 14),
    ((7, 1),) + starts(16, 9, 10, 11, 12, 13, 14, 16),
    ((7, 1),) + starts(16, 10, 11, 12, 13, 14, 15, 16),
)
LAST_PLACES = (
    starts(8, 0, 1, 2, 3, 4, 5, 6, 7),
    starts(8, 0, 1, 2, 3, 4, 6, 7, 8),
)
VECTOR_PLACES = starts(8, 1, 2, 4, 6)


def reduction_partners():
    return [core_flip()] + [dp_flip(shift, other) for shift in SHIFTS for other in (1, 2, 3)]


def first_kernel(
    spread, x_ref, gain_ref, shift_ref, bias_ref, w_in, *refs
):
    step = pl.program_id(0)
    if spread:
        sources = (w_in_any, w_out, w_up, w_down, bias_all) = refs[:5]
        normed_ref, heads_ref = refs[5:7]
        targets = refs[7:12]
        send_sem, recv_sem = refs[12:14]

        def copies():
            return [
                remote(src, dst, send_sem.at[n], recv_sem.at[n], core_flip())
                for n, (src, dst) in enumerate(zip(sources, targets))
            ]

        @pl.when(step == 0)
        def _():
            greet([core_flip()])
            for copy in copies():
                copy.start()
    else:
        normed_ref, heads_ref = refs

    for piece in range(2):
        rows = slice(piece * 256, (piece + 1) * 256)
        unit, _ = unit_of(x_ref[rows, :].astype(F32))
        normed_ref[rows, :] = (unit * gain_ref[...] + shift_ref[...]).astype(BF)
        project(normed_ref, w_in, bias_ref, heads_ref, rows)

    if spread:

        @pl.when(step == pl.num_programs(0) - 1)
        def _():
            for copy in copies():
                copy.wait()


def project(normed_ref, weights, bias_ref, heads_ref, rows=slice(0, LAT)):
    for which in range(3):
        heads = mul(normed_ref[rows, :], weights[which], NN)
        if which != 1:
            place = 0 if which == 0 else 1
            heads = heads + bias_ref[place : place + 1, :].astype(F32)
        heads_ref[which, rows, :] = heads.astype(BF)


def forward_kernel(
    x_ref,
    normed_ref,
    own_ref,
    g_ref,
    w_in,
    in_bias,
    wo_own,
    wo_other,
    out_bias,
    gain_ref,
    shift_ref,
    wu_own,
    wu_other,
    ub_own,
    ub_other,
    wd_own,
    wd_other,
    down_bias,
    block_ref,
    other_ref,
    probs_ref,
    inv_ref,
    mixed_ref,
    middle_ref,
    slope_ref,
    gdown_ref,
    gsum_ref,
    acc,
    normed_two,
    act,
    wide,
):
    step = pl.program_id(0)

    @pl.when(step == 0)
    def _():
        acc[...] = jnp.zeros_like(acc)
        gsum_ref[...] = jnp.zeros_like(gsum_ref)

    project(normed_ref, w_in, in_bias, other_ref)
    lane = lax.broadcasted_iota(jnp.int32, (LAT, HEAD), 1)
    inverses = jnp.zeros((LAT, HEAD), F32)
    for half, heads_ref in enumerate((own_ref, other_ref)):
        for head in range(HALF // HEAD):
            cols = slice(head * HEAD, (head + 1) * HEAD)
            scores = mul(heads_ref[0, :, cols], heads_ref[1, :, cols], NT)
            highest = jnp.max(scores, axis=-1, keepdims=True)
            powers = jnp.exp2((scores - highest) * (SCALE * LOG2E))
            inverse = 1.0 / jnp.sum(powers, axis=-1, keepdims=True)
            low = powers.astype(BF)
            probs_ref[half, head] = low
            mixed = mul(low, heads_ref[2, :, cols], NN) * inverse
            mixed_ref[half, :, cols] = mixed.astype(BF)
            inverses = jnp.where(lane == half * 4 + head, inverse, inverses)
    inv_ref[...] = inverses
    for piece in range(2):
        rows = slice(piece * 256, (piece + 1) * 256)
        for chunk in range(4):
            cols = slice(chunk * 256, (chunk + 1) * 256)
            wide[rows, cols] = (
                x_ref[rows, cols].astype(F32)
                + mul(mixed_ref[0, rows], wo_own[:, cols], NN)
                + mul(mixed_ref[1, rows], wo_other[:, cols], NN)
                + out_bias[:, cols]
            )
        middle = wide[rows, :]
        middle_ref[rows, :] = middle.astype(BF)
        unit, _ = unit_of(middle)
        normed_two[rows, :] = (unit * gain_ref[...] + shift_ref[...]).astype(BF)
        for half, (weight, bias) in enumerate(((wu_own, ub_own), (wu_other, ub_other))):
            for chunk in range(2):
                cols = slice(chunk * 256, (chunk + 1) * 256)
                hidden = mul(normed_two[rows, :], weight[:, cols], NN) + bias[:, cols].astype(F32)
                square = hidden * hidden
                gate = jnp.tanh(GELU_A * (hidden + GELU_B * (square * hidden)))
                lift = 0.5 * (1.0 + gate)
                act[half, rows, cols] = (hidden * lift).astype(BF)
                slope = lift + (0.5 * GELU_A) * hidden * (1.0 - gate * gate) * (
                    1.0 + (3.0 * GELU_B) * square
                )
                slope_ref[half, rows, cols] = slope.astype(BF)
        for chunk in range(4):
            cols = slice(chunk * 256, (chunk + 1) * 256)
            block_ref[rows, cols] = (
                wide[rows, cols]
                + mul(act[0, rows], wd_own[:, cols], NN)
                + mul(act[1, rows], wd_other[:, cols], NN)
                + down_bias[:, cols]
            )
    for half in range(2):
        acc[half] += mul(act[half], g_ref[...], TN)
    gsum_ref[...] += column_sum(g_ref[...].astype(F32))

    @pl.when(step == pl.num_programs(0) - 1)
    def _():
        gdown_ref[...] = acc[...].astype(BF)


def feed_back_kernel(
    job,
    places,
    g_ref,
    slope_ref,
    middle_ref,
    mixed_ref,
    inv_ref,
    wd_own,
    wd_other,
    wu_own,
    wu_other,
    wo_own,
    wo_other,
    gain_ref,
    shift_ref,
    *refs,
):
    tasks = []
    if job is not None:
        source, refs = refs[0], refs[1:]
    outs, refs = refs[:7], refs[7:]
    if job is not None:
        result, refs = refs[0], refs[1:]
    dmid_ref, dmix_ref, dot_ref, gup_ref, gout_ref, vec_ref, ubias_ref = outs
    acc_up, acc_out, normed_two, unit_ref, dhid, wide = refs[:6]
    if job is not None:
        tasks.append(Task(job, refs[6:], source, result, places))
    step = pl.program_id(0)

    @pl.when(step == 0)
    def _():
        if tasks:
            greet(reduction_partners())
        acc_up[...] = jnp.zeros_like(acc_up)
        acc_out[...] = jnp.zeros_like(acc_out)
        vec_ref[...] = jnp.zeros_like(vec_ref)
        ubias_ref[...] = jnp.zeros_like(ubias_ref)

    run_tasks(step, 0, tasks)
    lane = lax.broadcasted_iota(jnp.int32, (256, HEAD), 1)
    for piece in range(2):
        rows = slice(piece * 256, (piece + 1) * 256)
        for half, weight in enumerate((wd_own, wd_other)):
            for chunk in range(2):
                cols = slice(chunk * 256, (chunk + 1) * 256)
                down = mul(g_ref[rows, :], weight[cols, :], NT)
                dhid[half, rows, cols] = (down * slope_ref[half, rows, cols].astype(F32)).astype(BF)
            ubias_ref[half] += column_sum(dhid[half, rows].astype(F32))
        unit, inverse = unit_of(middle_ref[rows, :].astype(F32))
        unit_ref[rows, :] = unit
        normed_two[rows, :] = (unit * gain_ref[...] + shift_ref[...]).astype(BF)
        for chunk in range(4):
            cols = slice(chunk * 256, (chunk + 1) * 256)
            wide[rows, cols] = mul(dhid[0, rows], wu_own[cols, :], NT) + mul(
                dhid[1, rows], wu_other[cols, :], NT
            )
        upstream = wide[rows, :]
        unit = unit_ref[rows, :]
        vec_ref[0] += column_sum(upstream * unit)
        vec_ref[1] += column_sum(upstream)
        dmid = g_ref[rows, :].astype(F32) + norm_back(upstream, unit, inverse, gain_ref[...])
        vec_ref[2] += column_sum(dmid)
        dmid_ref[rows, :] = dmid.astype(BF)
    for half in range(2):
        acc_up[half] += mul(dhid[half], normed_two[...], TN)
    for half in range(2):
        acc_out[half] += mul(mixed_ref[half], dmid_ref[...], TN)
    for piece in range(2):
        rows = slice(piece * 256, (piece + 1) * 256)
        dots = jnp.zeros((256, HEAD), F32)
        for half, weight in enumerate((wo_own, wo_other)):
            for pair in range(2):
                both = mul(dmid_ref[rows, :], weight[pair * 256 : (pair + 1) * 256, :], NT)
                for one in range(2):
                    head = pair * 2 + one
                    cols = slice(head * HEAD, (head + 1) * HEAD)
                    place = half * 4 + head
                    scaled = both[:, one * HEAD : (one + 1) * HEAD] * inv_ref[rows, place : place + 1]
                    dmix_ref[half, rows, cols] = scaled.astype(BF)
                    total = jnp.sum(
                        scaled * mixed_ref[half, rows, cols].astype(F32), axis=-1, keepdims=True
                    )
                    dots = jnp.where(lane == place, total, dots)
        dot_ref[rows, :] = dots

    @pl.when(step == pl.num_programs(0) - 1)
    def _():
        gup_ref[...] = acc_up[...].astype(BF)
        gout_ref[...] = acc_out[...].astype(BF)
        for task in tasks:
            task.finish()


def attend_back_kernel(
    jobs,
    places,
    normed_ref,
    own_ref,
    other_ref,
    probs_ref,
    dmix_ref,
    dot_ref,
    *refs,
):
    tasks, count = [], len(jobs)
    if jobs:
        sources, refs = refs[: count - 2], refs[count - 2 :]
    dheads_ref, gin_ref, vec_ref = refs[:3]
    refs = refs[3:]
    if jobs:
        results, refs = refs[: count - 1], refs[count - 1 :]
    acc, joined, dots_now = refs[:3]
    if jobs:
        staged, refs = refs[3], refs[4:]
        for n, job in enumerate(jobs):
            mine = refs[7 * n : 7 * n + 7]
            if n < count - 2:
                tasks.append(Task(job, mine, sources[n], results[n], places[n]))
            else:
                piece = n - (count - 2)
                tasks.append(Task(job, mine, staged, results[-1], places[n], True, piece))
    group, step = pl.program_id(0), pl.program_id(1)
    now = group * pl.num_programs(1) + step
    per_group = HALF // HEAD // GROUPS
    width = per_group * HEAD

    if tasks:

        @pl.when(now == 0)
        def _():
            greet(reduction_partners())

    @pl.when(step == 0)
    def _():
        acc[...] = jnp.zeros_like(acc)
        vec_ref[...] = jnp.zeros_like(vec_ref)

    @pl.when(group == 0)
    def _():
        for place in range(4):
            lane = (place // 2) * 4 + place % 2
            dots_now[:, place : place + 1] = dot_ref[:, lane : lane + 1]

    @pl.when(group == 1)
    def _():
        for place in range(4):
            lane = (place // 2) * 4 + 2 + place % 2
            dots_now[:, place : place + 1] = dot_ref[:, lane : lane + 1]

    run_tasks(now, 0, tasks)
    for half, heads_ref in enumerate((own_ref, other_ref)):
        for head in range(per_group):
            cols = slice(head * HEAD, (head + 1) * HEAD)
            place = half * per_group + head
            probs = probs_ref[half, head]
            upstream = dmix_ref[half, :, cols]
            d_probs = mul(upstream, heads_ref[2, :, cols], NT) - dots_now[:, place : place + 1]
            d_scores = (probs.astype(F32) * d_probs).astype(BF)
            d_query = (mul(d_scores, heads_ref[1, :, cols], NN) * SCALE).astype(BF)
            d_keys = (mul(heads_ref[0, :, cols], d_scores, TN) * SCALE).T.astype(BF)
            d_values = mul(probs, upstream, TN).astype(BF)
            for which, value in enumerate((d_query, d_keys, d_values)):
                dheads_ref[half, which, :, cols] = value
                first = half * 3 * width + which * width + head * HEAD
                joined[:, first : first + HEAD] = value
    vec_ref[...] += column_sum(joined[...].astype(F32))
    for chunk in range(4):
        rows = slice(chunk * 256, (chunk + 1) * 256)
        acc[rows, :] += mul(normed_ref[:, rows], joined[...], TN)

    @pl.when((now if tasks else step) == pl.num_programs(1) * (GROUPS if tasks else 1) - 1)
    def _():
        for half in range(2):
            cols = slice(half * 3 * width, (half + 1) * 3 * width)
            gin_ref[half] = acc[:, cols].astype(BF)

    if tasks:

        @pl.when(now == pl.num_programs(1) - 1)
        def _():
            for piece in range(2):
                rows = slice(piece * D // 2, (piece + 1) * D // 2)
                tasks[piece - 2].refs[0][...] = acc[rows, : 3 * width].astype(BF)
            staged[...] = acc[:, 3 * width :].astype(BF)

    run_tasks(now, 1, tasks)

    if tasks:

        @pl.when(now == pl.num_programs(0) * pl.num_programs(1) - 1)
        def _():
            for task in tasks:
                task.finish()


def total_row(v):
    return jnp.sum(v, axis=0, keepdims=True)


def pack_vectors(two_ref, sum_ref, up_ref, in_ref, out_ref):
    width = HALF // GROUPS
    out_ref[...] = jnp.zeros_like(out_ref)
    out_ref[0:1, :] = total_row(two_ref[2])
    out_ref[1:2, :] = total_row(two_ref[0])
    out_ref[2:3, :] = total_row(two_ref[1])
    out_ref[3:4, :] = total_row(sum_ref[...])
    for half in range(2):
        for group in range(GROUPS):
            cols = slice(half * HALF + group * width, half * HALF + (group + 1) * width)
            for row, which in ((4, 0), (5, 2)):
                first = (half * 3 + which) * width
                out_ref[row : row + 1, cols] = total_row(in_ref[group, :, first : first + width])
        out_ref[6:7, half * HALF : (half + 1) * HALF] = total_row(up_ref[half])


def pack_late(vec_ref, out_ref):
    for which in range(2):
        row = total_row(vec_ref[which])
        for n in range(D // HEAD):
            place = which * (D // HEAD) + n
            out_ref[place : place + 1, :] = row[:, n * HEAD : (n + 1) * HEAD]


class VectorTask:
    def __init__(self, refs, whole, places=(), pack=None, done=None):
        self.held, self.landed, self.send_sem, self.recv_sem = refs
        self.whole, self.places, self.pack, self.done = whole, places, pack, done

    def copies(self, stage):
        groups = [[core_flip()]] + [[dp_flip(shift, n) for n in (1, 2, 3)] for shift in SHIFTS]
        return [
            remote(
                self.held.at[stage],
                self.landed.at[stage, n],
                self.send_sem.at[stage, n],
                self.recv_sem.at[stage, n],
                partner,
            )
            for n, partner in enumerate(groups[stage])
        ]

    def add(self, stage):
        held, landed = self.held, self.landed
        if stage > 0:
            held[stage + 1] = (held[stage] + landed[stage, 0]) + (
                landed[stage, 1] + landed[stage, 2]
            )
            return
        got = landed[0, 0]
        if self.whole < got.shape[0]:
            crossed = jnp.concatenate([got[:, HALF:], got[:, :HALF]], axis=1)
            row = lax.broadcasted_iota(jnp.int32, got.shape, 0)
            got = jnp.where(row < self.whole, got, crossed)
        held[1] = held[0] + got

    def run(self, tick):
        if tick == 0:
            self.pack()
        else:
            wait(self.copies(tick - 1))
            self.add(tick - 1)
        if tick <= len(SHIFTS):
            start(self.copies(tick))
        else:
            self.done()

    def finish(self):
        pass


def last_kernel(
    job,
    places,
    factor,
    x_ref,
    dheads_ref,
    dmid_ref,
    w_own,
    w_other,
    gain_ref,
    two_ref,
    sum_ref,
    up_ref,
    in_ref,
    *refs,
):
    tasks = []
    if job is not None:
        source, refs = refs[0], refs[1:]
    (grad_ref, total_ref, late_ref), refs = refs[:3], refs[3:]
    if job is not None:
        result, refs = refs[0], refs[1:]
    (wide, vec_ref), refs = refs[:2], refs[2:]
    if job is not None:
        early, late, refs = refs[:4], refs[4:8], refs[8:]
        for piece in range(2):
            mine = refs[7 * piece : 7 * piece + 7]
            tasks.append(Task(job, mine, source, result, places[piece], piece=piece))

        def pack():
            pack_vectors(two_ref, sum_ref, up_ref, in_ref, early[0].at[0])

        def done():
            total_ref[...] = early[0][1 + len(SHIFTS)] * factor

        tasks.append(VectorTask(early, 4, VECTOR_PLACES, pack, done))
    step = pl.program_id(0)
    last = pl.num_programs(0) - 1

    @pl.when(step == 0)
    def _():
        if tasks:
            greet(reduction_partners())
        vec_ref[...] = jnp.zeros_like(vec_ref)

    run_tasks(step, 0, tasks)
    for piece in range(2):
        take = slice(piece * 256, (piece + 1) * 256)
        for chunk in range(4):
            rows = slice(chunk * 256, (chunk + 1) * 256)
            total = None
            for half, weight in enumerate((w_own, w_other)):
                for which in range(3):
                    term = mul(dheads_ref[half, which, take], weight[which, rows, :], NT)
                    total = term if total is None else total + term
            wide[take, rows] = total
        unit, inverse = unit_of(x_ref[take, :].astype(F32))
        upstream = wide[take, :]
        vec_ref[0] += column_sum(upstream * unit)
        vec_ref[1] += column_sum(upstream)
        grad = dmid_ref[take, :].astype(F32) + norm_back(upstream, unit, inverse, gain_ref[...])
        grad_ref[take, :] = grad.astype(BF)

    if tasks:

        def pack_last():
            pack_late(vec_ref, late[0].at[0])

        def done_last():
            late_ref[...] = late[0][1 + len(SHIFTS)] * factor

        final = VectorTask(late, 2 * D // HEAD, (), pack_last, done_last)

        @pl.when(step == last)
        def _():
            final.run(0)

    run_tasks(step, 1, tasks)

    @pl.when(step == last)
    def _():
        if tasks:
            for tick in range(1, 2 + len(SHIFTS)):
                final.run(tick)
        else:
            pack_vectors(two_ref, sum_ref, up_ref, in_ref, total_ref)
            pack_late(vec_ref, late_ref)
        for task in tasks:
            task.finish()


def finish_kernel(factor, lat_ref, *refs):
    if len(refs) > 1:
        down_in, up_in, out_in, in_a, in_b, lat_out, down_out, up_out, out_out, in_out = refs
        width = HALF // GROUPS
        down_out[...] = down_in[...].astype(F32) * factor
        out_out[...] = out_in[...].astype(F32) * factor
        up_out[...] = up_in[...].astype(F32).T * factor
        for which in range(3):
            for group, part in enumerate((in_a, in_b)):
                in_out[which, :, group * width : (group + 1) * width] = (
                    part[:, which * width : (which + 1) * width].astype(F32) * factor
                )
    else:
        (lat_out,) = refs
    lat_out[...] = lat_ref[...].astype(F32)


def params(**more):
    return pltpu.CompilerParams(vmem_limit_bytes=VMEM_LIMIT, **more)


def per_device(
    latents,
    first_scale,
    first_shift,
    input_weights,
    input_bias,
    output_weight,
    output_bias,
    second_scale,
    second_shift,
    up_weight,
    up_bias,
    down_weight,
    down_bias,
    output_grad,
):
    rows = latents.shape[0]
    images = rows // LAT
    dp, mp = lax.axis_size("dp"), lax.axis_size("mp")
    direct = dp == 16 and mp == 2
    factor = LAT / (rows * dp * mp)
    row = lambda v: v[None, :]
    first_scale, first_shift = row(first_scale), row(first_shift)
    second_scale, second_shift = row(second_scale), row(second_shift)
    output_bias, down_bias = row(output_bias), row(down_bias)

    if direct:
        own = (input_weights, output_weight, up_weight, down_weight)
        small = jnp.concatenate(
            [input_bias, up_bias[None], jnp.zeros((13, HALF), BF)], axis=0
        )
    else:
        gather = lambda v, axis: lax.all_gather(v, "mp", axis=axis, tiled=True)
        w_in, w_out = gather(input_weights, 2), gather(output_weight, 0)
        w_up, w_down = gather(up_weight, 1), gather(down_weight, 0)
        small = jnp.concatenate([gather(input_bias, 1), gather(up_bias, 0)[None]], axis=0)
        own = (w_in[..., :HALF], w_out[:HALF], w_up[:, :HALF], w_down[:HALF])
        others = (w_in[..., HALF:], w_out[HALF:], w_up[:, HALF:], w_down[HALF:], small[:, HALF:])
        small = small[:, :HALF]

    w_shapes = [(3, D, HALF), (HALF, D), (D, HALF), (HALF, D), (16, HALF)]
    normed_shape = shape_of((rows, D), BF)
    heads_shape = shape_of((3, rows, HALF), BF)
    heads_spec = pl.BlockSpec((3, LAT, HALF), lambda i: (0, i, 0))
    vector = kept_spec((1, D))
    bias_spec = whole_spec(small.shape)
    outs = pl.pallas_call(
        functools.partial(first_kernel, direct),
        grid=(images,),
        name="project_own",
        in_specs=[row_spec(D), vector, vector, bias_spec, whole_spec((3, D, HALF))]
        + ([ANY] * 5 if direct else []),
        out_specs=[row_spec(D), heads_spec] + ([ANY] * 5 if direct else []),
        out_shape=[normed_shape, heads_shape]
        + ([shape_of(s, BF) for s in w_shapes] if direct else []),
        scratch_shapes=[pltpu.SemaphoreType.DMA((5,))] * 2 if direct else [],
        compiler_params=params(collective_id=0, has_side_effects=True) if direct else params(),
        cost_estimate=cost(6 * rows * D * HALF, 12 * rows * D),
    )(
        latents,
        first_scale,
        first_shift,
        small,
        own[0],
        *((own + (small,)) if direct else ()),
    )
    normed_one, heads_own = outs[:2]
    if direct:
        others = outs[2:]
    w_in_other, w_out_other, w_up_other, w_down_other, small_other = others
    w_in_own, w_out_own, w_up_own, w_down_own = own

    half_spec = pl.BlockSpec((2, LAT, HALF), lambda i: (0, i, 0))
    half_shape = shape_of((2, rows, HALF), BF)
    head_count = HALF // HEAD
    probs_shape = shape_of((2, head_count, rows, LAT), BF)
    probs_spec = pl.BlockSpec((2, head_count, LAT, LAT), lambda i: (0, 0, i, 0))
    square = (HALF, D)
    tall = (D, HALF)
    parts = ((0, 384), (384, 768), (768, 1024))
    job = Reduction(HALF, D, parts, ORDERS) if direct else None
    result = shape_of(square, BF)
    (
        block_output,
        heads_other,
        probs,
        inverses,
        mixed,
        middle,
        slope,
        g_down,
        g_sum,
    ) = pl.pallas_call(
        forward_kernel,
        grid=(images,),
        name="forward",
        in_specs=[
            row_spec(D),
            row_spec(D),
            heads_spec,
            row_spec(D),
            whole_spec((3, D, HALF)),
            whole_spec(small_other.shape),
            whole_spec(square),
            whole_spec(square),
            vector,
            vector,
            vector,
            whole_spec(tall),
            whole_spec(tall),
            kept_spec((1, HALF)),
            kept_spec((1, HALF)),
            whole_spec(square),
            whole_spec(square),
            vector,
        ],
        out_specs=[
            row_spec(D),
            heads_spec,
            probs_spec,
            row_spec(HEAD),
            half_spec,
            row_spec(D),
            half_spec,
            kept_spec((2, HALF, D)),
            kept_spec((8, D)),
        ],
        out_shape=[
            shape_of((rows, D), F32),
            heads_shape,
            probs_shape,
            shape_of((rows, HEAD), F32),
            half_shape,
            shape_of((rows, D), BF),
            half_shape,
            shape_of((2, HALF, D), BF),
            shape_of((8, D), F32),
        ],
        scratch_shapes=[
            pltpu.VMEM((2, HALF, D), F32),
            pltpu.VMEM((LAT, D), BF),
            pltpu.VMEM((2, LAT, HALF), BF),
            pltpu.VMEM((LAT, D), F32),
        ],
        compiler_params=params(),
        cost_estimate=cost(16 * rows * D * D, 24 * rows * D),
    )(
        latents,
        normed_one,
        heads_own,
        output_grad,
        w_in_other,
        small_other,
        w_out_own,
        w_out_other,
        output_bias,
        second_scale,
        second_shift,
        w_up_own,
        w_up_other,
        small[2:3],
        small_other[2:3],
        w_down_own,
        w_down_other,
        down_bias,
    )

    d_middle, d_mixed, d_dots, g_up, g_out, vec_two, vec_up, *sums = pl.pallas_call(
        functools.partial(feed_back_kernel, job, FEED_PLACES),
        grid=(images,),
        name="feed_back",
        in_specs=[
            row_spec(D),
            half_spec,
            row_spec(D),
            half_spec,
            row_spec(HEAD),
            whole_spec(square),
            whole_spec(square),
            whole_spec(tall),
            whole_spec(tall),
            whole_spec(square),
            whole_spec(square),
            vector,
            vector,
        ]
        + ([ANY] if direct else []),
        out_specs=[
            row_spec(D),
            half_spec,
            row_spec(HEAD),
            kept_spec((2, HALF, D)),
            kept_spec((2, HALF, D)),
            kept_spec((3, 8, D)),
            kept_spec((2, 8, HALF)),
        ]
        + ([ANY] if direct else []),
        out_shape=[
            shape_of((rows, D), BF),
            half_shape,
            shape_of((rows, HEAD), F32),
            shape_of((2, HALF, D), BF),
            shape_of((2, HALF, D), BF),
            shape_of((3, 8, D), F32),
            shape_of((2, 8, HALF), F32),
        ]
        + ([result] if direct else []),
        scratch_shapes=[
            pltpu.VMEM((2, HALF, D), F32),
            pltpu.VMEM((2, HALF, D), F32),
            pltpu.VMEM((LAT, D), BF),
            pltpu.VMEM((LAT, D), F32),
            pltpu.VMEM((2, LAT, HALF), BF),
            pltpu.VMEM((LAT, D), F32),
        ]
        + (job.scratch() if direct else []),
        compiler_params=params(collective_id=1, has_side_effects=True) if direct else params(),
        cost_estimate=cost(10 * rows * D * D, 14 * rows * D),
    )(
        output_grad,
        slope,
        middle,
        mixed,
        inverses,
        w_down_own,
        w_down_other,
        w_up_own,
        w_up_other,
        w_out_own,
        w_out_other,
        second_scale,
        second_shift,
        *((g_down,) if direct else ()),
    )

    per_group = head_count // GROUPS
    width = per_group * HEAD
    group_heads = pl.BlockSpec((3, LAT, width), lambda g, i: (0, i, g))
    group_job = Reduction(
        D // 2, 3 * width, tuple((n * width, (n + 1) * width) for n in range(3)), ORDERS
    )
    group_result = shape_of((D, 3 * width), BF)
    jobs = [job, job, group_job, group_job] if direct else []
    d_heads, g_in, vec_in, *more = pl.pallas_call(
        functools.partial(attend_back_kernel, jobs, ATTEND_PLACES),
        grid=(GROUPS, images),
        name="attend_back",
        in_specs=[
            pl.BlockSpec((LAT, D), lambda g, i: (i, 0)),
            group_heads,
            group_heads,
            pl.BlockSpec((2, per_group, LAT, LAT), lambda g, i: (0, g, i, 0)),
            pl.BlockSpec((2, LAT, width), lambda g, i: (0, i, g)),
            pl.BlockSpec((LAT, HEAD), lambda g, i: (i, 0)),
        ]
        + ([ANY] * 2 if direct else []),
        out_specs=[
            pl.BlockSpec((2, 3, LAT, width), lambda g, i: (0, 0, i, g)),
            pl.BlockSpec(
                (None, 2, D, 3 * width), lambda g, i: (0 if direct else g, 0, 0, 0)
            ),
            pl.BlockSpec((None, 8, 6 * width), lambda g, i: (g, 0, 0)),
        ]
        + [ANY] * (3 if direct else 0),
        out_shape=[
            shape_of((2, 3, rows, HALF), BF),
            shape_of((1 if direct else GROUPS, 2, D, 3 * width), BF),
            shape_of((GROUPS, 8, 6 * width), F32),
        ]
        + ([result, result, group_result] if direct else []),
        scratch_shapes=[
            pltpu.VMEM((D, 6 * width), F32),
            pltpu.VMEM((LAT, 6 * width), BF),
            pltpu.VMEM((LAT, HEAD), F32),
        ]
        + ([pltpu.VMEM((D, 3 * width), BF)] if direct else [])
        + sum([one.scratch() for one in jobs], []),
        compiler_params=params(collective_id=2, has_side_effects=True) if direct else params(),
        cost_estimate=cost(8 * rows * D * D, 20 * rows * D),
    )(
        normed_one,
        heads_own,
        heads_other,
        probs,
        d_mixed,
        d_dots,
        *((g_up, g_out) if direct else ()),
    )

    late_shape = (2 * D // HEAD, HEAD)
    stages = 1 + len(SHIFTS)

    def vector_scratch(shape):
        return [
            pltpu.VMEM((stages + 1,) + shape, F32),
            pltpu.VMEM((stages, 3) + shape, F32),
            pltpu.SemaphoreType.DMA((stages, 3)),
            pltpu.SemaphoreType.DMA((stages, 3)),
        ]

    grad_low, vectors, late, *last = pl.pallas_call(
        functools.partial(
            last_kernel, group_job if direct else None, LAST_PLACES, factor
        ),
        grid=(images,),
        name="input_back",
        in_specs=[
            row_spec(D),
            pl.BlockSpec((2, 3, LAT, HALF), lambda i: (0, 0, i, 0)),
            row_spec(D),
            whole_spec((3, D, HALF)),
            whole_spec((3, D, HALF)),
            vector,
            kept_spec((3, 8, D)),
            kept_spec((8, D)),
            kept_spec((2, 8, HALF)),
            kept_spec((GROUPS, 8, 6 * width)),
        ]
        + ([ANY] if direct else []),
        out_specs=[row_spec(D), kept_spec((8, D)), kept_spec(late_shape)]
        + ([ANY] if direct else []),
        out_shape=[shape_of((rows, D), BF), shape_of((8, D), F32), shape_of(late_shape, F32)]
        + ([group_result] if direct else []),
        scratch_shapes=[pltpu.VMEM((LAT, D), F32), pltpu.VMEM((2, 8, D), F32)]
        + (
            vector_scratch((8, D))
            + vector_scratch(late_shape)
            + group_job.scratch() * 2
            if direct
            else []
        ),
        compiler_params=params(collective_id=3, has_side_effects=True) if direct else params(),
        cost_estimate=cost(6 * rows * D * D, 14 * rows * D),
    )(
        latents,
        d_heads,
        d_middle,
        w_in_own,
        w_in_other,
        first_scale,
        vec_two,
        g_sum,
        vec_up,
        vec_in,
        *((g_in.reshape(2, D, 3 * width),) if direct else ()),
    )

    pieces = 8
    cut = rows // pieces
    if direct:
        latents_grad, g_down, g_up, g_out, g_in = pl.pallas_call(
            functools.partial(finish_kernel, factor),
            grid=(pieces,),
            name="finish",
            in_specs=[
                pl.BlockSpec((cut, D), lambda i: (i, 0)),
                pl.BlockSpec((HALF // pieces, D), lambda i: (i, 0)),
                pl.BlockSpec((HALF, D // pieces), lambda i: (0, i)),
                pl.BlockSpec((HALF // pieces, D), lambda i: (i, 0)),
                pl.BlockSpec((D // pieces, 3 * width), lambda i: (i, 0)),
                pl.BlockSpec((D // pieces, 3 * width), lambda i: (i, 0)),
            ],
            out_specs=[
                pl.BlockSpec((cut, D), lambda i: (i, 0)),
                pl.BlockSpec((HALF // pieces, D), lambda i: (i, 0)),
                pl.BlockSpec((D // pieces, HALF), lambda i: (i, 0)),
                pl.BlockSpec((HALF // pieces, D), lambda i: (i, 0)),
                pl.BlockSpec((3, D // pieces, HALF), lambda i: (0, i, 0)),
            ],
            out_shape=[
                shape_of((rows, D), F32),
                shape_of((HALF, D), F32),
                shape_of((D, HALF), F32),
                shape_of((HALF, D), F32),
                shape_of((3, D, HALF), F32),
            ],
            compiler_params=params(),
        )(grad_low, sums[0], more[0], more[1], more[2], last[0])
        mine = vectors[4:7, :HALF]
    else:
        latents_grad = pl.pallas_call(
            functools.partial(finish_kernel, factor),
            grid=(pieces,),
            name="finish",
            in_specs=[pl.BlockSpec((cut, D), lambda i: (i, 0))],
            out_specs=pl.BlockSpec((cut, D), lambda i: (i, 0)),
            out_shape=shape_of((rows, D), F32),
            compiler_params=params(),
        )(grad_low)
        vectors = lax.psum(vectors, ("dp", "mp")) * factor
        late = lax.psum(late, ("dp", "mp")) * factor
        own_width = D // mp
        mine = lax.dynamic_slice_in_dim(
            vectors[4:7], lax.axis_index("mp") * own_width, own_width, 1
        )
        g_down, g_up, g_out = (v.reshape(D, D) for v in (g_down, g_up, g_out))
        g_in = jnp.transpose(g_in.reshape(GROUPS, 2, D, 3, width), (3, 2, 1, 0, 4))
        g_in = g_in.reshape(3, D, D)

        def scatter(v, axis):
            v = lax.psum_scatter(v, "mp", scatter_dimension=axis, tiled=True)
            return lax.psum(v, "dp").astype(F32) * factor

        g_down, g_up, g_out = scatter(g_down, 0), scatter(g_up.T, 1), scatter(g_out, 0)
        g_in = scatter(g_in, 2)

    late = late.reshape(2, D)
    return (
        block_output,
        latents_grad,
        late[0],
        late[1],
        g_in,
        mine[:2],
        g_out,
        vectors[0],
        vectors[1],
        vectors[2],
        g_up,
        mine[2],
        g_down,
        vectors[3],
    )


def solution(mesh):
    return jax.shard_map(
        per_device,
        mesh=mesh,
        in_specs=(
            P(("dp", "mp"), None),
            P(),
            P(),
            P(None, None, "mp"),
            P(None, "mp"),
            P("mp", None),
            P(),
            P(),
            P(),
            P(None, "mp"),
            P("mp"),
            P("mp", None),
            P(),
            P(("dp", "mp"), None),
        ),
        out_specs=(
            P(("dp", "mp"), None),
            P(("dp", "mp"), None),
            P(),
            P(),
            P(None, None, "mp"),
            P(None, "mp"),
            P("mp", None),
            P(),
            P(),
            P(),
            P(None, "mp"),
            P("mp"),
            P("mp", None),
            P(),
        ),
        check_vma=False,
    )
```

```python
import functools

import jax
import jax.numpy as jnp
from jax import lax
from jax.experimental import pallas as pl
from jax.experimental.pallas import tpu as pltpu
from jax.sharding import PartitionSpec as P

D = 1024
HEAD = 128
HEADS = 8
LAT = 512
HALF = 512
GROUPS = 2
EPS = 1e-05
SCALE = HEAD ** (-0.5)
LOG2E = 1.4426950408889634
GELU_A = 0.7978845608028654
GELU_B = 0.044715
MESH = pl.DeviceIdType.MESH
NN = (((1,), (0,)), ((), ()))
NT = (((1,), (1,)), ((), ()))
TN = (((0,), (0,)), ((), ()))
BF = jnp.bfloat16
F32 = jnp.float32
VMEM_LIMIT = 60 << 20


def mul(a, b, dims):
    return lax.dot_general(a, b, dims, preferred_element_type=F32)


def unit_of(rows):
    centred = rows - jnp.mean(rows, axis=-1, keepdims=True)
    inverse = lax.rsqrt(jnp.mean(centred * centred, axis=-1, keepdims=True) + EPS)
    return centred * inverse, inverse


def norm_back(upstream, unit, inverse, gain):
    scaled = upstream * gain
    inner = (
        scaled
        - jnp.mean(scaled, axis=-1, keepdims=True)
        - unit * jnp.mean(scaled * unit, axis=-1, keepdims=True)
    )
    return inverse * inner


def column_sum(values):
    return jnp.sum(values.reshape(values.shape[0] // 8, 8, values.shape[1]), axis=0)


def row_spec(width):
    return pl.BlockSpec((LAT, width), lambda i: (i, 0))


def whole_spec(shape):
    return pl.BlockSpec(shape, lambda *_: (0,) * len(shape), pipeline_mode=pl.Buffered(1))


def kept_spec(shape):
    return pl.BlockSpec(shape, lambda *_: (0,) * len(shape))


ANY = pl.BlockSpec(memory_space=pl.ANY)


def shape_of(shape, dtype):
    return jax.ShapeDtypeStruct(shape, dtype)


def cost(flops, moved):
    return pl.CostEstimate(flops=int(flops), bytes_accessed=int(moved), transcendentals=0)


def flipped(place, other):
    for bit in (1, 2):
        if other & bit:
            place = place + bit - 2 * bit * lax.rem(place // bit, 2)
    return place


def dp_flip(shift, other):
    me = lax.axis_index("dp")
    place = lax.rem(me // (1 << shift), 4)
    return (me + (flipped(place, other) - place) * (1 << shift), lax.axis_index("mp"))


def start(copies):
    for copy in copies:
        copy.start()


def wait(copies):
    for copy in copies:
        copy.wait()


def core_flip():
    return (lax.axis_index("dp"), 1 - lax.axis_index("mp"))


def greet(partners):
    barrier = pltpu.get_barrier_semaphore()
    for partner in partners:
        pl.semaphore_signal(barrier, inc=1, device_id=partner, device_id_type=MESH)
    pl.semaphore_wait(barrier, len(partners))


def remote(src, dst, send, recv, partner):
    return pltpu.make_async_remote_copy(
        src_ref=src,
        dst_ref=dst,
        send_sem=send,
        recv_sem=recv,
        device_id=partner,
        device_id_type=MESH,
    )


class Reduction:
    def __init__(self, rows, columns, parts, orders):
        self.rows, self.columns, self.parts, self.orders = rows, columns, parts, orders
        self.stages = len(orders[0])
        self.ticks = 2 * self.stages + 2

    def scratch(self):
        copies = (len(self.parts), 2 * self.stages, 3)
        return [
            pltpu.VMEM((self.rows, self.columns), BF),
            pltpu.VMEM((self.rows, self.columns), BF),
            pltpu.VMEM((self.rows, self.columns), BF),
            pltpu.SemaphoreType.DMA((2,)),
            pltpu.SemaphoreType.DMA(copies),
            pltpu.SemaphoreType.DMA(copies),
            pltpu.SemaphoreType.DMA((2,)),
        ]

    def place(self, part, stage):
        shift, members = self.orders[part][stage]
        return lax.rem(lax.axis_index("dp") // (1 << shift), members)

    def size(self, stage):
        rows = self.rows
        for _, members in self.orders[0][: stage + 1]:
            rows //= members
        return rows

    def others(self, stage):
        return (1,) if self.orders[0][stage][1] == 2 else (3, 1, 2)

    def offset(self, part, level):
        row = 0
        for stage in range(level):
            row = row + self.place(part, stage) * self.size(stage)
        return row

    def aligned(self, row, size):
        return pl.ds(pl.multiple_of(row, size), size)

    def columns_of(self, part):
        first, last = self.parts[part]
        return pl.ds(first, last - first)

    def partner(self, part, stage, other):
        return dp_flip(self.orders[part][stage][0], other)

    def landing(self, stage, other):
        size = self.size(stage)
        first = self.rows - self.orders[0][stage][1] * size
        return pl.ds(first + (other - 1) * size, size)

    def adding(self, refs, part, stage):
        cur, _, recv, _, send_sem, recv_sem = refs[:6]
        size = self.size(stage)
        base, cols = self.offset(part, stage), self.columns_of(part)
        copies = []
        for other in self.others(stage):
            theirs = flipped(self.place(part, stage), other)
            copies.append(
                remote(
                    cur.at[self.aligned(base + theirs * size, size), cols],
                    recv.at[self.landing(stage, other), cols],
                    send_sem.at[part, stage, other - 1],
                    recv_sem.at[part, stage, other - 1],
                    self.partner(part, stage, other),
                )
            )
        return copies

    def handing(self, refs, part, step):
        _, full, _, _, send_sem, recv_sem = refs[:6]
        stage = self.stages - 1 - step
        size = self.size(stage)
        rows, cols = self.aligned(self.offset(part, stage + 1), size), self.columns_of(part)
        return [
            remote(
                full.at[rows, cols],
                full.at[rows, cols],
                send_sem.at[part, self.stages + step, other - 1],
                recv_sem.at[part, self.stages + step, other - 1],
                self.partner(part, stage, other),
            )
            for other in self.others(stage)
        ]

    def exchange(self, refs, other):
        return remote(other, refs[1], refs[3].at[0], refs[3].at[1], core_flip())

    def tick(self, refs, tick, other):
        cur, landed, recv = refs[:3]
        parts = range(len(self.parts))
        if tick == 0:
            self.exchange(refs, other).start()
            return
        if tick == 1:
            self.exchange(refs, other).wait()
            cur[...] = (cur[...].astype(F32) + landed[...].astype(F32)).astype(BF)
            for part in parts:
                start(self.adding(refs, part, 0))
            return
        if tick <= self.stages + 1:
            stage = tick - 2
            for part in parts:
                wait(self.adding(refs, part, stage))
                size = self.size(stage)
                keep, cols = self.aligned(self.offset(part, stage + 1), size), self.columns_of(part)
                total = cur[keep, cols].astype(F32)
                for other in sorted(self.others(stage)):
                    total = total + recv[self.landing(stage, other), cols].astype(F32)
                if stage + 1 < self.stages:
                    cur[keep, cols] = total.astype(BF)
                    start(self.adding(refs, part, stage + 1))
                else:
                    landed[keep, cols] = total.astype(BF)
                    start(self.handing(refs, part, 0))
            return
        step = tick - self.stages - 2
        for part in parts:
            wait(self.handing(refs, part, step))
            if step + 1 < self.stages:
                start(self.handing(refs, part, step + 1))


class Task:
    def __init__(self, job, refs, source, result, places, staged=False, piece=0):
        self.job, self.refs, self.places, self.staged = job, refs, places, staged
        window = pl.ds(piece * job.rows, job.rows)
        self.own = None if staged else source.at[0, window]
        self.other = source.at[window] if staged else source.at[1, window]
        self.result = result.at[window]

    def load(self):
        return pltpu.make_async_copy(self.own, self.refs[0], self.refs[6].at[0])

    def store(self):
        return pltpu.make_async_copy(self.refs[1], self.result, self.refs[6].at[1])

    def run(self, tick):
        if tick == 0 and not self.staged:
            self.load().start()
        if tick == 1 and not self.staged:
            self.load().wait()
        self.job.tick(self.refs, tick, self.other)
        if tick == self.job.ticks - 1:
            self.store().start()

    def finish(self):
        self.store().wait()


def run_tasks(step, place, tasks):
    for now in sorted({at[0] for task in tasks for at in task.places if at[1] == place}):

        @pl.when(step == now)
        def _():
            for task in tasks:
                for tick, at in enumerate(task.places):
                    if at == (now, place):
                        task.run(tick)


ORDERS = (((0, 2), (1, 2), (2, 4)), ((1, 2), (0, 2), (2, 4)), ((2, 2), (3, 2), (0, 4)))
SHIFTS = (0, 2)


def starts(steps, *numbers):
    return tuple((n, 0) if n < steps else (steps - 1, 1) for n in numbers)


FEED_PLACES = starts(8, 0, 1, 2, 3, 4, 5, 6, 7)
ATTEND_PLACES = (
    starts(16, 0, 1, 3, 5, 7, 9, 11, 13),
    starts(16, 1, 2, 4, 6, 8, 10, 12, 15),
    ((7, 1),) + starts(16, 9, 10, 11, 12, 13, 14, 16),
    ((7, 1),) + starts(16, 10, 11, 12, 13, 14, 15, 16),
)
LAST_PLACES = (
    starts(8, 0, 1, 2, 3, 4, 5, 6, 7),
    starts(8, 0, 1, 2, 3, 4, 6, 7, 8),
)
VECTOR_PLACES = starts(8, 1, 2, 4, 6)


def reduction_partners():
    return [core_flip()] + [dp_flip(shift, other) for shift in SHIFTS for other in (1, 2, 3)]


def first_kernel(
    spread, x_ref, gain_ref, shift_ref, bias_ref, w_in, *refs
):
    step = pl.program_id(0)
    if spread:
        sources = (w_in_any, w_out, w_up, w_down, bias_all) = refs[:5]
        normed_ref, heads_ref = refs[5:7]
        targets = refs[7:12]
        send_sem, recv_sem = refs[12:14]

        def copies():
            return [
                remote(src, dst, send_sem.at[n], recv_sem.at[n], core_flip())
                for n, (src, dst) in enumerate(zip(sources, targets))
            ]

        @pl.when(step == 0)
        def _():
            greet([core_flip()])
            for copy in copies():
                copy.start()
    else:
        normed_ref, heads_ref = refs

    for piece in range(2):
        rows = slice(piece * 256, (piece + 1) * 256)
        unit, _ = unit_of(x_ref[rows, :].astype(F32))
        normed_ref[rows, :] = (unit * gain_ref[...] + shift_ref[...]).astype(BF)
        project(normed_ref, w_in, bias_ref, heads_ref, rows)

    if spread:

        @pl.when(step == pl.num_programs(0) - 1)
        def _():
            for copy in copies():
                copy.wait()


def project(normed_ref, weights, bias_ref, heads_ref, rows=slice(0, LAT)):
    for which in range(3):
        heads = mul(normed_ref[rows, :], weights[which], NN)
        if which != 1:
            place = 0 if which == 0 else 1
            heads = heads + bias_ref[place : place + 1, :].astype(F32)
        heads_ref[which, rows, :] = heads.astype(BF)


def forward_kernel(
    x_ref,
    normed_ref,
    own_ref,
    g_ref,
    w_in,
    in_bias,
    wo_own,
    wo_other,
    out_bias,
    gain_ref,
    shift_ref,
    wu_own,
    wu_other,
    ub_own,
    ub_other,
    wd_own,
    wd_other,
    down_bias,
    block_ref,
    other_ref,
    probs_ref,
    inv_ref,
    mixed_ref,
    middle_ref,
    slope_ref,
    gdown_ref,
    gsum_ref,
    acc,
    normed_two,
    act,
    wide,
):
    step = pl.program_id(0)

    @pl.when(step == 0)
    def _():
        acc[...] = jnp.zeros_like(acc)
        gsum_ref[...] = jnp.zeros_like(gsum_ref)

    project(normed_ref, w_in, in_bias, other_ref)
    lane = lax.broadcasted_iota(jnp.int32, (LAT, HEAD), 1)
    ones = jnp.ones((LAT, HEAD), BF)
    inverses = jnp.zeros((LAT, HEAD), F32)
    for half, heads_ref in enumerate((own_ref, other_ref)):
        for head in range(HALF // HEAD):
            cols = slice(head * HEAD, (head + 1) * HEAD)
            scores = mul(heads_ref[0, :, cols], heads_ref[1, :, cols], NT)
            highest = jnp.max(scores, axis=-1, keepdims=True)
            powers = jnp.exp2((scores - highest) * (SCALE * LOG2E))
            low = powers.astype(BF)
            probs_ref[half, head] = low
            both = mul(low, jnp.concatenate([heads_ref[2, :, cols], ones], axis=1), NN)
            inverse = 1.0 / both[:, HEAD:]
            mixed_ref[half, :, cols] = (both[:, :HEAD] * inverse).astype(BF)
            inverses = jnp.where(lane == half * 4 + head, inverse, inverses)
    inv_ref[...] = inverses
    for chunk in range(4):
        cols = slice(chunk * 256, (chunk + 1) * 256)
        wide[:, cols] = (
            x_ref[:, cols].astype(F32)
            + mul(mixed_ref[0], wo_own[:, cols], NN)
            + mul(mixed_ref[1], wo_other[:, cols], NN)
            + out_bias[:, cols]
        )
    middle = wide[...]
    middle_ref[...] = middle.astype(BF)
    unit, _ = unit_of(middle)
    normed_two[...] = (unit * gain_ref[...] + shift_ref[...]).astype(BF)
    for half, (weight, bias) in enumerate(((wu_own, ub_own), (wu_other, ub_other))):
        for chunk in range(2):
            cols = slice(chunk * 256, (chunk + 1) * 256)
            hidden = mul(normed_two[...], weight[:, cols], NN) + bias[2:3, cols].astype(F32)
            square = hidden * hidden
            gate = jnp.tanh(GELU_A * (hidden + GELU_B * (square * hidden)))
            lift = 0.5 * (1.0 + gate)
            act[half, :, cols] = (hidden * lift).astype(BF)
            slope = lift + (0.5 * GELU_A) * hidden * (1.0 - gate * gate) * (
                1.0 + (3.0 * GELU_B) * square
            )
            slope_ref[half, :, cols] = slope.astype(BF)
    for chunk in range(4):
        cols = slice(chunk * 256, (chunk + 1) * 256)
        block_ref[:, cols] = (
            wide[:, cols]
            + mul(act[0], wd_own[:, cols], NN)
            + mul(act[1], wd_other[:, cols], NN)
            + down_bias[:, cols]
        )
    for half in range(2):
        acc[half] += mul(act[half], g_ref[...], TN)
    gsum_ref[...] += column_sum(g_ref[...].astype(F32))

    @pl.when(step == pl.num_programs(0) - 1)
    def _():
        gdown_ref[...] = acc[...].astype(BF)


def feed_back_kernel(
    job,
    places,
    g_ref,
    slope_ref,
    middle_ref,
    mixed_ref,
    inv_ref,
    wd_own,
    wd_other,
    wu_own,
    wu_other,
    wo_own,
    wo_other,
    gain_ref,
    shift_ref,
    *refs,
):
    tasks = []
    if job is not None:
        source, refs = refs[0], refs[1:]
    outs, refs = refs[:7], refs[7:]
    if job is not None:
        result, refs = refs[0], refs[1:]
    dmid_ref, dmix_ref, dot_ref, gup_ref, gout_ref, vec_ref, ubias_ref = outs
    acc_up, acc_out, normed_two, unit_ref, dhid, wide = refs[:6]
    if job is not None:
        tasks.append(Task(job, refs[6:], source, result, places))
    step = pl.program_id(0)

    @pl.when(step == 0)
    def _():
        if tasks:
            greet(reduction_partners())
        acc_up[...] = jnp.zeros_like(acc_up)
        acc_out[...] = jnp.zeros_like(acc_out)
        vec_ref[...] = jnp.zeros_like(vec_ref)
        ubias_ref[...] = jnp.zeros_like(ubias_ref)

    run_tasks(step, 0, tasks)
    lane = lax.broadcasted_iota(jnp.int32, (256, HEAD), 1)
    for piece in range(2):
        rows = slice(piece * 256, (piece + 1) * 256)
        for half, weight in enumerate((wd_own, wd_other)):
            for chunk in range(2):
                cols = slice(chunk * 256, (chunk + 1) * 256)
                down = mul(g_ref[rows, :], weight[cols, :], NT)
                dhid[half, rows, cols] = (down * slope_ref[half, rows, cols].astype(F32)).astype(BF)
            ubias_ref[half] += column_sum(dhid[half, rows].astype(F32))
        unit, inverse = unit_of(middle_ref[rows, :].astype(F32))
        unit_ref[rows, :] = unit
        normed_two[rows, :] = (unit * gain_ref[...] + shift_ref[...]).astype(BF)
        for chunk in range(4):
            cols = slice(chunk * 256, (chunk + 1) * 256)
            wide[rows, cols] = mul(dhid[0, rows], wu_own[cols, :], NT) + mul(
                dhid[1, rows], wu_other[cols, :], NT
            )
        upstream = wide[rows, :]
        unit = unit_ref[rows, :]
        vec_ref[0] += column_sum(upstream * unit)
        vec_ref[1] += column_sum(upstream)
        dmid = g_ref[rows, :].astype(F32) + norm_back(upstream, unit, inverse, gain_ref[...])
        vec_ref[2] += column_sum(dmid)
        dmid_ref[rows, :] = dmid.astype(BF)
    for half in range(2):
        acc_up[half] += mul(dhid[half], normed_two[...], TN)
    for half in range(2):
        acc_out[half] += mul(mixed_ref[half], dmid_ref[...], TN)
    for piece in range(2):
        rows = slice(piece * 256, (piece + 1) * 256)
        dots = jnp.zeros((256, HEAD), F32)
        for half, weight in enumerate((wo_own, wo_other)):
            for pair in range(2):
                both = mul(dmid_ref[rows, :], weight[pair * 256 : (pair + 1) * 256, :], NT)
                for one in range(2):
                    head = pair * 2 + one
                    cols = slice(head * HEAD, (head + 1) * HEAD)
                    place = half * 4 + head
                    scaled = both[:, one * HEAD : (one + 1) * HEAD] * inv_ref[rows, place : place + 1]
                    dmix_ref[half, rows, cols] = scaled.astype(BF)
                    total = jnp.sum(
                        scaled * mixed_ref[half, rows, cols].astype(F32), axis=-1, keepdims=True
                    )
                    dots = jnp.where(lane == place, total, dots)
        dot_ref[rows, :] = dots

    @pl.when(step == pl.num_programs(0) - 1)
    def _():
        gup_ref[...] = acc_up[...].astype(BF)
        gout_ref[...] = acc_out[...].astype(BF)
        for task in tasks:
            task.finish()


def attend_back_kernel(
    jobs,
    places,
    normed_ref,
    own_ref,
    other_ref,
    probs_ref,
    dmix_ref,
    dot_ref,
    *refs,
):
    tasks, count = [], len(jobs)
    if jobs:
        sources, refs = refs[: count - 2], refs[count - 2 :]
    dheads_ref, gin_ref, vec_ref = refs[:3]
    refs = refs[3:]
    if jobs:
        results, refs = refs[: count - 1], refs[count - 1 :]
    acc, joined, dots_now = refs[:3]
    if jobs:
        staged, refs = refs[3], refs[4:]
        for n, job in enumerate(jobs):
            mine = refs[7 * n : 7 * n + 7]
            if n < count - 2:
                tasks.append(Task(job, mine, sources[n], results[n], places[n]))
            else:
                piece = n - (count - 2)
                tasks.append(Task(job, mine, staged, results[-1], places[n], True, piece))
    group, step = pl.program_id(0), pl.program_id(1)
    now = group * pl.num_programs(1) + step
    per_group = HALF // HEAD // GROUPS
    width = per_group * HEAD

    if tasks:

        @pl.when(now == 0)
        def _():
            greet(reduction_partners())

    @pl.when(step == 0)
    def _():
        acc[...] = jnp.zeros_like(acc)
        vec_ref[...] = jnp.zeros_like(vec_ref)

    @pl.when(group == 0)
    def _():
        for place in range(4):
            lane = (place // 2) * 4 + place % 2
            dots_now[:, place : place + 1] = dot_ref[:, lane : lane + 1]

    @pl.when(group == 1)
    def _():
        for place in range(4):
            lane = (place // 2) * 4 + 2 + place % 2
            dots_now[:, place : place + 1] = dot_ref[:, lane : lane + 1]

    run_tasks(now, 0, tasks)
    for half, heads_ref in enumerate((own_ref, other_ref)):
        for head in range(per_group):
            cols = slice(head * HEAD, (head + 1) * HEAD)
            place = half * per_group + head
            probs = probs_ref[half, head]
            upstream = dmix_ref[half, :, cols]
            d_probs = mul(upstream, heads_ref[2, :, cols], NT) - dots_now[:, place : place + 1]
            d_scores = (probs.astype(F32) * d_probs).astype(BF)
            d_query = (mul(d_scores, heads_ref[1, :, cols], NN) * SCALE).astype(BF)
            d_keys = (mul(heads_ref[0, :, cols], d_scores, TN) * SCALE).T.astype(BF)
            d_values = mul(upstream, probs, TN).T.astype(BF)
            for which, value in enumerate((d_query, d_keys, d_values)):
                dheads_ref[half, which, :, cols] = value
                first = half * 3 * width + which * width + head * HEAD
                joined[:, first : first + HEAD] = value
    vec_ref[...] += column_sum(joined[...].astype(F32))
    for chunk in range(4):
        rows = slice(chunk * 256, (chunk + 1) * 256)
        acc[rows, :] += mul(normed_ref[:, rows], joined[...], TN)

    @pl.when((now if tasks else step) == pl.num_programs(1) * (GROUPS if tasks else 1) - 1)
    def _():
        for half in range(2):
            cols = slice(half * 3 * width, (half + 1) * 3 * width)
            gin_ref[half] = acc[:, cols].astype(BF)

    if tasks:

        @pl.when(now == pl.num_programs(1) - 1)
        def _():
            for piece in range(2):
                rows = slice(piece * D // 2, (piece + 1) * D // 2)
                tasks[piece - 2].refs[0][...] = acc[rows, : 3 * width].astype(BF)
            staged[...] = acc[:, 3 * width :].astype(BF)

    run_tasks(now, 1, tasks)

    if tasks:

        @pl.when(now == pl.num_programs(0) * pl.num_programs(1) - 1)
        def _():
            for task in tasks:
                task.finish()


def total_row(v):
    return jnp.sum(v, axis=0, keepdims=True)


def pack_vectors(two_ref, sum_ref, up_ref, in_ref, out_ref):
    width = HALF // GROUPS
    out_ref[...] = jnp.zeros_like(out_ref)
    out_ref[0:1, :] = total_row(two_ref[2])
    out_ref[1:2, :] = total_row(two_ref[0])
    out_ref[2:3, :] = total_row(two_ref[1])
    out_ref[3:4, :] = total_row(sum_ref[...])
    for half in range(2):
        for group in range(GROUPS):
            cols = slice(half * HALF + group * width, half * HALF + (group + 1) * width)
            for row, which in ((4, 0), (5, 2)):
                first = (half * 3 + which) * width
                out_ref[row : row + 1, cols] = total_row(in_ref[group, :, first : first + width])
        out_ref[6:7, half * HALF : (half + 1) * HALF] = total_row(up_ref[half])


def pack_late(vec_ref, out_ref):
    for which in range(2):
        row = total_row(vec_ref[which])
        for n in range(D // HEAD):
            place = which * (D // HEAD) + n
            out_ref[place : place + 1, :] = row[:, n * HEAD : (n + 1) * HEAD]


class VectorTask:
    def __init__(self, refs, whole, places=(), pack=None, done=None):
        self.held, self.landed, self.send_sem, self.recv_sem = refs
        self.whole, self.places, self.pack, self.done = whole, places, pack, done

    def copies(self, stage):
        groups = [[core_flip()]] + [[dp_flip(shift, n) for n in (1, 2, 3)] for shift in SHIFTS]
        return [
            remote(
                self.held.at[stage],
                self.landed.at[stage, n],
                self.send_sem.at[stage, n],
                self.recv_sem.at[stage, n],
                partner,
            )
            for n, partner in enumerate(groups[stage])
        ]

    def add(self, stage):
        held, landed = self.held, self.landed
        if stage > 0:
            held[stage + 1] = (held[stage] + landed[stage, 0]) + (
                landed[stage, 1] + landed[stage, 2]
            )
            return
        got = landed[0, 0]
        if self.whole < got.shape[0]:
            crossed = jnp.concatenate([got[:, HALF:], got[:, :HALF]], axis=1)
            row = lax.broadcasted_iota(jnp.int32, got.shape, 0)
            got = jnp.where(row < self.whole, got, crossed)
        held[1] = held[0] + got

    def run(self, tick):
        if tick == 0:
            self.pack()
        else:
            wait(self.copies(tick - 1))
            self.add(tick - 1)
        if tick <= len(SHIFTS):
            start(self.copies(tick))
        else:
            self.done()

    def finish(self):
        pass


def last_kernel(
    job,
    places,
    factor,
    x_ref,
    dheads_ref,
    dmid_ref,
    w_own,
    w_other,
    gain_ref,
    two_ref,
    sum_ref,
    up_ref,
    in_ref,
    *refs,
):
    tasks = []
    if job is not None:
        source, refs = refs[0], refs[1:]
    (grad_ref, total_ref, late_ref), refs = refs[:3], refs[3:]
    if job is not None:
        result, refs = refs[0], refs[1:]
    (wide, vec_ref), refs = refs[:2], refs[2:]
    if job is not None:
        early, late, refs = refs[:4], refs[4:8], refs[8:]
        for piece in range(2):
            mine = refs[7 * piece : 7 * piece + 7]
            tasks.append(Task(job, mine, source, result, places[piece], piece=piece))

        def pack():
            pack_vectors(two_ref, sum_ref, up_ref, in_ref, early[0].at[0])

        def done():
            total_ref[...] = early[0][1 + len(SHIFTS)] * factor

        tasks.append(VectorTask(early, 4, VECTOR_PLACES, pack, done))
    step = pl.program_id(0)
    last = pl.num_programs(0) - 1

    @pl.when(step == 0)
    def _():
        if tasks:
            greet(reduction_partners())
        vec_ref[...] = jnp.zeros_like(vec_ref)

    run_tasks(step, 0, tasks)
    for piece in range(2):
        take = slice(piece * 256, (piece + 1) * 256)
        for chunk in range(4):
            rows = slice(chunk * 256, (chunk + 1) * 256)
            total = None
            for half, weight in enumerate((w_own, w_other)):
                for which in range(3):
                    term = mul(dheads_ref[half, which, take], weight[which, rows, :], NT)
                    total = term if total is None else total + term
            wide[take, rows] = total
        unit, inverse = unit_of(x_ref[take, :].astype(F32))
        upstream = wide[take, :]
        vec_ref[0] += column_sum(upstream * unit)
        vec_ref[1] += column_sum(upstream)
        grad = dmid_ref[take, :].astype(F32) + norm_back(upstream, unit, inverse, gain_ref[...])
        grad_ref[take, :] = grad.astype(BF)

    if tasks:

        def pack_last():
            pack_late(vec_ref, late[0].at[0])

        def done_last():
            late_ref[...] = late[0][1 + len(SHIFTS)] * factor

        final = VectorTask(late, 2 * D // HEAD, (), pack_last, done_last)

        @pl.when(step == last)
        def _():
            final.run(0)

    run_tasks(step, 1, tasks)

    @pl.when(step == last)
    def _():
        if tasks:
            for tick in range(1, 2 + len(SHIFTS)):
                final.run(tick)
        else:
            pack_vectors(two_ref, sum_ref, up_ref, in_ref, total_ref)
            pack_late(vec_ref, late_ref)
        for task in tasks:
            task.finish()


def finish_kernel(factor, lat_ref, *refs):
    if len(refs) > 1:
        down_in, up_in, out_in, in_a, in_b, total_ref, late_ref = refs[:7]
        lat_out, down_out, up_out, out_out, in_out = refs[7:12]
        rows, late_rows = refs[12:16], refs[16:18]
        in_bias_out, up_bias_out = refs[18:]
        width = HALF // GROUPS
        down_out[...] = down_in[...].astype(F32) * factor
        out_out[...] = out_in[...].astype(F32) * factor
        up_out[...] = up_in[...].astype(F32).T * factor
        for which in range(3):
            for group, part in enumerate((in_a, in_b)):
                in_out[which, :, group * width : (group + 1) * width] = (
                    part[:, which * width : (which + 1) * width].astype(F32) * factor
                )

        @pl.when(pl.program_id(0) == 0)
        def _():
            for n, row in enumerate(rows):
                row[...] = total_ref[n : n + 1, :]
            for which, row in enumerate(late_rows):
                for n in range(D // HEAD):
                    place = which * (D // HEAD) + n
                    row[:, n * HEAD : (n + 1) * HEAD] = late_ref[place : place + 1, :]
            in_bias_out[...] = total_ref[4:6, :HALF]
            up_bias_out[...] = total_ref[6:7, :HALF]

    else:
        (lat_out,) = refs
    lat_out[...] = lat_ref[...].astype(F32)


def params(**more):
    return pltpu.CompilerParams(vmem_limit_bytes=VMEM_LIMIT, **more)


def per_device(
    latents,
    first_scale,
    first_shift,
    input_weights,
    input_bias,
    output_weight,
    output_bias,
    second_scale,
    second_shift,
    up_weight,
    up_bias,
    down_weight,
    down_bias,
    output_grad,
):
    rows = latents.shape[0]
    images = rows // LAT
    dp, mp = lax.axis_size("dp"), lax.axis_size("mp")
    direct = dp == 16 and mp == 2
    factor = LAT / (rows * dp * mp)
    row = lambda v: v[None, :]
    first_scale, first_shift = row(first_scale), row(first_shift)
    second_scale, second_shift = row(second_scale), row(second_shift)
    output_bias, down_bias = row(output_bias), row(down_bias)

    if direct:
        own = (input_weights, output_weight, up_weight, down_weight)
        small = jnp.concatenate(
            [input_bias, up_bias[None], jnp.zeros((13, HALF), BF)], axis=0
        )
    else:
        gather = lambda v, axis: lax.all_gather(v, "mp", axis=axis, tiled=True)
        w_in, w_out = gather(input_weights, 2), gather(output_weight, 0)
        w_up, w_down = gather(up_weight, 1), gather(down_weight, 0)
        small = jnp.concatenate([gather(input_bias, 1), gather(up_bias, 0)[None]], axis=0)
        own = (w_in[..., :HALF], w_out[:HALF], w_up[:, :HALF], w_down[:HALF])
        others = (w_in[..., HALF:], w_out[HALF:], w_up[:, HALF:], w_down[HALF:], small[:, HALF:])
        small = small[:, :HALF]

    w_shapes = [(3, D, HALF), (HALF, D), (D, HALF), (HALF, D), (16, HALF)]
    normed_shape = shape_of((rows, D), BF)
    heads_shape = shape_of((3, rows, HALF), BF)
    heads_spec = pl.BlockSpec((3, LAT, HALF), lambda i: (0, i, 0))
    vector = kept_spec((1, D))
    bias_spec = whole_spec(small.shape)
    outs = pl.pallas_call(
        functools.partial(first_kernel, direct),
        grid=(images,),
        name="project_own",
        in_specs=[row_spec(D), vector, vector, bias_spec, whole_spec((3, D, HALF))]
        + ([ANY] * 5 if direct else []),
        out_specs=[row_spec(D), heads_spec] + ([ANY] * 5 if direct else []),
        out_shape=[normed_shape, heads_shape]
        + ([shape_of(s, BF) for s in w_shapes] if direct else []),
        scratch_shapes=[pltpu.SemaphoreType.DMA((5,))] * 2 if direct else [],
        compiler_params=params(collective_id=0, has_side_effects=True) if direct else params(),
        cost_estimate=cost(6 * rows * D * HALF, 12 * rows * D),
    )(
        latents,
        first_scale,
        first_shift,
        small,
        own[0],
        *((own + (small,)) if direct else ()),
    )
    normed_one, heads_own = outs[:2]
    if direct:
        others = outs[2:]
    w_in_other, w_out_other, w_up_other, w_down_other, small_other = others
    w_in_own, w_out_own, w_up_own, w_down_own = own

    half_spec = pl.BlockSpec((2, LAT, HALF), lambda i: (0, i, 0))
    half_shape = shape_of((2, rows, HALF), BF)
    head_count = HALF // HEAD
    probs_shape = shape_of((2, head_count, rows, LAT), BF)
    probs_spec = pl.BlockSpec((2, head_count, LAT, LAT), lambda i: (0, 0, i, 0))
    square = (HALF, D)
    tall = (D, HALF)
    parts = ((0, 384), (384, 768), (768, 1024))
    job = Reduction(HALF, D, parts, ORDERS) if direct else None
    result = shape_of(square, BF)
    (
        block_output,
        heads_other,
        probs,
        inverses,
        mixed,
        middle,
        slope,
        g_down,
        g_sum,
    ) = pl.pallas_call(
        forward_kernel,
        grid=(images,),
        name="forward",
        in_specs=[
            row_spec(D),
            row_spec(D),
            heads_spec,
            row_spec(D),
            whole_spec((3, D, HALF)),
            whole_spec(small_other.shape),
            whole_spec(square),
            whole_spec(square),
            vector,
            vector,
            vector,
            whole_spec(tall),
            whole_spec(tall),
            bias_spec,
            bias_spec,
            whole_spec(square),
            whole_spec(square),
            vector,
        ],
        out_specs=[
            row_spec(D),
            heads_spec,
            probs_spec,
            row_spec(HEAD),
            half_spec,
            row_spec(D),
            half_spec,
            kept_spec((2, HALF, D)),
            kept_spec((8, D)),
        ],
        out_shape=[
            shape_of((rows, D), F32),
            heads_shape,
            probs_shape,
            shape_of((rows, HEAD), F32),
            half_shape,
            shape_of((rows, D), BF),
            half_shape,
            shape_of((2, HALF, D), BF),
            shape_of((8, D), F32),
        ],
        scratch_shapes=[
            pltpu.VMEM((2, HALF, D), F32),
            pltpu.VMEM((LAT, D), BF),
            pltpu.VMEM((2, LAT, HALF), BF),
            pltpu.VMEM((LAT, D), F32),
        ],
        compiler_params=params(),
        cost_estimate=cost(16 * rows * D * D, 24 * rows * D),
    )(
        latents,
        normed_one,
        heads_own,
        output_grad,
        w_in_other,
        small_other,
        w_out_own,
        w_out_other,
        output_bias,
        second_scale,
        second_shift,
        w_up_own,
        w_up_other,
        small,
        small_other,
        w_down_own,
        w_down_other,
        down_bias,
    )

    d_middle, d_mixed, d_dots, g_up, g_out, vec_two, vec_up, *sums = pl.pallas_call(
        functools.partial(feed_back_kernel, job, FEED_PLACES),
        grid=(images,),
        name="feed_back",
        in_specs=[
            row_spec(D),
            half_spec,
            row_spec(D),
            half_spec,
            row_spec(HEAD),
            whole_spec(square),
            whole_spec(square),
            whole_spec(tall),
            whole_spec(tall),
            whole_spec(square),
            whole_spec(square),
            vector,
            vector,
        ]
        + ([ANY] if direct else []),
        out_specs=[
            row_spec(D),
            half_spec,
            row_spec(HEAD),
            kept_spec((2, HALF, D)),
            kept_spec((2, HALF, D)),
            kept_spec((3, 8, D)),
            kept_spec((2, 8, HALF)),
        ]
        + ([ANY] if direct else []),
        out_shape=[
            shape_of((rows, D), BF),
            half_shape,
            shape_of((rows, HEAD), F32),
            shape_of((2, HALF, D), BF),
            shape_of((2, HALF, D), BF),
            shape_of((3, 8, D), F32),
            shape_of((2, 8, HALF), F32),
        ]
        + ([result] if direct else []),
        scratch_shapes=[
            pltpu.VMEM((2, HALF, D), F32),
            pltpu.VMEM((2, HALF, D), F32),
            pltpu.VMEM((LAT, D), BF),
            pltpu.VMEM((LAT, D), F32),
            pltpu.VMEM((2, LAT, HALF), BF),
            pltpu.VMEM((LAT, D), F32),
        ]
        + (job.scratch() if direct else []),
        compiler_params=params(collective_id=1, has_side_effects=True) if direct else params(),
        cost_estimate=cost(10 * rows * D * D, 14 * rows * D),
    )(
        output_grad,
        slope,
        middle,
        mixed,
        inverses,
        w_down_own,
        w_down_other,
        w_up_own,
        w_up_other,
        w_out_own,
        w_out_other,
        second_scale,
        second_shift,
        *((g_down,) if direct else ()),
    )

    per_group = head_count // GROUPS
    width = per_group * HEAD
    group_heads = pl.BlockSpec((3, LAT, width), lambda g, i: (0, i, g))
    group_job = Reduction(
        D // 2, 3 * width, tuple((n * width, (n + 1) * width) for n in range(3)), ORDERS
    )
    group_result = shape_of((D, 3 * width), BF)
    jobs = [job, job, group_job, group_job] if direct else []
    d_heads, g_in, vec_in, *more = pl.pallas_call(
        functools.partial(attend_back_kernel, jobs, ATTEND_PLACES),
        grid=(GROUPS, images),
        name="attend_back",
        in_specs=[
            pl.BlockSpec((LAT, D), lambda g, i: (i, 0)),
            group_heads,
            group_heads,
            pl.BlockSpec((2, per_group, LAT, LAT), lambda g, i: (0, g, i, 0)),
            pl.BlockSpec((2, LAT, width), lambda g, i: (0, i, g)),
            pl.BlockSpec((LAT, HEAD), lambda g, i: (i, 0)),
        ]
        + ([ANY] * 2 if direct else []),
        out_specs=[
            pl.BlockSpec((2, 3, LAT, width), lambda g, i: (0, 0, i, g)),
            pl.BlockSpec(
                (None, 2, D, 3 * width), lambda g, i: (0 if direct else g, 0, 0, 0)
            ),
            pl.BlockSpec((None, 8, 6 * width), lambda g, i: (g, 0, 0)),
        ]
        + [ANY] * (3 if direct else 0),
        out_shape=[
            shape_of((2, 3, rows, HALF), BF),
            shape_of((1 if direct else GROUPS, 2, D, 3 * width), BF),
            shape_of((GROUPS, 8, 6 * width), F32),
        ]
        + ([result, result, group_result] if direct else []),
        scratch_shapes=[
            pltpu.VMEM((D, 6 * width), F32),
            pltpu.VMEM((LAT, 6 * width), BF),
            pltpu.VMEM((LAT, HEAD), F32),
        ]
        + ([pltpu.VMEM((D, 3 * width), BF)] if direct else [])
        + sum([one.scratch() for one in jobs], []),
        compiler_params=params(collective_id=2, has_side_effects=True) if direct else params(),
        cost_estimate=cost(8 * rows * D * D, 20 * rows * D),
    )(
        normed_one,
        heads_own,
        heads_other,
        probs,
        d_mixed,
        d_dots,
        *((g_up, g_out) if direct else ()),
    )

    late_shape = (2 * D // HEAD, HEAD)
    stages = 1 + len(SHIFTS)

    def vector_scratch(shape):
        return [
            pltpu.VMEM((stages + 1,) + shape, F32),
            pltpu.VMEM((stages, 3) + shape, F32),
            pltpu.SemaphoreType.DMA((stages, 3)),
            pltpu.SemaphoreType.DMA((stages, 3)),
        ]

    grad_low, vectors, late, *last = pl.pallas_call(
        functools.partial(
            last_kernel, group_job if direct else None, LAST_PLACES, factor
        ),
        grid=(images,),
        name="input_back",
        in_specs=[
            row_spec(D),
            pl.BlockSpec((2, 3, LAT, HALF), lambda i: (0, 0, i, 0)),
            row_spec(D),
            whole_spec((3, D, HALF)),
            whole_spec((3, D, HALF)),
            vector,
            kept_spec((3, 8, D)),
            kept_spec((8, D)),
            kept_spec((2, 8, HALF)),
            kept_spec((GROUPS, 8, 6 * width)),
        ]
        + ([ANY] if direct else []),
        out_specs=[row_spec(D), kept_spec((8, D)), kept_spec(late_shape)]
        + ([ANY] if direct else []),
        out_shape=[shape_of((rows, D), BF), shape_of((8, D), F32), shape_of(late_shape, F32)]
        + ([group_result] if direct else []),
        scratch_shapes=[pltpu.VMEM((LAT, D), F32), pltpu.VMEM((2, 8, D), F32)]
        + (
            vector_scratch((8, D))
            + vector_scratch(late_shape)
            + group_job.scratch() * 2
            if direct
            else []
        ),
        compiler_params=params(collective_id=3, has_side_effects=True) if direct else params(),
        cost_estimate=cost(6 * rows * D * D, 14 * rows * D),
    )(
        latents,
        d_heads,
        d_middle,
        w_in_own,
        w_in_other,
        first_scale,
        vec_two,
        g_sum,
        vec_up,
        vec_in,
        *((g_in.reshape(2, D, 3 * width),) if direct else ()),
    )

    pieces = 8
    vector_shapes = [(1, D)] * 6 + [(2, HALF), (1, HALF)]
    cut = rows // pieces
    if direct:
        latents_grad, g_down, g_up, g_out, g_in, *vectors = pl.pallas_call(
            functools.partial(finish_kernel, factor),
            grid=(pieces,),
            name="finish",
            in_specs=[
                pl.BlockSpec((cut, D), lambda i: (i, 0)),
                pl.BlockSpec((HALF // pieces, D), lambda i: (i, 0)),
                pl.BlockSpec((HALF, D // pieces), lambda i: (0, i)),
                pl.BlockSpec((HALF // pieces, D), lambda i: (i, 0)),
                pl.BlockSpec((D // pieces, 3 * width), lambda i: (i, 0)),
                pl.BlockSpec((D // pieces, 3 * width), lambda i: (i, 0)),
                kept_spec((8, D)),
                kept_spec(late_shape),
            ],
            out_specs=[
                pl.BlockSpec((cut, D), lambda i: (i, 0)),
                pl.BlockSpec((HALF // pieces, D), lambda i: (i, 0)),
                pl.BlockSpec((D // pieces, HALF), lambda i: (i, 0)),
                pl.BlockSpec((HALF // pieces, D), lambda i: (i, 0)),
                pl.BlockSpec((3, D // pieces, HALF), lambda i: (0, i, 0)),
            ]
            + [kept_spec(shape) for shape in vector_shapes],
            out_shape=[
                shape_of((rows, D), F32),
                shape_of((HALF, D), F32),
                shape_of((D, HALF), F32),
                shape_of((HALF, D), F32),
                shape_of((3, D, HALF), F32),
            ]
            + [shape_of(shape, F32) for shape in vector_shapes],
            compiler_params=params(),
        )(grad_low, sums[0], more[0], more[1], more[2], last[0], vectors, late)
        in_bias, up_grad = vectors[6], vectors[7].reshape(HALF)
        late = [v.reshape(D) for v in vectors[4:6]]
        vectors = [v.reshape(D) for v in vectors[:4]]
    else:
        latents_grad = pl.pallas_call(
            functools.partial(finish_kernel, factor),
            grid=(pieces,),
            name="finish",
            in_specs=[pl.BlockSpec((cut, D), lambda i: (i, 0))],
            out_specs=pl.BlockSpec((cut, D), lambda i: (i, 0)),
            out_shape=shape_of((rows, D), F32),
            compiler_params=params(),
        )(grad_low)
        vectors = lax.psum(vectors, ("dp", "mp")) * factor
        late = lax.psum(late, ("dp", "mp")) * factor
        own_width = D // mp
        mine = lax.dynamic_slice_in_dim(
            vectors[4:7], lax.axis_index("mp") * own_width, own_width, 1
        )
        in_bias, up_grad, late = mine[:2], mine[2], late.reshape(2, D)
        g_down, g_up, g_out = (v.reshape(D, D) for v in (g_down, g_up, g_out))
        g_in = jnp.transpose(g_in.reshape(GROUPS, 2, D, 3, width), (3, 2, 1, 0, 4))
        g_in = g_in.reshape(3, D, D)

        def scatter(v, axis):
            v = lax.psum_scatter(v, "mp", scatter_dimension=axis, tiled=True)
            return lax.psum(v, "dp").astype(F32) * factor

        g_down, g_up, g_out = scatter(g_down, 0), scatter(g_up.T, 1), scatter(g_out, 0)
        g_in = scatter(g_in, 2)

    return (
        block_output,
        latents_grad,
        late[0],
        late[1],
        g_in,
        in_bias,
        g_out,
        vectors[0],
        vectors[1],
        vectors[2],
        g_up,
        up_grad,
        g_down,
        vectors[3],
    )


def solution(mesh):
    return jax.shard_map(
        per_device,
        mesh=mesh,
        in_specs=(
            P(("dp", "mp"), None),
            P(),
            P(),
            P(None, None, "mp"),
            P(None, "mp"),
            P("mp", None),
            P(),
            P(),
            P(),
            P(None, "mp"),
            P("mp"),
            P("mp", None),
            P(),
            P(("dp", "mp"), None),
        ),
        out_specs=(
            P(("dp", "mp"), None),
            P(("dp", "mp"), None),
            P(),
            P(),
            P(None, None, "mp"),
            P(None, "mp"),
            P("mp", None),
            P(),
            P(),
            P(),
            P(None, "mp"),
            P("mp"),
            P("mp", None),
            P(),
        ),
        check_vma=False,
    )
```

```python
import functools

import jax
import jax.numpy as jnp
from jax import lax
from jax.experimental import pallas as pl
from jax.experimental.pallas import tpu as pltpu
from jax.sharding import PartitionSpec as P

D = 1024
HEAD = 128
HEADS = 8
LAT = 512
HALF = 512
GROUPS = 2
EPS = 1e-05
SCALE = HEAD ** (-0.5)
LOG2E = 1.4426950408889634
GELU_A = 0.7978845608028654
GELU_B = 0.044715
MESH = pl.DeviceIdType.MESH
NN = (((1,), (0,)), ((), ()))
NT = (((1,), (1,)), ((), ()))
TN = (((0,), (0,)), ((), ()))
BF = jnp.bfloat16
F32 = jnp.float32
VMEM_LIMIT = 60 << 20


def mul(a, b, dims):
    return lax.dot_general(a, b, dims, preferred_element_type=F32)


def unit_of(rows):
    centred = rows - jnp.mean(rows, axis=-1, keepdims=True)
    inverse = lax.rsqrt(jnp.mean(centred * centred, axis=-1, keepdims=True) + EPS)
    return centred * inverse, inverse


def norm_back(upstream, unit, inverse, gain):
    scaled = upstream * gain
    inner = (
        scaled
        - jnp.mean(scaled, axis=-1, keepdims=True)
        - unit * jnp.mean(scaled * unit, axis=-1, keepdims=True)
    )
    return inverse * inner


def column_sum(values):
    return jnp.sum(values.reshape(values.shape[0] // 8, 8, values.shape[1]), axis=0)


def row_spec(width):
    return pl.BlockSpec((LAT, width), lambda i: (i, 0))


def whole_spec(shape):
    return pl.BlockSpec(shape, lambda *_: (0,) * len(shape), pipeline_mode=pl.Buffered(1))


def kept_spec(shape):
    return pl.BlockSpec(shape, lambda *_: (0,) * len(shape))


ANY = pl.BlockSpec(memory_space=pl.ANY)


def shape_of(shape, dtype):
    return jax.ShapeDtypeStruct(shape, dtype)


def cost(flops, moved):
    return pl.CostEstimate(flops=int(flops), bytes_accessed=int(moved), transcendentals=0)


def flipped(place, other):
    for bit in (1, 2):
        if other & bit:
            place = place + bit - 2 * bit * lax.rem(place // bit, 2)
    return place


def dp_flip(shift, other):
    me = lax.axis_index("dp")
    place = lax.rem(me // (1 << shift), 4)
    return (me + (flipped(place, other) - place) * (1 << shift), lax.axis_index("mp"))


def start(copies):
    for copy in copies:
        copy.start()


def wait(copies):
    for copy in copies:
        copy.wait()


def core_flip():
    return (lax.axis_index("dp"), 1 - lax.axis_index("mp"))


def greet(partners):
    barrier = pltpu.get_barrier_semaphore()
    for partner in partners:
        pl.semaphore_signal(barrier, inc=1, device_id=partner, device_id_type=MESH)
    pl.semaphore_wait(barrier, len(partners))


def remote(src, dst, send, recv, partner):
    return pltpu.make_async_remote_copy(
        src_ref=src,
        dst_ref=dst,
        send_sem=send,
        recv_sem=recv,
        device_id=partner,
        device_id_type=MESH,
    )


class Reduction:
    def __init__(self, rows, columns, parts, orders):
        self.rows, self.columns, self.parts, self.orders = rows, columns, parts, orders
        self.stages = len(orders[0])
        self.ticks = 2 * self.stages + 2

    def scratch(self):
        copies = (len(self.parts), 2 * self.stages, 3)
        return [
            pltpu.VMEM((self.rows, self.columns), BF),
            pltpu.VMEM((self.rows, self.columns), BF),
            pltpu.VMEM((self.rows, self.columns), BF),
            pltpu.SemaphoreType.DMA((2,)),
            pltpu.SemaphoreType.DMA(copies),
            pltpu.SemaphoreType.DMA(copies),
            pltpu.SemaphoreType.DMA((2,)),
        ]

    def place(self, part, stage):
        shift, members = self.orders[part][stage]
        return lax.rem(lax.axis_index("dp") // (1 << shift), members)

    def size(self, stage):
        rows = self.rows
        for _, members in self.orders[0][: stage + 1]:
            rows //= members
        return rows

    def others(self, stage):
        return (1,) if self.orders[0][stage][1] == 2 else (3, 1, 2)

    def offset(self, part, level):
        row = 0
        for stage in range(level):
            row = row + self.place(part, stage) * self.size(stage)
        return row

    def aligned(self, row, size):
        return pl.ds(pl.multiple_of(row, size), size)

    def columns_of(self, part):
        first, last = self.parts[part]
        return pl.ds(first, last - first)

    def partner(self, part, stage, other):
        return dp_flip(self.orders[part][stage][0], other)

    def landing(self, stage, other):
        size = self.size(stage)
        first = self.rows - self.orders[0][stage][1] * size
        return pl.ds(first + (other - 1) * size, size)

    def adding(self, refs, part, stage):
        cur, _, recv, _, send_sem, recv_sem = refs[:6]
        size = self.size(stage)
        base, cols = self.offset(part, stage), self.columns_of(part)
        copies = []
        for other in self.others(stage):
            theirs = flipped(self.place(part, stage), other)
            copies.append(
                remote(
                    cur.at[self.aligned(base + theirs * size, size), cols],
                    recv.at[self.landing(stage, other), cols],
                    send_sem.at[part, stage, other - 1],
                    recv_sem.at[part, stage, other - 1],
                    self.partner(part, stage, other),
                )
            )
        return copies

    def handing(self, refs, part, step):
        _, full, _, _, send_sem, recv_sem = refs[:6]
        stage = self.stages - 1 - step
        size = self.size(stage)
        rows, cols = self.aligned(self.offset(part, stage + 1), size), self.columns_of(part)
        return [
            remote(
                full.at[rows, cols],
                full.at[rows, cols],
                send_sem.at[part, self.stages + step, other - 1],
                recv_sem.at[part, self.stages + step, other - 1],
                self.partner(part, stage, other),
            )
            for other in self.others(stage)
        ]

    def exchange(self, refs, other):
        return remote(other, refs[1], refs[3].at[0], refs[3].at[1], core_flip())

    def tick(self, refs, tick, other):
        cur, landed, recv = refs[:3]
        parts = range(len(self.parts))
        if tick == 0:
            self.exchange(refs, other).start()
            return
        if tick == 1:
            self.exchange(refs, other).wait()
            cur[...] = (cur[...].astype(F32) + landed[...].astype(F32)).astype(BF)
            for part in parts:
                start(self.adding(refs, part, 0))
            return
        if tick <= self.stages + 1:
            stage = tick - 2
            for part in parts:
                wait(self.adding(refs, part, stage))
                size = self.size(stage)
                keep, cols = self.aligned(self.offset(part, stage + 1), size), self.columns_of(part)
                total = cur[keep, cols].astype(F32)
                for other in sorted(self.others(stage)):
                    total = total + recv[self.landing(stage, other), cols].astype(F32)
                if stage + 1 < self.stages:
                    cur[keep, cols] = total.astype(BF)
                    start(self.adding(refs, part, stage + 1))
                else:
                    landed[keep, cols] = total.astype(BF)
                    start(self.handing(refs, part, 0))
            return
        step = tick - self.stages - 2
        for part in parts:
            wait(self.handing(refs, part, step))
            if step + 1 < self.stages:
                start(self.handing(refs, part, step + 1))


class Task:
    def __init__(self, job, refs, source, result, places, staged=False, piece=0):
        self.job, self.refs, self.places, self.staged = job, refs, places, staged
        window = pl.ds(piece * job.rows, job.rows)
        self.own = None if staged else source.at[0, window]
        self.other = source.at[window] if staged else source.at[1, window]
        self.result = result.at[window]

    def load(self):
        return pltpu.make_async_copy(self.own, self.refs[0], self.refs[6].at[0])

    def store(self):
        return pltpu.make_async_copy(self.refs[1], self.result, self.refs[6].at[1])

    def run(self, tick):
        if tick == 0 and not self.staged:
            self.load().start()
        if tick == 1 and not self.staged:
            self.load().wait()
        self.job.tick(self.refs, tick, self.other)
        if tick == self.job.ticks - 1:
            self.store().start()

    def finish(self):
        self.store().wait()


def run_tasks(step, place, tasks):
    for now in sorted({at[0] for task in tasks for at in task.places if at[1] == place}):

        @pl.when(step == now)
        def _():
            for task in tasks:
                for tick, at in enumerate(task.places):
                    if at == (now, place):
                        task.run(tick)


ORDERS = (((0, 2), (1, 2), (2, 4)), ((1, 2), (0, 2), (2, 4)), ((2, 2), (3, 2), (0, 4)))
SHIFTS = (0, 2)


def starts(steps, *numbers):
    return tuple((n, 0) if n < steps else (steps - 1, 1) for n in numbers)


FEED_PLACES = starts(8, 0, 1, 2, 3, 4, 5, 6, 7)
ATTEND_PLACES = (
    starts(16, 0, 1, 3, 5, 7, 9, 11, 13),
    starts(16, 1, 2, 4, 6, 8, 10, 12, 15),
    ((7, 1),) + starts(16, 9, 10, 11, 12, 13, 14, 16),
    ((7, 1),) + starts(16, 10, 11, 12, 13, 14, 15, 16),
)
LAST_PLACES = (starts(8, 0, 1, 2, 3, 5, 6, 7, 8),) * 2
VECTOR_PLACES = starts(8, 1, 2, 4, 6)


def reduction_partners():
    return [core_flip()] + [dp_flip(shift, other) for shift in SHIFTS for other in (1, 2, 3)]


def first_kernel(
    spread, x_ref, gain_ref, shift_ref, bias_ref, w_in, *refs
):
    step = pl.program_id(0)
    if spread:
        sources = (w_in_any, w_out, w_up, w_down, bias_all) = refs[:5]
        normed_ref, heads_ref = refs[5:7]
        targets = refs[7:12]
        send_sem, recv_sem = refs[12:14]

        def copies():
            return [
                remote(src, dst, send_sem.at[n], recv_sem.at[n], core_flip())
                for n, (src, dst) in enumerate(zip(sources, targets))
            ]

        @pl.when(step == 0)
        def _():
            greet([core_flip()])
            for copy in copies():
                copy.start()
    else:
        normed_ref, heads_ref = refs

    for piece in range(2):
        rows = slice(piece * 256, (piece + 1) * 256)
        unit, _ = unit_of(x_ref[rows, :].astype(F32))
        normed_ref[rows, :] = (unit * gain_ref[...] + shift_ref[...]).astype(BF)
        project(normed_ref, w_in, bias_ref, heads_ref, rows)

    if spread:

        @pl.when(step == pl.num_programs(0) - 1)
        def _():
            for copy in copies():
                copy.wait()


def project(normed_ref, weights, bias_ref, heads_ref, rows=slice(0, LAT)):
    for which in range(3):
        heads = mul(normed_ref[rows, :], weights[which], NN)
        if which != 1:
            place = 0 if which == 0 else 1
            heads = heads + bias_ref[place : place + 1, :].astype(F32)
        heads_ref[which, rows, :] = heads.astype(BF)


def forward_kernel(
    x_ref,
    normed_ref,
    own_ref,
    g_ref,
    w_in,
    in_bias,
    wo_own,
    wo_other,
    out_bias,
    gain_ref,
    shift_ref,
    wu_own,
    wu_other,
    ub_own,
    ub_other,
    wd_own,
    wd_other,
    down_bias,
    block_ref,
    other_ref,
    probs_ref,
    inv_ref,
    mixed_ref,
    middle_ref,
    slope_ref,
    gdown_ref,
    gsum_ref,
    acc,
    normed_two,
    act,
    wide,
):
    step = pl.program_id(0)

    @pl.when(step == 0)
    def _():
        acc[...] = jnp.zeros_like(acc)
        gsum_ref[...] = jnp.zeros_like(gsum_ref)

    project(normed_ref, w_in, in_bias, other_ref)
    lane = lax.broadcasted_iota(jnp.int32, (LAT, HEAD), 1)
    ones = jnp.ones((LAT, HEAD), BF)
    inverses = jnp.zeros((LAT, HEAD), F32)
    for half, heads_ref in enumerate((own_ref, other_ref)):
        for head in range(HALF // HEAD):
            cols = slice(head * HEAD, (head + 1) * HEAD)
            scores = mul(heads_ref[0, :, cols], heads_ref[1, :, cols], NT)
            highest = jnp.max(scores, axis=-1, keepdims=True)
            powers = jnp.exp2((scores - highest) * (SCALE * LOG2E))
            low = powers.astype(BF)
            probs_ref[half, head] = low
            both = mul(low, jnp.concatenate([heads_ref[2, :, cols], ones], axis=1), NN)
            inverse = 1.0 / both[:, HEAD:]
            mixed_ref[half, :, cols] = (both[:, :HEAD] * inverse).astype(BF)
            inverses = jnp.where(lane == half * 4 + head, inverse, inverses)
    inv_ref[...] = inverses
    for chunk in range(4):
        cols = slice(chunk * 256, (chunk + 1) * 256)
        wide[:, cols] = (
            x_ref[:, cols].astype(F32)
            + mul(mixed_ref[0], wo_own[:, cols], NN)
            + mul(mixed_ref[1], wo_other[:, cols], NN)
            + out_bias[:, cols]
        )
    middle = wide[...]
    middle_ref[...] = middle.astype(BF)
    unit, _ = unit_of(middle)
    normed_two[...] = (unit * gain_ref[...] + shift_ref[...]).astype(BF)
    for half, (weight, bias) in enumerate(((wu_own, ub_own), (wu_other, ub_other))):
        for chunk in range(2):
            cols = slice(chunk * 256, (chunk + 1) * 256)
            hidden = mul(normed_two[...], weight[:, cols], NN) + bias[2:3, cols].astype(F32)
            square = hidden * hidden
            gate = jnp.tanh(GELU_A * (hidden + GELU_B * (square * hidden)))
            lift = 0.5 * (1.0 + gate)
            act[half, :, cols] = (hidden * lift).astype(BF)
            slope = lift + (0.5 * GELU_A) * hidden * (1.0 - gate * gate) * (
                1.0 + (3.0 * GELU_B) * square
            )
            slope_ref[half, :, cols] = slope.astype(BF)
    for chunk in range(4):
        cols = slice(chunk * 256, (chunk + 1) * 256)
        block_ref[:, cols] = (
            wide[:, cols]
            + mul(act[0], wd_own[:, cols], NN)
            + mul(act[1], wd_other[:, cols], NN)
            + down_bias[:, cols]
        )
    for half in range(2):
        acc[half] += mul(act[half], g_ref[...], TN)
    gsum_ref[...] += column_sum(g_ref[...].astype(F32))

    @pl.when(step == pl.num_programs(0) - 1)
    def _():
        gdown_ref[...] = acc[...].astype(BF)


def feed_back_kernel(
    job,
    places,
    g_ref,
    slope_ref,
    middle_ref,
    mixed_ref,
    inv_ref,
    wd_own,
    wd_other,
    wu_own,
    wu_other,
    wo_own,
    wo_other,
    gain_ref,
    shift_ref,
    *refs,
):
    tasks = []
    if job is not None:
        source, refs = refs[0], refs[1:]
    outs, refs = refs[:7], refs[7:]
    if job is not None:
        result, refs = refs[0], refs[1:]
    dmid_ref, dmix_ref, dot_ref, gup_ref, gout_ref, vec_ref, ubias_ref = outs
    acc_up, acc_out, normed_two, unit_ref, dhid, wide = refs[:6]
    if job is not None:
        tasks.append(Task(job, refs[6:], source, result, places))
    step = pl.program_id(0)

    @pl.when(step == 0)
    def _():
        if tasks:
            greet(reduction_partners())
        acc_up[...] = jnp.zeros_like(acc_up)
        acc_out[...] = jnp.zeros_like(acc_out)
        vec_ref[...] = jnp.zeros_like(vec_ref)
        ubias_ref[...] = jnp.zeros_like(ubias_ref)

    run_tasks(step, 0, tasks)
    lane = lax.broadcasted_iota(jnp.int32, (256, HEAD), 1)
    for piece in range(2):
        rows = slice(piece * 256, (piece + 1) * 256)
        for half, weight in enumerate((wd_own, wd_other)):
            for chunk in range(2):
                cols = slice(chunk * 256, (chunk + 1) * 256)
                down = mul(g_ref[rows, :], weight[cols, :], NT)
                dhid[half, rows, cols] = (down * slope_ref[half, rows, cols].astype(F32)).astype(BF)
            ubias_ref[half] += column_sum(dhid[half, rows].astype(F32))
        unit, inverse = unit_of(middle_ref[rows, :].astype(F32))
        unit_ref[rows, :] = unit
        normed_two[rows, :] = (unit * gain_ref[...] + shift_ref[...]).astype(BF)
        for chunk in range(4):
            cols = slice(chunk * 256, (chunk + 1) * 256)
            wide[rows, cols] = mul(dhid[0, rows], wu_own[cols, :], NT) + mul(
                dhid[1, rows], wu_other[cols, :], NT
            )
        upstream = wide[rows, :]
        unit = unit_ref[rows, :]
        vec_ref[0] += column_sum(upstream * unit)
        vec_ref[1] += column_sum(upstream)
        dmid = g_ref[rows, :].astype(F32) + norm_back(upstream, unit, inverse, gain_ref[...])
        vec_ref[2] += column_sum(dmid)
        dmid_ref[rows, :] = dmid.astype(BF)
    for half in range(2):
        acc_up[half] += mul(dhid[half], normed_two[...], TN)
    for half in range(2):
        acc_out[half] += mul(mixed_ref[half], dmid_ref[...], TN)
    for piece in range(2):
        rows = slice(piece * 256, (piece + 1) * 256)
        dots = jnp.zeros((256, HEAD), F32)
        for half, weight in enumerate((wo_own, wo_other)):
            for pair in range(2):
                both = mul(dmid_ref[rows, :], weight[pair * 256 : (pair + 1) * 256, :], NT)
                for one in range(2):
                    head = pair * 2 + one
                    cols = slice(head * HEAD, (head + 1) * HEAD)
                    place = half * 4 + head
                    scaled = both[:, one * HEAD : (one + 1) * HEAD] * inv_ref[rows, place : place + 1]
                    dmix_ref[half, rows, cols] = scaled.astype(BF)
                    total = jnp.sum(
                        scaled * mixed_ref[half, rows, cols].astype(F32), axis=-1, keepdims=True
                    )
                    dots = jnp.where(lane == place, total, dots)
        dot_ref[rows, :] = dots

    @pl.when(step == pl.num_programs(0) - 1)
    def _():
        gup_ref[...] = acc_up[...].astype(BF)
        gout_ref[...] = acc_out[...].astype(BF)
        for task in tasks:
            task.finish()


def attend_back_kernel(
    jobs,
    places,
    normed_ref,
    own_ref,
    other_ref,
    probs_ref,
    dmix_ref,
    dot_ref,
    *refs,
):
    tasks, count = [], len(jobs)
    if jobs:
        sources, refs = refs[: count - 2], refs[count - 2 :]
    dheads_ref, gin_ref, vec_ref = refs[:3]
    refs = refs[3:]
    if jobs:
        results, refs = refs[: count - 1], refs[count - 1 :]
    acc, joined, dots_now = refs[:3]
    if jobs:
        staged, refs = refs[3], refs[4:]
        for n, job in enumerate(jobs):
            mine = refs[7 * n : 7 * n + 7]
            if n < count - 2:
                tasks.append(Task(job, mine, sources[n], results[n], places[n]))
            else:
                piece = n - (count - 2)
                tasks.append(Task(job, mine, staged, results[-1], places[n], True, piece))
    group, step = pl.program_id(0), pl.program_id(1)
    now = group * pl.num_programs(1) + step
    per_group = HALF // HEAD // GROUPS
    width = per_group * HEAD

    if tasks:

        @pl.when(now == 0)
        def _():
            greet(reduction_partners())

    @pl.when(step == 0)
    def _():
        acc[...] = jnp.zeros_like(acc)
        vec_ref[...] = jnp.zeros_like(vec_ref)

    @pl.when(group == 0)
    def _():
        for place in range(4):
            lane = (place // 2) * 4 + place % 2
            dots_now[:, place : place + 1] = dot_ref[:, lane : lane + 1]

    @pl.when(group == 1)
    def _():
        for place in range(4):
            lane = (place // 2) * 4 + 2 + place % 2
            dots_now[:, place : place + 1] = dot_ref[:, lane : lane + 1]

    run_tasks(now, 0, tasks)
    for half, heads_ref in enumerate((own_ref, other_ref)):
        for head in range(per_group):
            cols = slice(head * HEAD, (head + 1) * HEAD)
            place = half * per_group + head
            probs = probs_ref[half, head]
            upstream = dmix_ref[half, :, cols]
            d_probs = mul(upstream, heads_ref[2, :, cols], NT) - dots_now[:, place : place + 1]
            d_scores = (probs.astype(F32) * d_probs).astype(BF)
            d_query = (mul(d_scores, heads_ref[1, :, cols], NN) * SCALE).astype(BF)
            d_keys = (mul(heads_ref[0, :, cols], d_scores, TN) * SCALE).T.astype(BF)
            d_values = mul(upstream, probs, TN).T.astype(BF)
            for which, value in enumerate((d_query, d_keys, d_values)):
                dheads_ref[half, which, :, cols] = value
                first = half * 3 * width + which * width + head * HEAD
                joined[:, first : first + HEAD] = value
    vec_ref[...] += column_sum(joined[...].astype(F32))
    for chunk in range(4):
        rows = slice(chunk * 256, (chunk + 1) * 256)
        acc[rows, :] += mul(normed_ref[:, rows], joined[...], TN)

    @pl.when((now if tasks else step) == pl.num_programs(1) * (GROUPS if tasks else 1) - 1)
    def _():
        for half in range(2):
            cols = slice(half * 3 * width, (half + 1) * 3 * width)
            gin_ref[half] = acc[:, cols].astype(BF)

    if tasks:

        @pl.when(now == pl.num_programs(1) - 1)
        def _():
            for piece in range(2):
                rows = slice(piece * D // 2, (piece + 1) * D // 2)
                tasks[piece - 2].refs[0][...] = acc[rows, : 3 * width].astype(BF)
            staged[...] = acc[:, 3 * width :].astype(BF)

    run_tasks(now, 1, tasks)

    if tasks:

        @pl.when(now == pl.num_programs(0) * pl.num_programs(1) - 1)
        def _():
            for task in tasks:
                task.finish()


def total_row(v):
    return jnp.sum(v, axis=0, keepdims=True)


def pack_vectors(two_ref, sum_ref, up_ref, in_ref, out_ref):
    width = HALF // GROUPS
    out_ref[...] = jnp.zeros_like(out_ref)
    out_ref[0:1, :] = total_row(two_ref[2])
    out_ref[1:2, :] = total_row(two_ref[0])
    out_ref[2:3, :] = total_row(two_ref[1])
    out_ref[3:4, :] = total_row(sum_ref[...])
    for half in range(2):
        for group in range(GROUPS):
            cols = slice(half * HALF + group * width, half * HALF + (group + 1) * width)
            for row, which in ((4, 0), (5, 2)):
                first = (half * 3 + which) * width
                out_ref[row : row + 1, cols] = total_row(in_ref[group, :, first : first + width])
        out_ref[6:7, half * HALF : (half + 1) * HALF] = total_row(up_ref[half])


def pack_late(vec_ref, out_ref):
    for which in range(2):
        row = total_row(vec_ref[which])
        for n in range(D // HEAD):
            place = which * (D // HEAD) + n
            out_ref[place : place + 1, :] = row[:, n * HEAD : (n + 1) * HEAD]


class VectorTask:
    def __init__(self, refs, whole, places=(), pack=None, done=None):
        self.held, self.landed, self.send_sem, self.recv_sem = refs
        self.whole, self.places, self.pack, self.done = whole, places, pack, done

    def copies(self, stage):
        groups = [[core_flip()]] + [[dp_flip(shift, n) for n in (1, 2, 3)] for shift in SHIFTS]
        return [
            remote(
                self.held.at[stage],
                self.landed.at[stage, n],
                self.send_sem.at[stage, n],
                self.recv_sem.at[stage, n],
                partner,
            )
            for n, partner in enumerate(groups[stage])
        ]

    def add(self, stage):
        held, landed = self.held, self.landed
        if stage > 0:
            held[stage + 1] = (held[stage] + landed[stage, 0]) + (
                landed[stage, 1] + landed[stage, 2]
            )
            return
        got = landed[0, 0]
        if self.whole < got.shape[0]:
            crossed = jnp.concatenate([got[:, HALF:], got[:, :HALF]], axis=1)
            row = lax.broadcasted_iota(jnp.int32, got.shape, 0)
            got = jnp.where(row < self.whole, got, crossed)
        held[1] = held[0] + got

    def run(self, tick):
        if tick == 0:
            self.pack()
        else:
            wait(self.copies(tick - 1))
            self.add(tick - 1)
        if tick <= len(SHIFTS):
            start(self.copies(tick))
        else:
            self.done()

    def finish(self):
        pass


def last_kernel(
    job,
    places,
    factor,
    x_ref,
    dheads_ref,
    dmid_ref,
    w_own,
    w_other,
    gain_ref,
    two_ref,
    sum_ref,
    up_ref,
    in_ref,
    *refs,
):
    tasks = []
    if job is not None:
        source, refs = refs[0], refs[1:]
    (grad_ref, total_ref, late_ref), refs = refs[:3], refs[3:]
    if job is not None:
        result, refs = refs[0], refs[1:]
    (wide, vec_ref), refs = refs[:2], refs[2:]
    if job is not None:
        early, late, refs = refs[:4], refs[4:8], refs[8:]
        for piece in range(2):
            mine = refs[7 * piece : 7 * piece + 7]
            tasks.append(Task(job, mine, source, result, places[piece], piece=piece))

        def pack():
            pack_vectors(two_ref, sum_ref, up_ref, in_ref, early[0].at[0])

        def done():
            total_ref[...] = early[0][1 + len(SHIFTS)] * factor

        tasks.append(VectorTask(early, 4, VECTOR_PLACES, pack, done))
    step = pl.program_id(0)
    last = pl.num_programs(0) - 1

    @pl.when(step == 0)
    def _():
        if tasks:
            greet(reduction_partners())
        vec_ref[...] = jnp.zeros_like(vec_ref)

    run_tasks(step, 0, tasks)
    for piece in range(2):
        take = slice(piece * 256, (piece + 1) * 256)
        for chunk in range(4):
            rows = slice(chunk * 256, (chunk + 1) * 256)
            total = None
            for half, weight in enumerate((w_own, w_other)):
                for which in range(3):
                    term = mul(dheads_ref[half, which, take], weight[which, rows, :], NT)
                    total = term if total is None else total + term
            wide[take, rows] = total
        unit, inverse = unit_of(x_ref[take, :].astype(F32))
        upstream = wide[take, :]
        vec_ref[0] += column_sum(upstream * unit)
        vec_ref[1] += column_sum(upstream)
        grad = dmid_ref[take, :].astype(F32) + norm_back(upstream, unit, inverse, gain_ref[...])
        grad_ref[take, :] = grad.astype(BF)

    if tasks:

        def pack_last():
            pack_late(vec_ref, late[0].at[0])

        def done_last():
            late_ref[...] = late[0][1 + len(SHIFTS)] * factor

        final = VectorTask(late, 2 * D // HEAD, (), pack_last, done_last)

        @pl.when(step == last)
        def _():
            final.run(0)

    run_tasks(step, 1, tasks)

    @pl.when(step == last)
    def _():
        if tasks:
            for tick in range(1, 2 + len(SHIFTS)):
                final.run(tick)
        else:
            pack_vectors(two_ref, sum_ref, up_ref, in_ref, total_ref)
            pack_late(vec_ref, late_ref)
        for task in tasks:
            task.finish()


def finish_kernel(factor, lat_ref, *refs):
    if len(refs) > 1:
        down_in, up_in, out_in, in_a, in_b, total_ref, late_ref = refs[:7]
        lat_out, down_out, up_out, out_out, in_out = refs[7:12]
        rows, late_rows = refs[12:16], refs[16:18]
        in_bias_out, up_bias_out = refs[18:]
        width = HALF // GROUPS
        down_out[...] = down_in[...].astype(F32) * factor
        out_out[...] = out_in[...].astype(F32) * factor
        up_out[...] = up_in[...].astype(F32).T * factor
        for which in range(3):
            for group, part in enumerate((in_a, in_b)):
                in_out[which, :, group * width : (group + 1) * width] = (
                    part[:, which * width : (which + 1) * width].astype(F32) * factor
                )

        @pl.when(pl.program_id(0) == 0)
        def _():
            for n, row in enumerate(rows):
                row[...] = total_ref[n : n + 1, :]
            for which, row in enumerate(late_rows):
                for n in range(D // HEAD):
                    place = which * (D // HEAD) + n
                    row[:, n * HEAD : (n + 1) * HEAD] = late_ref[place : place + 1, :]
            in_bias_out[...] = total_ref[4:6, :HALF]
            up_bias_out[...] = total_ref[6:7, :HALF]

    else:
        (lat_out,) = refs
    lat_out[...] = lat_ref[...].astype(F32)


def params(**more):
    return pltpu.CompilerParams(vmem_limit_bytes=VMEM_LIMIT, **more)


def per_device(
    latents,
    first_scale,
    first_shift,
    input_weights,
    input_bias,
    output_weight,
    output_bias,
    second_scale,
    second_shift,
    up_weight,
    up_bias,
    down_weight,
    down_bias,
    output_grad,
):
    rows = latents.shape[0]
    images = rows // LAT
    dp, mp = lax.axis_size("dp"), lax.axis_size("mp")
    direct = dp == 16 and mp == 2
    factor = LAT / (rows * dp * mp)
    row = lambda v: v[None, :]
    first_scale, first_shift = row(first_scale), row(first_shift)
    second_scale, second_shift = row(second_scale), row(second_shift)
    output_bias, down_bias = row(output_bias), row(down_bias)

    if direct:
        own = (input_weights, output_weight, up_weight, down_weight)
        small = jnp.concatenate(
            [input_bias, up_bias[None], jnp.zeros((13, HALF), BF)], axis=0
        )
    else:
        gather = lambda v, axis: lax.all_gather(v, "mp", axis=axis, tiled=True)
        w_in, w_out = gather(input_weights, 2), gather(output_weight, 0)
        w_up, w_down = gather(up_weight, 1), gather(down_weight, 0)
        small = jnp.concatenate([gather(input_bias, 1), gather(up_bias, 0)[None]], axis=0)
        own = (w_in[..., :HALF], w_out[:HALF], w_up[:, :HALF], w_down[:HALF])
        others = (w_in[..., HALF:], w_out[HALF:], w_up[:, HALF:], w_down[HALF:], small[:, HALF:])
        small = small[:, :HALF]

    w_shapes = [(3, D, HALF), (HALF, D), (D, HALF), (HALF, D), (16, HALF)]
    normed_shape = shape_of((rows, D), BF)
    heads_shape = shape_of((3, rows, HALF), BF)
    heads_spec = pl.BlockSpec((3, LAT, HALF), lambda i: (0, i, 0))
    vector = kept_spec((1, D))
    bias_spec = whole_spec(small.shape)
    outs = pl.pallas_call(
        functools.partial(first_kernel, direct),
        grid=(images,),
        name="project_own",
        in_specs=[row_spec(D), vector, vector, bias_spec, whole_spec((3, D, HALF))]
        + ([ANY] * 5 if direct else []),
        out_specs=[row_spec(D), heads_spec] + ([ANY] * 5 if direct else []),
        out_shape=[normed_shape, heads_shape]
        + ([shape_of(s, BF) for s in w_shapes] if direct else []),
        scratch_shapes=[pltpu.SemaphoreType.DMA((5,))] * 2 if direct else [],
        compiler_params=params(collective_id=0, has_side_effects=True) if direct else params(),
        cost_estimate=cost(6 * rows * D * HALF, 12 * rows * D),
    )(
        latents,
        first_scale,
        first_shift,
        small,
        own[0],
        *((own + (small,)) if direct else ()),
    )
    normed_one, heads_own = outs[:2]
    if direct:
        others = outs[2:]
    w_in_other, w_out_other, w_up_other, w_down_other, small_other = others
    w_in_own, w_out_own, w_up_own, w_down_own = own

    half_spec = pl.BlockSpec((2, LAT, HALF), lambda i: (0, i, 0))
    half_shape = shape_of((2, rows, HALF), BF)
    head_count = HALF // HEAD
    probs_shape = shape_of((2, head_count, rows, LAT), BF)
    probs_spec = pl.BlockSpec((2, head_count, LAT, LAT), lambda i: (0, 0, i, 0))
    square = (HALF, D)
    tall = (D, HALF)
    parts = ((0, 384), (384, 768), (768, 1024))
    job = Reduction(HALF, D, parts, ORDERS) if direct else None
    result = shape_of(square, BF)
    (
        block_output,
        heads_other,
        probs,
        inverses,
        mixed,
        middle,
        slope,
        g_down,
        g_sum,
    ) = pl.pallas_call(
        forward_kernel,
        grid=(images,),
        name="forward",
        in_specs=[
            row_spec(D),
            row_spec(D),
            heads_spec,
            row_spec(D),
            whole_spec((3, D, HALF)),
            whole_spec(small_other.shape),
            whole_spec(square),
            whole_spec(square),
            vector,
            vector,
            vector,
            whole_spec(tall),
            whole_spec(tall),
            bias_spec,
            bias_spec,
            whole_spec(square),
            whole_spec(square),
            vector,
        ],
        out_specs=[
            row_spec(D),
            heads_spec,
            probs_spec,
            row_spec(HEAD),
            half_spec,
            row_spec(D),
            half_spec,
            kept_spec((2, HALF, D)),
            kept_spec((8, D)),
        ],
        out_shape=[
            shape_of((rows, D), F32),
            heads_shape,
            probs_shape,
            shape_of((rows, HEAD), F32),
            half_shape,
            shape_of((rows, D), BF),
            half_shape,
            shape_of((2, HALF, D), BF),
            shape_of((8, D), F32),
        ],
        scratch_shapes=[
            pltpu.VMEM((2, HALF, D), F32),
            pltpu.VMEM((LAT, D), BF),
            pltpu.VMEM((2, LAT, HALF), BF),
            pltpu.VMEM((LAT, D), F32),
        ],
        compiler_params=params(),
        cost_estimate=cost(16 * rows * D * D, 24 * rows * D),
    )(
        latents,
        normed_one,
        heads_own,
        output_grad,
        w_in_other,
        small_other,
        w_out_own,
        w_out_other,
        output_bias,
        second_scale,
        second_shift,
        w_up_own,
        w_up_other,
        small,
        small_other,
        w_down_own,
        w_down_other,
        down_bias,
    )

    d_middle, d_mixed, d_dots, g_up, g_out, vec_two, vec_up, *sums = pl.pallas_call(
        functools.partial(feed_back_kernel, job, FEED_PLACES),
        grid=(images,),
        name="feed_back",
        in_specs=[
            row_spec(D),
            half_spec,
            row_spec(D),
            half_spec,
            row_spec(HEAD),
            whole_spec(square),
            whole_spec(square),
            whole_spec(tall),
            whole_spec(tall),
            whole_spec(square),
            whole_spec(square),
            vector,
            vector,
        ]
        + ([ANY] if direct else []),
        out_specs=[
            row_spec(D),
            half_spec,
            row_spec(HEAD),
            kept_spec((2, HALF, D)),
            kept_spec((2, HALF, D)),
            kept_spec((3, 8, D)),
            kept_spec((2, 8, HALF)),
        ]
        + ([ANY] if direct else []),
        out_shape=[
            shape_of((rows, D), BF),
            half_shape,
            shape_of((rows, HEAD), F32),
            shape_of((2, HALF, D), BF),
            shape_of((2, HALF, D), BF),
            shape_of((3, 8, D), F32),
            shape_of((2, 8, HALF), F32),
        ]
        + ([result] if direct else []),
        scratch_shapes=[
            pltpu.VMEM((2, HALF, D), F32),
            pltpu.VMEM((2, HALF, D), F32),
            pltpu.VMEM((LAT, D), BF),
            pltpu.VMEM((LAT, D), F32),
            pltpu.VMEM((2, LAT, HALF), BF),
            pltpu.VMEM((LAT, D), F32),
        ]
        + (job.scratch() if direct else []),
        compiler_params=params(collective_id=1, has_side_effects=True) if direct else params(),
        cost_estimate=cost(10 * rows * D * D, 14 * rows * D),
    )(
        output_grad,
        slope,
        middle,
        mixed,
        inverses,
        w_down_own,
        w_down_other,
        w_up_own,
        w_up_other,
        w_out_own,
        w_out_other,
        second_scale,
        second_shift,
        *((g_down,) if direct else ()),
    )

    per_group = head_count // GROUPS
    width = per_group * HEAD
    group_heads = pl.BlockSpec((3, LAT, width), lambda g, i: (0, i, g))
    group_job = Reduction(
        D // 2, 3 * width, tuple((n * width, (n + 1) * width) for n in range(3)), ORDERS
    )
    group_result = shape_of((D, 3 * width), BF)
    jobs = [job, job, group_job, group_job] if direct else []
    d_heads, g_in, vec_in, *more = pl.pallas_call(
        functools.partial(attend_back_kernel, jobs, ATTEND_PLACES),
        grid=(GROUPS, images),
        name="attend_back",
        in_specs=[
            pl.BlockSpec((LAT, D), lambda g, i: (i, 0)),
            group_heads,
            group_heads,
            pl.BlockSpec((2, per_group, LAT, LAT), lambda g, i: (0, g, i, 0)),
            pl.BlockSpec((2, LAT, width), lambda g, i: (0, i, g)),
            pl.BlockSpec((LAT, HEAD), lambda g, i: (i, 0)),
        ]
        + ([ANY] * 2 if direct else []),
        out_specs=[
            pl.BlockSpec((2, 3, LAT, width), lambda g, i: (0, 0, i, g)),
            pl.BlockSpec(
                (None, 2, D, 3 * width), lambda g, i: (0 if direct else g, 0, 0, 0)
            ),
            pl.BlockSpec((None, 8, 6 * width), lambda g, i: (g, 0, 0)),
        ]
        + [ANY] * (3 if direct else 0),
        out_shape=[
            shape_of((2, 3, rows, HALF), BF),
            shape_of((1 if direct else GROUPS, 2, D, 3 * width), BF),
            shape_of((GROUPS, 8, 6 * width), F32),
        ]
        + ([result, result, group_result] if direct else []),
        scratch_shapes=[
            pltpu.VMEM((D, 6 * width), F32),
            pltpu.VMEM((LAT, 6 * width), BF),
            pltpu.VMEM((LAT, HEAD), F32),
        ]
        + ([pltpu.VMEM((D, 3 * width), BF)] if direct else [])
        + sum([one.scratch() for one in jobs], []),
        compiler_params=params(collective_id=2, has_side_effects=True) if direct else params(),
        cost_estimate=cost(8 * rows * D * D, 20 * rows * D),
    )(
        normed_one,
        heads_own,
        heads_other,
        probs,
        d_mixed,
        d_dots,
        *((g_up, g_out) if direct else ()),
    )

    late_shape = (2 * D // HEAD, HEAD)
    stages = 1 + len(SHIFTS)

    def vector_scratch(shape):
        return [
            pltpu.VMEM((stages + 1,) + shape, F32),
            pltpu.VMEM((stages, 3) + shape, F32),
            pltpu.SemaphoreType.DMA((stages, 3)),
            pltpu.SemaphoreType.DMA((stages, 3)),
        ]

    grad_low, vectors, late, *last = pl.pallas_call(
        functools.partial(
            last_kernel, group_job if direct else None, LAST_PLACES, factor
        ),
        grid=(images,),
        name="input_back",
        in_specs=[
            row_spec(D),
            pl.BlockSpec((2, 3, LAT, HALF), lambda i: (0, 0, i, 0)),
            row_spec(D),
            whole_spec((3, D, HALF)),
            whole_spec((3, D, HALF)),
            vector,
            kept_spec((3, 8, D)),
            kept_spec((8, D)),
            kept_spec((2, 8, HALF)),
            kept_spec((GROUPS, 8, 6 * width)),
        ]
        + ([ANY] if direct else []),
        out_specs=[row_spec(D), kept_spec((8, D)), kept_spec(late_shape)]
        + ([ANY] if direct else []),
        out_shape=[shape_of((rows, D), BF), shape_of((8, D), F32), shape_of(late_shape, F32)]
        + ([group_result] if direct else []),
        scratch_shapes=[pltpu.VMEM((LAT, D), F32), pltpu.VMEM((2, 8, D), F32)]
        + (
            vector_scratch((8, D))
            + vector_scratch(late_shape)
            + group_job.scratch() * 2
            if direct
            else []
        ),
        compiler_params=params(collective_id=3, has_side_effects=True) if direct else params(),
        cost_estimate=cost(6 * rows * D * D, 14 * rows * D),
    )(
        latents,
        d_heads,
        d_middle,
        w_in_own,
        w_in_other,
        first_scale,
        vec_two,
        g_sum,
        vec_up,
        vec_in,
        *((g_in.reshape(2, D, 3 * width),) if direct else ()),
    )

    pieces = 8
    vector_shapes = [(1, D)] * 6 + [(2, HALF), (1, HALF)]
    cut = rows // pieces
    if direct:
        latents_grad, g_down, g_up, g_out, g_in, *vectors = pl.pallas_call(
            functools.partial(finish_kernel, factor),
            grid=(pieces,),
            name="finish",
            in_specs=[
                pl.BlockSpec((cut, D), lambda i: (i, 0)),
                pl.BlockSpec((HALF // pieces, D), lambda i: (i, 0)),
                pl.BlockSpec((HALF, D // pieces), lambda i: (0, i)),
                pl.BlockSpec((HALF // pieces, D), lambda i: (i, 0)),
                pl.BlockSpec((D // pieces, 3 * width), lambda i: (i, 0)),
                pl.BlockSpec((D // pieces, 3 * width), lambda i: (i, 0)),
                kept_spec((8, D)),
                kept_spec(late_shape),
            ],
            out_specs=[
                pl.BlockSpec((cut, D), lambda i: (i, 0)),
                pl.BlockSpec((HALF // pieces, D), lambda i: (i, 0)),
                pl.BlockSpec((D // pieces, HALF), lambda i: (i, 0)),
                pl.BlockSpec((HALF // pieces, D), lambda i: (i, 0)),
                pl.BlockSpec((3, D // pieces, HALF), lambda i: (0, i, 0)),
            ]
            + [kept_spec(shape) for shape in vector_shapes],
            out_shape=[
                shape_of((rows, D), F32),
                shape_of((HALF, D), F32),
                shape_of((D, HALF), F32),
                shape_of((HALF, D), F32),
                shape_of((3, D, HALF), F32),
            ]
            + [shape_of(shape, F32) for shape in vector_shapes],
            compiler_params=params(),
        )(grad_low, sums[0], more[0], more[1], more[2], last[0], vectors, late)
        in_bias, up_grad = vectors[6], vectors[7].reshape(HALF)
        late = [v.reshape(D) for v in vectors[4:6]]
        vectors = [v.reshape(D) for v in vectors[:4]]
    else:
        latents_grad = pl.pallas_call(
            functools.partial(finish_kernel, factor),
            grid=(pieces,),
            name="finish",
            in_specs=[pl.BlockSpec((cut, D), lambda i: (i, 0))],
            out_specs=pl.BlockSpec((cut, D), lambda i: (i, 0)),
            out_shape=shape_of((rows, D), F32),
            compiler_params=params(),
        )(grad_low)
        vectors = lax.psum(vectors, ("dp", "mp")) * factor
        late = lax.psum(late, ("dp", "mp")) * factor
        own_width = D // mp
        mine = lax.dynamic_slice_in_dim(
            vectors[4:7], lax.axis_index("mp") * own_width, own_width, 1
        )
        in_bias, up_grad, late = mine[:2], mine[2], late.reshape(2, D)
        g_down, g_up, g_out = (v.reshape(D, D) for v in (g_down, g_up, g_out))
        g_in = jnp.transpose(g_in.reshape(GROUPS, 2, D, 3, width), (3, 2, 1, 0, 4))
        g_in = g_in.reshape(3, D, D)

        def scatter(v, axis):
            v = lax.psum_scatter(v, "mp", scatter_dimension=axis, tiled=True)
            return lax.psum(v, "dp").astype(F32) * factor

        g_down, g_up, g_out = scatter(g_down, 0), scatter(g_up.T, 1), scatter(g_out, 0)
        g_in = scatter(g_in, 2)

    return (
        block_output,
        latents_grad,
        late[0],
        late[1],
        g_in,
        in_bias,
        g_out,
        vectors[0],
        vectors[1],
        vectors[2],
        g_up,
        up_grad,
        g_down,
        vectors[3],
    )


def solution(mesh):
    return jax.shard_map(
        per_device,
        mesh=mesh,
        in_specs=(
            P(("dp", "mp"), None),
            P(),
            P(),
            P(None, None, "mp"),
            P(None, "mp"),
            P("mp", None),
            P(),
            P(),
            P(),
            P(None, "mp"),
            P("mp"),
            P("mp", None),
            P(),
            P(("dp", "mp"), None),
        ),
        out_specs=(
            P(("dp", "mp"), None),
            P(("dp", "mp"), None),
            P(),
            P(),
            P(None, None, "mp"),
            P(None, "mp"),
            P("mp", None),
            P(),
            P(),
            P(),
            P(None, "mp"),
            P("mp"),
            P("mp", None),
            P(),
        ),
        check_vma=False,
    )
```
